32 devices in a mesh: seq: 16 (over z, y, core), fsdp: 2 (over x).
Axes of the slice: x: 2, y: 2, z: 4, core: 2. Of those that a mesh axis runs over, the one named last changes fastest.
Arguments:
- tokens_in: bfloat16 [2, 2048, 1152], P('fsdp', 'seq'), may hold values from -6 to 6
- condition: float32 [2, 16, 1152], P('fsdp'), may hold values from -6 to 6
- crop_pieces: int32 [2, 16], P('fsdp'), may hold values from 1 to 16, 128 in all within a row
- pad_counts: int32 [2, 16], P('fsdp'), may hold values from 0 to 32, as said below
- head_mask: int32 [2, 16, 16], P('fsdp'), may hold values 0 or 1
- channel_mask: int32 [2, 16, 36], P('fsdp'), may hold values 0 or 1
- keep_mask: int32 [2, 2048], P('fsdp', 'seq'), may hold values 0 or 1
- qkv_weight: bfloat16 [1152, 3456], P('fsdp'), may hold values from -0.1875 to 0.1875
- out_weight: bfloat16 [1152, 1152], P('fsdp'), may hold values from -1.75 to 1.75
- up_weight: bfloat16 [1152, 4608], P('fsdp'), may hold values from -0.1875 to 0.1875
- down_weight: bfloat16 [4608, 1152], P('fsdp'), may hold values from -0.09375 to 0.09375
- ada_weight: bfloat16 [1152, 6912], P(None, 'fsdp'), may hold values from -0.1875 to 0.1875
- cotangent: bfloat16 [2, 2048, 1152], P('fsdp', 'seq'), may hold values from -6 to 6
Outputs:
- block_out: bfloat16 [2, 2048, 1152], P('fsdp', 'seq')
- input_grad: float32 [2, 2048, 1152], P('fsdp', 'seq')
- qkv_grad: float32 [1152, 3456], P('fsdp', 'seq')
- out_grad: float32 [1152, 1152], P('fsdp', 'seq')
- up_grad: float32 [1152, 4608], P('fsdp', 'seq')
- down_grad: float32 [4608, 1152], P('fsdp', 'seq')
- ada_grad: float32 [1152, 6912], P(None, 'fsdp')
The draws below stay inside these ranges and needn't reach their ends.
Inputs may be any that keep to these rules, and one draw needn't show every extreme that they name: `pad_counts`: in every row some cycle position has no padding and some has 32 padding slots. `crop_pieces`: each row's pieces sum to 128 and the largest is 16.
All inputs are finite; a program needn't handle non-finite values. No bound on the sum of `head_mask` or of `channel_mask` or of `keep_mask` on one device may be relied on, other than what follows from the above.
Results may differ from the reference program's by a relative error of at most 0.02865.
Values may be sent and summed in bfloat16 or wider, within the bound.
No kernel may reach another device: no remote copies, remote signals or barrier semaphores. Data moves between devices by JAX's collectives and lax.ppermute only.
A program may use at most 256 MiB of HBM per device.

```python
import math
import jax
import jax.numpy as jnp
import numpy as np
from jax import lax

D = 1152
H = 16
HD = 72
FF = 4608
CHAN_GROUP = 128
PIECE_MAX = 16
PAD_MAX = 32
TOK_DEV = 128
CROPS = 16
GROUPS = 36
ROWS = 2
L = 2048
N_SEQ = 16


def draw_pad_counts(key, part):
    base_key, order_key = jax.random.split(key)
    counts = jax.random.randint(base_key, (ROWS, N_SEQ), 0, PAD_MAX + 1)
    row_keys = jax.random.split(order_key, ROWS)
    orders = jax.vmap(lambda row_key: jax.random.permutation(row_key, N_SEQ))(row_keys)
    position_ids = jnp.arange(N_SEQ)
    counts = jnp.where(position_ids[None, :] == orders[:, 0:1], 0, counts)
    counts = jnp.where(position_ids[None, :] == orders[:, 1:2], PAD_MAX, counts)
    return counts.astype(jnp.int32)


def set_ends(drawn, rng, least, top_value):
    spot = [jax.random.randint(jax.random.fold_in(rng, axis), (), 0, length) for axis, length in enumerate(drawn.shape)]
    longest = drawn.shape.index(max(drawn.shape))
    next_to = spot[:longest] + [(spot[longest] + 1) % drawn.shape[longest]] + spot[longest + 1:]
    return drawn.at[tuple(spot)].set(least).at[tuple(next_to)].set(top_value)


def shard_levels(own_key, dims, cuts, low, top_value):
    level, own = 1.0, jax.random.fold_in(own_key, 6)
    for dim, parts in cuts:
        heights = jnp.exp(jax.random.uniform(jax.random.fold_in(own, dim), (parts,), jnp.float32, low / len(cuts), top_value / len(cuts)))
        level = level * jnp.repeat(heights, dims[dim] // parts).reshape([-1 if axis == dim else 1 for axis in range(len(dims))])
    return level


def split_up(amount, total, most, slope):
    loads = [(1 << 20) // math.isqrt(grade ** slope) + 1 for grade in range(2, amount + 1)]
    rest, given = total - most - (amount - 1), [1] * (amount - 1)
    while rest > 0:
        free = [i for i in range(amount - 1) if given[i] < most]
        mass, budget = sum([loads[i] for i in free]), rest
        for i in free:
            extra = min(most - given[i], max(1, budget * loads[i] // mass), rest)
            given[i] = given[i] + extra
            rest = rest - extra
    return np.array([most] + given)


def ragged(stream_key, amount, total, reach, skew):
    if amount == 2:
        one = jax.random.randint(stream_key, (), max(1, total - reach), min(reach, total - 1) + 1)
        return jnp.stack([one, total - one])
    tallies = jnp.asarray(split_up(amount, total, reach, skew), jnp.int32)
    pairs = (amount - 1) // 2
    donor, taker = tallies[1:1 + 2 * pairs:2], tallies[2:2 + 2 * pairs:2]
    slack = jnp.minimum(donor - 1, reach - taker)
    moved = jax.random.randint(jax.random.fold_in(stream_key, 1), (pairs,), 0, 1 << 20) % (slack + 1)
    tallies = tallies.at[1:1 + 2 * pairs:2].set(donor - moved).at[2:2 + 2 * pairs:2].set(taker + moved)
    return tallies[jax.random.permutation(jax.random.fold_in(stream_key, 2), amount)]


def scatter_about(rng, shape, width, limit, cuts=(), held_as=jnp.bfloat16):
    array = width * jax.random.normal(rng, shape, jnp.float32)
    if cuts:
        array = array * shard_levels(rng, shape, cuts, -0.22, 0.18)
    return jnp.clip(array, -limit, limit).astype(held_as)


def setup_inputs(seed: int = 0) -> dict:
    keys = jax.random.split(jax.random.key(seed), 14)
    tokens_in = scatter_about(keys[0], (ROWS, L, D), 1.0, 6.0, ((0, 2), (1, 16)))
    condition = scatter_about(keys[1], (ROWS, CROPS, D), 1.0, 6.0, ((0, 2),), jnp.float32)
    crop_pieces = jax.vmap(lambda own: ragged(own, CROPS, TOK_DEV, PIECE_MAX, 1))(jax.random.split(keys[2], ROWS)).reshape((ROWS, CROPS)).astype(jnp.int32)
    pad_counts = draw_pad_counts(jax.random.fold_in(keys[13], 71), 0)
    head_mask = set_ends((jax.random.randint(keys[4], (ROWS, CROPS, H), 0, 4) < 3).astype(jnp.int32), jax.random.fold_in(keys[4], 1), 0, 1)
    channel_mask = set_ends((jax.random.randint(keys[5], (ROWS, CROPS, GROUPS), 0, 4) < 3).astype(jnp.int32), jax.random.fold_in(keys[5], 1), 0, 1)
    keep_mask = set_ends((jax.random.randint(keys[6], (ROWS, L), 0, 4) < 3).astype(jnp.int32), jax.random.fold_in(keys[6], 1), 0, 1)
    qkv_weight = scatter_about(keys[7], (D, 3 * D), D ** -0.5, 0.1875, ((0, 2),))
    out_weight = scatter_about(keys[8], (D, D), (max(D // 96, 2)) ** -0.5, 1.75, ((0, 2),))
    up_weight = scatter_about(keys[9], (D, FF), D ** -0.5, 0.1875, ((0, 2),))
    down_weight = scatter_about(keys[10], (FF, D), FF ** -0.5, 0.09375, ((0, 2),))
    ada_weight = scatter_about(keys[11], (D, 6 * D), D ** -0.5, 0.1875, ((1, 2),))
    cotangent = scatter_about(keys[12], (ROWS, L, D), 1.0, 6.0, ((0, 2), (1, 16)))
    return dict(tokens_in=tokens_in, condition=condition, crop_pieces=crop_pieces, pad_counts=pad_counts, head_mask=head_mask, channel_mask=channel_mask, keep_mask=keep_mask, qkv_weight=qkv_weight, out_weight=out_weight, up_weight=up_weight, down_weight=down_weight, ada_weight=ada_weight, cotangent=cotangent)


@jax.custom_vjp
def low(v):
    return lax.optimization_barrier(v.astype(jnp.bfloat16)).astype(jnp.float32)

@jax.custom_vjp
def low_back(v):
    return v

def low_keep(v):
    return (low(v), None)

def low_pass(kept, grad):
    return (grad,)

def back_keep(v):
    return (v, None)

def back_low(kept, grad):
    return (low(grad),)
low.defvjp(low_keep, low_pass)
low_back.defvjp(back_keep, back_low)
highest = lax.Precision.HIGHEST
norm_epsilon = 1e-06
masked_score = -1e+30

def normalize(values):
    average = lax.optimization_barrier(jnp.mean(values, axis=-1, keepdims=True))
    centred = values - average
    spread = lax.optimization_barrier(jnp.mean(centred * centred, axis=-1, keepdims=True))
    return centred * lax.rsqrt(spread + norm_epsilon)

def row_layout(pieces, pad_row):
    crop_ends = jnp.cumsum(pieces)
    slot_index = jnp.arange(TOK_DEV, dtype=jnp.int32)
    crop_local = lax.optimization_barrier(jnp.sum((slot_index[:, None] >= crop_ends[None, :-1]).astype(jnp.int32), axis=1))
    crop_ids = jnp.tile(crop_local, N_SEQ)
    key_valid = (slot_index[None, :] < (TOK_DEV - pad_row)[:, None]).reshape(TOK_DEV * N_SEQ)
    return (crop_ids, key_valid)

def row_forward(tokens_row, cond_row, pieces, pad_row, heads_on, groups_on, keep_row, qkv_weight, out_weight, up_weight, down_weight, ada_weight):
    positions = TOK_DEV * N_SEQ
    crop_ids, key_valid = row_layout(pieces, pad_row)
    selector = (crop_ids[:, None] == jnp.arange(CROPS, dtype=jnp.int32)[None, :]).astype(jnp.float32)
    cond_act = low(jax.nn.silu(cond_row))
    modulation = low_back(jnp.dot(cond_act, ada_weight, precision=highest))
    per_token = jnp.dot(selector, modulation, precision=highest)
    shift_attn = per_token[:, 0:D]
    scale_attn = per_token[:, D:2 * D]
    gate_attn = per_token[:, 2 * D:3 * D]
    shift_mlp = per_token[:, 3 * D:4 * D]
    scale_mlp = per_token[:, 4 * D:5 * D]
    gate_mlp = per_token[:, 5 * D:6 * D]
    head_tokens = jnp.dot(selector, heads_on.astype(jnp.float32), precision=highest)
    channel_tokens = jnp.repeat(jnp.dot(selector, groups_on.astype(jnp.float32), precision=highest), CHAN_GROUP, axis=1)
    normed_in = low(normalize(tokens_row) * (1.0 + scale_attn) + shift_attn)
    projected = jnp.dot(normed_in, qkv_weight, precision=highest)
    queries = low_back(low(projected[:, 0:D])).reshape(positions, H, HD)
    keys_all = low_back(low(projected[:, D:2 * D])).reshape(positions, H, HD)
    values_all = low_back(low(projected[:, 2 * D:3 * D])).reshape(positions, H, HD)
    block_rows = min(512, positions)
    score_scale = HD ** (-0.5)

    def attend(block_in):
        query_block, crop_block = block_in
        scores = low_back(jnp.einsum('qhd,khd->hqk', query_block, keys_all, precision=highest) * score_scale)
        allowed = ((crop_block[:, None] == crop_ids[None, :]) & key_valid[None, :])[None]
        masked = jnp.where(allowed, scores, masked_score)
        top_score = lax.optimization_barrier(jnp.max(masked, axis=-1, keepdims=True))
        weights_exp = jnp.where(allowed, jnp.exp(masked - top_score), 0.0)
        probabilities = weights_exp / lax.optimization_barrier(jnp.sum(weights_exp, axis=-1, keepdims=True))
        return jnp.einsum('hqk,khd->qhd', low(probabilities), values_all, precision=highest)
    heads_out = lax.map(jax.checkpoint(attend), (queries.reshape(positions // block_rows, block_rows, H, HD), crop_ids.reshape(positions // block_rows, block_rows)))
    heads_out = low_back(heads_out.reshape(positions, H, HD))
    merged = low((heads_out * head_tokens[:, :, None]).reshape(positions, D))
    attn_proj = low_back(jnp.dot(merged, out_weight, precision=highest))
    mid_state = tokens_row + gate_attn * attn_proj
    normed_mid = low(normalize(mid_state) * (1.0 + scale_mlp) + shift_mlp)
    hidden_pre = low_back(jnp.dot(normed_mid, up_weight, precision=highest))
    hidden_act = low(jax.nn.gelu(hidden_pre, approximate=True) * channel_tokens)
    mlp_out = low_back(jnp.dot(hidden_act, down_weight, precision=highest))
    return mid_state + gate_mlp * keep_row.astype(jnp.float32)[:, None] * mlp_out

def reference(tokens_in, condition, crop_pieces, pad_counts, head_mask, channel_mask, keep_mask, qkv_weight, out_weight, up_weight, down_weight, ada_weight, cotangent):

    def whole(tokens_all, weight_qkv, weight_out, weight_up, weight_down, weight_ada):

        def one_row(running, row_in):
            tokens_row, cond_row, pieces, pad_row, heads_on, groups_on, keep_row = row_in
            result = jax.checkpoint(row_forward)(tokens_row, cond_row, pieces, pad_row, heads_on, groups_on, keep_row, weight_qkv, weight_out, weight_up, weight_down, weight_ada)
            return (running, result)
        ignored, outputs = lax.scan(one_row, jnp.zeros((), jnp.float32), (tokens_all, condition.astype(jnp.float32), crop_pieces, pad_counts, head_mask, channel_mask, keep_mask))
        return outputs
    block_out, pullback = jax.vjp(whole, tokens_in.astype(jnp.float32), qkv_weight.astype(jnp.float32), out_weight.astype(jnp.float32), up_weight.astype(jnp.float32), down_weight.astype(jnp.float32), ada_weight.astype(jnp.float32))
    gradients = pullback(cotangent.astype(jnp.float32))
    return (block_out.astype(jnp.bfloat16), gradients[0], gradients[1], gradients[2], gradients[3], gradients[4], gradients[5])
```

```python
import functools

import jax
import jax.numpy as jnp
from jax import lax
from jax.experimental import pallas as pl
from jax.experimental.pallas import tpu as pltpu
from jax.sharding import PartitionSpec as P

D = 1152
H = 16
HD = 72
CHAN_GROUP = 128
PIECE_MAX = 16

bf16 = jnp.bfloat16
f32 = jnp.float32
highest = lax.Precision.HIGHEST
norm_epsilon = 1e-06
masked_score = -1e30
score_scale = HD ** (-0.5)
VMEM_LIMIT = 48 * 1024 * 1024


def head_window(head):
    start = head * HD
    low = start // 128 * 128
    width = 128 if start + HD - low <= 128 else 256
    return low, min(width, D - low), start - low


def head_lanes(rows, width, first):
    lane = lax.broadcasted_iota(jnp.int32, (rows, width), 1)
    return (lane >= first) & (lane < first + HD)


def dot_nt(a, b):
    return lax.dot_general(a, b, (((1,), (1,)), ((), ())), preferred_element_type=f32)


def dot_nn(a, b):
    return lax.dot_general(a, b, (((1,), (0,)), ((), ())), preferred_element_type=f32)


def dot_tn(a, b):
    return lax.dot_general(a, b, (((0,), (0,)), ((), ())), preferred_element_type=f32)


def attend_kernel(q_ref, kv_ref, bias_ref, mask_ref, out_ref, acc_ref):
    tokens = q_ref.shape[0]
    acc_ref[...] = jnp.zeros_like(acc_ref)
    for head in range(H):
        low, width, first = head_window(head)
        window = pl.ds(low, width)
        lanes = head_lanes(tokens, width, first)
        query = jnp.where(lanes, q_ref[:, window], jnp.zeros((), bf16))
        scores = dot_nt(query, kv_ref[:, window]) * score_scale + bias_ref[...]
        top = jnp.max(scores, axis=1, keepdims=True)
        weights = jnp.exp(scores - top)
        probs = (weights * (1.0 / jnp.sum(weights, axis=1, keepdims=True))).astype(bf16)
        out = dot_nn(probs, kv_ref[:, pl.ds(D + low, width)])
        acc_ref[:, window] += jnp.where(lanes, out, 0.0)
    slots = mask_ref.shape[0]
    for start in range(0, tokens, slots):
        rows = pl.ds(start, slots)
        out_ref[rows, :] = (acc_ref[rows, :] * mask_ref[...]).astype(bf16)


def attend(queries, kv_window, bias, head_slots):
    tokens = queries.shape[0]
    return pl.pallas_call(
        attend_kernel,
        out_shape=jax.ShapeDtypeStruct((tokens, D), bf16),
        in_specs=[pl.BlockSpec(memory_space=pltpu.VMEM)] * 4,
        out_specs=pl.BlockSpec(memory_space=pltpu.VMEM),
        scratch_shapes=[pltpu.VMEM((tokens, D), f32)],
        compiler_params=pltpu.CompilerParams(vmem_limit_bytes=VMEM_LIMIT),
        name="attend",
    )(queries, kv_window, bias, head_slots)


def attend_back_kernel(
    q_ref, kv_ref, bias_ref, grad_ref, dq_ref, dkv_ref, dq_acc, dk_acc, dv_acc
):
    tokens = q_ref.shape[0]
    dq_acc[...] = jnp.zeros_like(dq_acc)
    dk_acc[...] = jnp.zeros_like(dk_acc)
    dv_acc[...] = jnp.zeros_like(dv_acc)
    for head in range(H):
        low, width, first = head_window(head)
        window = pl.ds(low, width)
        lanes = head_lanes(tokens, width, first)
        query = jnp.where(lanes, q_ref[:, window], jnp.zeros((), bf16))
        grad = jnp.where(lanes, grad_ref[:, window], jnp.zeros((), bf16))
        keys = kv_ref[:, window]
        scores = dot_nt(keys, query) * score_scale + bias_ref[...]
        top = jnp.max(scores, axis=0, keepdims=True)
        weights = jnp.exp(scores - top)
        probs = weights * (1.0 / jnp.sum(weights, axis=0, keepdims=True))
        probs_low = probs.astype(bf16)
        grad_probs = dot_nt(kv_ref[:, pl.ds(D + low, width)], grad)
        row_dot = jnp.sum(probs_low.astype(f32) * grad_probs, axis=0, keepdims=True)
        grad_scores = (probs * (grad_probs - row_dot)).astype(bf16)
        dk_acc[:, window] += dot_nn(grad_scores, query)
        dv_acc[:, window] += dot_nn(probs_low, grad)
        dq_acc[:, window] += jnp.where(lanes, dot_tn(grad_scores, keys), 0.0)
    dq_ref[...] = (dq_acc[...] * score_scale).astype(bf16)
    dkv_ref[:, pl.ds(0, D)] = (dk_acc[...] * score_scale).astype(bf16)
    dkv_ref[:, pl.ds(D, D)] = dv_acc[...].astype(bf16)


def attend_back(queries, kv_window, bias_t, grad_heads):
    tokens = queries.shape[0]
    keys = kv_window.shape[0]
    return pl.pallas_call(
        attend_back_kernel,
        out_shape=(
            jax.ShapeDtypeStruct((tokens, D), bf16),
            jax.ShapeDtypeStruct((keys, 2 * D), bf16),
        ),
        in_specs=[pl.BlockSpec(memory_space=pltpu.VMEM)] * 4,
        out_specs=(pl.BlockSpec(memory_space=pltpu.VMEM),) * 2,
        scratch_shapes=[
            pltpu.VMEM((tokens, D), f32),
            pltpu.VMEM((keys, D), f32),
            pltpu.VMEM((keys, D), f32),
        ],
        compiler_params=pltpu.CompilerParams(vmem_limit_bytes=VMEM_LIMIT),
        name="attend_back",
    )(queries, kv_window, bias_t, grad_heads)


def assemble_kernel(place_ref, *refs, count, col_start, cols):
    local_ref, piece_refs, out_ref, sems = refs[0], refs[1 : 1 + count], refs[-2], refs[-1]
    half = out_ref.shape[0] // 2
    rows = half // count
    mine, quarter, column = place_ref[0], place_ref[1], place_ref[2]
    source = local_ref.at[:, pl.ds(pl.multiple_of(col_start + column * cols, 128), cols)]
    copies = [
        pltpu.make_async_copy(
            source, out_ref.at[pl.ds(pl.multiple_of(mine * half, 8), half), :], sems.at[count]
        )
    ]
    for step, piece in enumerate(piece_refs):
        start = (1 - mine) * half + (quarter ^ step) * rows
        copies.append(
            pltpu.make_async_copy(
                piece, out_ref.at[pl.ds(pl.multiple_of(start, 8), rows), :], sems.at[step]
            )
        )
    for copy in copies:
        copy.start()
    for copy in copies:
        copy.wait()


def assemble(place, local_weight, pieces, col_start, cols):
    count = len(pieces)
    return pl.pallas_call(
        functools.partial(assemble_kernel, count=count, col_start=col_start, cols=cols),
        out_shape=jax.ShapeDtypeStruct((2 * local_weight.shape[0], cols), bf16),
        in_specs=[pl.BlockSpec(memory_space=pltpu.SMEM)]
        + [pl.BlockSpec(memory_space=pl.ANY)] * (1 + count),
        out_specs=pl.BlockSpec(memory_space=pl.ANY),
        scratch_shapes=[pltpu.SemaphoreType.DMA((count + 1,))],
        name="assemble",
    )(place, local_weight, *pieces)


def layer_norm(values):
    average = jnp.mean(values, axis=-1, keepdims=True)
    centred = values - average
    spread = jnp.mean(centred * centred, axis=-1, keepdims=True)
    inverse = lax.rsqrt(spread + norm_epsilon)
    return centred * inverse, inverse


def layer_norm_back(grad_normed, normed, inverse):
    mean_grad = jnp.mean(grad_normed, axis=-1, keepdims=True)
    mean_dot = jnp.mean(grad_normed * normed, axis=-1, keepdims=True)
    return (grad_normed - mean_grad - normed * mean_dot) * inverse


def running_ends(pieces):
    index = jnp.arange(pieces.shape[0], dtype=jnp.int32)
    return jnp.sum(jnp.where(index[None, :] <= index[:, None], pieces[None, :], 0), axis=1)


def crop_of(slots, ends):
    return jnp.sum((slots[..., None] >= ends[:-1]).astype(jnp.int32), axis=-1)


def one_hot(crops, count):
    return (crops[..., None] == jnp.arange(count, dtype=jnp.int32)).astype(f32)


def block_order(size):
    def device(block):
        chip, core = block // 2, block % 2
        return 2 * (chip ^ ((chip >> 1) & 1)) + core if size % 8 == 0 else block

    return [device(block) for block in range(size)]


def local(
    tokens_in,
    condition,
    crop_pieces,
    pad_counts,
    head_mask,
    channel_mask,
    keep_mask,
    qkv_weight,
    out_weight,
    up_weight,
    down_weight,
    ada_weight,
    cotangent,
):
    seq = lax.axis_size("seq")
    rows = lax.axis_size("fsdp")
    tokens = tokens_in.shape[1]
    slots = tokens // seq
    crops = crop_pieces.shape[1]
    hidden = up_weight.shape[1]
    hidden_part = hidden // rows
    half = D // rows
    seq_at = lax.axis_index("seq")
    row_at = lax.axis_index("fsdp")
    fast = rows == 2 and seq == 16
    order = block_order(seq)
    if seq % 8 == 0:
        chip = seq_at // 2
        block_at = 2 * (chip ^ ((chip >> 1) & 1)) + seq_at % 2
    else:
        block_at = seq_at

    def flip(value, bit):
        return lax.ppermute(value, "seq", [(i, i ^ bit) for i in range(seq)])

    def cross(value):
        return lax.ppermute(value, "fsdp", [(0, 1), (1, 0)])

    def shift(value, distance):
        pairs = [
            (order[b], order[b + distance]) for b in range(seq) if 0 <= b + distance < seq
        ]
        return lax.ppermute(value, "seq", pairs)

    def reorder(blocks):
        runs, start = [], 0
        while start < seq:
            stop = start + 1
            while stop < seq and order[stop] == order[stop - 1] + 1:
                stop += 1
            runs.append(blocks[order[start] : order[start] + stop - start])
            start = stop
        return jnp.concatenate(runs, axis=0) if len(runs) > 1 else blocks

    def to_slots(value):
        return lax.all_to_all(reorder(value.reshape(seq, slots, -1)), "seq", 0, 0)

    def from_slots(value):
        return reorder(lax.all_to_all(value, "seq", 0, 0)).reshape(tokens, -1)

    def gather_rows(value):
        if rows == 2:
            return jnp.stack([value, cross(value)])
        return lax.all_gather(value, "fsdp", axis=0)

    def sum_rows(parts):
        if rows == 2:
            return parts[0] + cross(parts[1].astype(bf16)).astype(f32)
        total = lax.psum_scatter(parts.astype(bf16), "fsdp", scatter_dimension=0, tiled=True)
        return total.reshape(parts.shape[1:]).astype(f32)

    def pick(low_part, high_part):
        return jnp.where(row_at == 0, low_part, high_part)

    slot_index = block_at * slots + jnp.arange(slots, dtype=jnp.int32)
    ends = running_ends(crop_pieces[0])
    crop_here = crop_of(slot_index, ends)
    selector = one_hot(crop_here, crops)
    pads = pad_counts[0]

    cond_act = jax.nn.silu(condition[0]).astype(bf16)
    extra = jnp.concatenate(
        [channel_mask[0].astype(bf16), crop_pieces[0].astype(bf16)[:, None]], axis=1
    )
    extra = jnp.pad(extra, ((0, 0), (0, 128 - extra.shape[1])))
    packed = gather_rows(jnp.concatenate([cond_act, extra], axis=1))
    groups = channel_mask.shape[2]
    cond_rows = packed[:, :, :D]
    group_rows = packed[:, :, D : D + groups].astype(f32)
    ends_rows = jax.vmap(running_ends)(packed[:, :, D + groups].astype(jnp.int32))
    selector_rows = jax.vmap(lambda own: one_hot(crop_of(slot_index, own), crops))(ends_rows)

    columns = ada_weight.shape[1]
    mod_rows = jnp.dot(
        cond_rows.reshape(rows * crops, D), ada_weight, preferred_element_type=f32
    ).reshape(rows, crops, columns)
    if rows == 2:
        mod_slots = jnp.einsum("rsc,rcm->rsm", selector_rows, mod_rows, precision=highest)
        arrived = cross(mod_slots[1])
        mod_attn = pick(mod_slots[0], arrived)
        mod_mlp = pick(arrived, mod_slots[0])
    else:
        mine = lax.all_to_all(mod_rows, "fsdp", 0, 0)
        mine = jnp.transpose(mine, (1, 0, 2)).reshape(crops, rows * columns)
        mine = jnp.dot(selector, mine, precision=highest)
        mod_attn, mod_mlp = mine[:, : 3 * D], mine[:, 3 * D :]
    shift_attn, scale_attn, gate_attn = (mod_attn[:, i * D : (i + 1) * D] for i in range(3))
    shift_mlp, scale_mlp, gate_mlp = (mod_mlp[:, i * D : (i + 1) * D] for i in range(3))

    place = jnp.stack([row_at, seq_at & 3, row_at]).astype(jnp.int32)

    def fetch(weight, row_start, col_start, shape):
        first = lax.dynamic_slice(weight, (row_start, col_start), shape)
        first = cross(first)
        second = flip(first, 2)
        return (first, flip(first, 1), second, flip(second, 1))

    def whole_rows(weight, col_start, cols):
        if not fast:
            part = weight[:, col_start : col_start + cols]
            return lax.all_gather(part, "fsdp", axis=0, tiled=True)
        quarter = weight.shape[0] // 4
        pieces = fetch(weight, (seq_at & 3) * quarter, col_start, (quarter, cols))
        return assemble(place * jnp.array([1, 1, 0], jnp.int32), weight, pieces, col_start, cols)

    kv_full = whole_rows(qkv_weight, D, 2 * D)
    q_full = whole_rows(qkv_weight, 0, D)
    out_full = whole_rows(out_weight, 0, D)
    if fast:
        quarter = half // 4
        pieces = fetch(
            up_weight, (seq_at & 3) * quarter, (1 - row_at) * hidden_part, (quarter, hidden_part)
        )
        up_part = assemble(place, up_weight, pieces, 0, hidden_part)
    else:
        up_part = lax.all_to_all(up_weight, "fsdp", 1, 0, tiled=True)

    residual = to_slots(tokens_in[0]).astype(f32)
    kept = jnp.broadcast_to(keep_mask[0].astype(bf16)[:, None], (tokens, 128))
    late_in = to_slots(jnp.concatenate([cotangent[0], kept], axis=1))
    grad_out = late_in[:, :, :D].astype(f32)
    keep = late_in[:, :, D : D + 1].astype(f32)

    normed_tokens, inverse_in = layer_norm(residual)
    normed_in = (normed_tokens * (1.0 + scale_attn) + shift_attn).astype(bf16)
    normed_in = normed_in.reshape(tokens, D)

    reach = -(-(PIECE_MAX - 1) // slots)
    paired = reach == 2 and seq % 2 == 0
    core = seq_at % 2
    if paired:
        below, above = shift(normed_in, 2), shift(normed_in, -2)
        passed = flip(jnp.where(core == 0, above, below), 1)
        near = [normed_in, flip(normed_in, 1), below, above, passed]
        near_at = [
            block_at,
            block_at ^ 1,
            block_at - 2,
            block_at + 2,
            block_at - 1 + 2 * core,
        ]
    else:
        near, near_at = [normed_in], [block_at]
        for distance in range(1, reach + 1):
            near += [shift(normed_in, distance), shift(normed_in, -distance)]
            near_at += [block_at - distance, block_at + distance]
    window_in = jnp.concatenate(near, axis=0)
    near_at = jnp.stack(near_at)
    key_slots = near_at[:, None] * slots + jnp.arange(slots, dtype=jnp.int32)[None, :]
    key_crop = jnp.where((near_at >= 0)[:, None] & (near_at < seq)[:, None], crop_of(key_slots, ends), -1)
    key_crop = jnp.where(
        key_slots[:, None, :] < tokens - pads[None, :, None], key_crop[:, None, :], -1
    ).reshape(-1)
    query_crop = jnp.broadcast_to(crop_here[None, :], (seq, slots)).reshape(tokens)
    bias = jnp.where(query_crop[:, None] == key_crop[None, :], 0.0, masked_score).astype(f32)
    bias_t = jnp.where(key_crop[:, None] == query_crop[None, :], 0.0, masked_score).astype(f32)
    head_slots = jnp.repeat(
        jnp.dot(selector, head_mask[0].astype(f32), precision=highest), HD, axis=1
    )

    kv_window = jnp.dot(window_in, kv_full, preferred_element_type=f32).astype(bf16)
    queries = jnp.dot(normed_in, q_full, preferred_element_type=f32).astype(bf16)
    merged = attend(queries, kv_window, bias, head_slots)
    attn_proj = jnp.dot(merged, out_full, preferred_element_type=f32).reshape(seq, slots, D)
    mid_state = residual + gate_attn * attn_proj
    normed, inverse_mid = layer_norm(mid_state)
    normed_mid = (normed * (1.0 + scale_mlp) + shift_mlp).astype(bf16).reshape(tokens, D)

    mid_rows = gather_rows(normed_mid).reshape(rows * tokens, D)
    grad_mlp = (grad_out * gate_mlp * keep).astype(bf16).reshape(tokens, D)
    grad_mlp_rows = gather_rows(grad_mlp).reshape(rows * tokens, D)
    channels = jnp.einsum("rsc,rcg->rsg", selector_rows, group_rows, precision=highest)
    channels = lax.dynamic_slice_in_dim(
        jnp.repeat(channels, CHAN_GROUP, axis=2), row_at * hidden_part, hidden_part, 2
    )
    channels = channels[:, None]
    wide = (rows, seq, slots, hidden_part)
    hidden_pre = jnp.dot(mid_rows, up_part, preferred_element_type=f32).reshape(wide)
    root = 0.7978845608028654
    inner = jnp.tanh(root * (hidden_pre + 0.044715 * hidden_pre * hidden_pre * hidden_pre))
    hidden_act = (0.5 * hidden_pre * (1.0 + inner) * channels).astype(bf16)
    hidden_act = hidden_act.reshape(rows * tokens, hidden_part)
    slope = 0.5 * (1.0 + inner) + 0.5 * hidden_pre * (1.0 - inner * inner) * root * (
        1.0 + 3.0 * 0.044715 * hidden_pre * hidden_pre
    )
    grad_act = lax.dot_general(
        grad_mlp_rows, down_weight, (((1,), (1,)), ((), ())), preferred_element_type=f32
    ).reshape(wide)
    grad_pre = (grad_act * channels * slope).astype(bf16).reshape(rows * tokens, hidden_part)
    grad_parts = lax.dot_general(
        grad_pre, up_part, (((1,), (1,)), ((), ())), preferred_element_type=f32
    )
    grad_normed_mid = sum_rows(grad_parts.reshape(rows, tokens, D)).reshape(seq, slots, D)
    mlp_parts = jnp.dot(hidden_act, down_weight, preferred_element_type=f32)
    mlp_out = sum_rows(mlp_parts.reshape(rows, tokens, D)).reshape(seq, slots, D)
    block_out = from_slots((mid_state + gate_mlp * keep * mlp_out).astype(bf16))

    grad_mid = grad_out + layer_norm_back(
        grad_normed_mid * (1.0 + scale_mlp), normed, inverse_mid
    )
    grad_attn = (grad_mid * gate_attn).astype(bf16).reshape(tokens, D)
    grad_merged = lax.dot_general(
        grad_attn, out_full, (((1,), (1,)), ((), ())), preferred_element_type=f32
    )
    grad_heads = (grad_merged.reshape(seq, slots, D) * head_slots).astype(bf16)
    grad_queries, grad_window = attend_back(
        queries, kv_window, bias_t, grad_heads.reshape(tokens, D)
    )
    parts = grad_window.reshape(-1, tokens, 2 * D)
    grad_kv = parts[0].astype(f32)
    if paired:
        handed = flip(parts[4], 1).astype(f32)
        down_part = (parts[2].astype(f32) + jnp.where(core == 1, handed, 0.0)).astype(bf16)
        up_side = (parts[3].astype(f32) + jnp.where(core == 0, handed, 0.0)).astype(bf16)
        grad_kv = grad_kv + flip(parts[1], 1).astype(f32)
        grad_kv = grad_kv + shift(down_part, -2).astype(f32) + shift(up_side, 2).astype(f32)
    else:
        for distance in range(1, reach + 1):
            grad_kv = grad_kv + shift(parts[2 * distance - 1], -distance).astype(f32)
            grad_kv = grad_kv + shift(parts[2 * distance], distance).astype(f32)
    grad_kv = grad_kv.astype(bf16)

    contract = (((1,), (1,)), ((), ()))
    grad_normed_in = lax.dot_general(grad_queries, q_full, contract, preferred_element_type=f32)
    grad_normed_in = grad_normed_in + lax.dot_general(
        grad_kv, kv_full, contract, preferred_element_type=f32
    )
    grad_normed_in = grad_normed_in.reshape(seq, slots, D)
    input_grad = grad_mid + layer_norm_back(
        grad_normed_in * (1.0 + scale_attn), normed_tokens, inverse_in
    )
    input_grad = from_slots(input_grad.astype(bf16)).astype(f32)

    def by_crop(parts_list):
        return jnp.dot(
            jnp.transpose(selector), jnp.concatenate(parts_list, axis=1), precision=highest
        ).astype(bf16)

    def all_sum(value):
        if not fast:
            return lax.psum(value, "seq")
        for bit in (1, 2, 4, 8):
            value = (value.astype(f32) + flip(value, bit).astype(f32)).astype(bf16)
        return value

    early = all_sum(
        by_crop(
            [
                jnp.sum(grad_mid * attn_proj, axis=0),
                jnp.sum(grad_normed_mid, axis=0),
                jnp.sum(grad_normed_mid * normed, axis=0),
                jnp.sum(grad_out * keep * mlp_out, axis=0),
            ]
        )
    )
    late = all_sum(
        by_crop(
            [jnp.sum(grad_normed_in, axis=0), jnp.sum(grad_normed_in * normed_tokens, axis=0)]
        )
    )
    mod_grads = jnp.concatenate([late, early], axis=1)
    if rows == 2:
        own = pick(mod_grads[:, : 3 * D], mod_grads[:, 3 * D :])
        other = cross(pick(mod_grads[:, 3 * D :], mod_grads[:, : 3 * D]))
        mod_grads = jnp.stack([own, other])
    else:
        split = jnp.transpose(mod_grads.reshape(crops, rows, columns), (1, 0, 2))
        mod_grads = lax.all_to_all(split, "fsdp", 0, 0)
    ada_grad = lax.dot_general(
        cond_rows.reshape(rows * crops, D),
        mod_grads.reshape(rows * crops, columns),
        (((0,), (0,)), ((), ())),
        preferred_element_type=f32,
    )

    def term(acts, grads):
        return lax.dot_general(
            acts, grads, (((0,), (0,)), ((), ())), preferred_element_type=f32
        ).astype(bf16)

    if not fast:

        def both(value):
            value = lax.psum_scatter(value, "fsdp", scatter_dimension=0, tiled=True)
            return lax.psum_scatter(value, "seq", scatter_dimension=1, tiled=True).astype(f32)

        grad_qkv = jnp.concatenate([grad_queries, grad_kv], axis=1)
        qkv_grad = both(term(normed_in, grad_qkv))
        out_grad = both(term(merged, grad_attn))
        up_cols = lax.all_to_all(term(mid_rows, grad_pre), "fsdp", 0, 1, tiled=True)
        up_grad = lax.psum_scatter(up_cols, "seq", scatter_dimension=1, tiled=True).astype(f32)
        down_cols = term(hidden_act, grad_mlp_rows)
        down_grad = lax.psum_scatter(
            down_cols, "seq", scatter_dimension=1, tiled=True
        ).astype(f32)
    else:

        def pooled(grads, acts, chunks):
            grads = grads.reshape(chunks, 2, grads.shape[0] // (2 * chunks), grads.shape[1])
            mine = lax.dynamic_index_in_dim(grads, core, 1, keepdims=False)
            other = lax.dynamic_index_in_dim(grads, 1 - core, 1, keepdims=False)
            grads = jnp.concatenate([mine, flip(other, 1)], axis=2)
            acts = jnp.concatenate([acts, flip(acts, 1)], axis=0)
            result = lax.dot_general(
                grads.reshape(-1, grads.shape[2]),
                acts,
                (((1,), (0,)), ((), ())),
                preferred_element_type=f32,
            ).astype(bf16)
            return result.reshape(chunks, -1, acts.shape[1])

        bits = {2: 8, 1: 4, 0: 2}

        def scatter(value, axes):
            axes = list(axes)
            for position, axis in enumerate(axes):
                bit = bits[axis]
                at = (seq_at // bit) % 2
                where = 2 - axis
                keep_part = lax.dynamic_index_in_dim(value, at, where, keepdims=True)
                send_part = lax.dynamic_index_in_dim(value, 1 - at, where, keepdims=True)
                value = keep_part.astype(f32) + flip(send_part, bit).astype(f32)
                if position < len(axes) - 1:
                    value = value.astype(bf16)
            return value[0, 0, 0]

        def own_half(value):
            return pick(value[:, :half], value[:, half:])

        def two_rows(acts):
            sent = pick(acts[:, half:], acts[:, :half])
            return jnp.concatenate([own_half(acts), cross(sent)], axis=0)

        def two_grads(grads):
            return jnp.concatenate([grads, cross(grads)], axis=1)

        down_value = pooled(jnp.transpose(grad_mlp_rows), hidden_act, 8)
        down_grad = scatter(down_value.reshape(2, 2, 2, *down_value.shape[1:]), (0, 1, 2))
        down_grad = jnp.transpose(down_grad)

        up_value = pooled(jnp.transpose(grad_pre), mid_rows, 4)
        chunk = up_value.shape[1]
        up_value = up_value.reshape(2, 2, chunk, 2, half)
        up_value = jnp.transpose(up_value, (3, 0, 1, 2, 4))
        up_mine = scatter(up_value, (1, 0, 2)).astype(bf16)
        pairs = []
        for place_seq in range(seq):
            for place_row in range(2):
                high = (place_seq // 8) % 2
                target_seq = (place_seq & 7) | (place_row * 8)
                pairs.append((place_seq * 2 + place_row, target_seq * 2 + high))
        up_grad = jnp.transpose(lax.ppermute(up_mine, ("seq", "fsdp"), pairs)).astype(f32)

        out_value = pooled(two_grads(jnp.transpose(grad_attn)), two_rows(merged), 8)
        out_grad = scatter(out_value.reshape(2, 2, 2, *out_value.shape[1:]), (0, 1, 2))
        out_grad = jnp.transpose(out_grad)

        grad_qkv = jnp.concatenate([grad_queries, grad_kv], axis=1)
        qkv_value = pooled(two_grads(jnp.transpose(grad_qkv)), two_rows(normed_in), 8)
        qkv_grad = scatter(qkv_value.reshape(2, 2, 2, *qkv_value.shape[1:]), (0, 1, 2))
        qkv_grad = jnp.transpose(qkv_grad)

    return (
        block_out[None],
        input_grad[None],
        qkv_grad,
        out_grad,
        up_grad,
        down_grad,
        ada_grad,
    )


def solution(mesh):
    in_specs = (
        P("fsdp", "seq", None),
        P("fsdp", None, None),
        P("fsdp", None),
        P("fsdp", None),
        P("fsdp", None, None),
        P("fsdp", None, None),
        P("fsdp", "seq"),
        P("fsdp", None),
        P("fsdp", None),
        P("fsdp", None),
        P("fsdp", None),
        P(None, "fsdp"),
        P("fsdp", "seq", None),
    )
    out_specs = (
        P("fsdp", "seq", None),
        P("fsdp", "seq", None),
        P("fsdp", "seq"),
        P("fsdp", "seq"),
        P("fsdp", "seq"),
        P("fsdp", "seq"),
        P(None, "fsdp"),
    )
    return jax.shard_map(local, mesh=mesh, in_specs=in_specs, out_specs=out_specs, check_vma=False)
```

```python
import functools

import jax
import jax.numpy as jnp
import numpy as np
from jax import lax
from jax.experimental import pallas as pl
from jax.experimental.pallas import tpu as pltpu
from jax.sharding import PartitionSpec as P

D = 1152
H = 16
HD = 72
CHAN_GROUP = 128
PIECE_MAX = 16
PERIOD = 16

bf16 = jnp.bfloat16
f32 = jnp.float32
highest = lax.Precision.HIGHEST
norm_epsilon = 1e-06
masked_score = -1e30
score_scale = HD ** (-0.5)
VMEM_LIMIT = 56 * 1024 * 1024
VMEM_SPEC = pl.BlockSpec(memory_space=pltpu.VMEM)


def params():
    return pltpu.CompilerParams(vmem_limit_bytes=VMEM_LIMIT)


def dot_nt(a, b):
    return lax.dot_general(a, b, (((1,), (1,)), ((), ())), preferred_element_type=f32)


def dot_nn(a, b):
    return lax.dot_general(a, b, (((1,), (0,)), ((), ())), preferred_element_type=f32)


def dot_tn(a, b):
    return lax.dot_general(a, b, (((0,), (0,)), ((), ())), preferred_element_type=f32)


def source_inputs(sources):
    arrays = [source[0] for source in sources]
    specs = [pl.BlockSpec(source[1], source[2]) for source in sources]
    parts = [(source[3], source[4]) for source in sources]
    return arrays, specs, parts


def fill(target_ref, place_ref, refs, parts):
    half = target_ref.shape[0] // 2
    mine, quarter = place_ref[0], place_ref[1]
    for ref, (step, column) in zip(refs, parts):
        rows, cols = ref.shape
        if step == "all":
            start = 0
        elif step is None:
            start = pl.multiple_of(mine * half, 16)
        else:
            start = pl.multiple_of((1 - mine) * half + (quarter ^ step) * rows, 16)
        target_ref[pl.ds(start, rows), pl.ds(column, cols)] = ref[...]


def whole(shape):
    return pl.BlockSpec(shape, lambda i, place: (0,) * len(shape))


def staged_call(kernel, place, sources, inputs, out_shapes, scratch, name):
    arrays, specs, parts = source_inputs(sources)
    return pl.pallas_call(
        functools.partial(kernel, parts=parts),
        out_shape=out_shapes,
        grid_spec=pltpu.PrefetchScalarGridSpec(
            num_scalar_prefetch=1,
            grid=(1,),
            in_specs=specs + [whole(value.shape) for value in inputs],
            out_specs=[whole(out.shape) for out in out_shapes],
            scratch_shapes=scratch,
        ),
        compiler_params=params(),
        name=name,
    )(place, *arrays, *inputs)


def shaped(*shape, dtype=f32):
    return jax.ShapeDtypeStruct(shape, dtype)


def normalized(values):
    centred = values - jnp.mean(values, axis=1, keepdims=True)
    inverse = lax.rsqrt(jnp.mean(centred * centred, axis=1, keepdims=True) + norm_epsilon)
    return centred * inverse, inverse


def normalized_back(grad, normed, inverse):
    mean_grad = jnp.mean(grad, axis=1, keepdims=True)
    mean_dot = jnp.mean(grad * normed, axis=1, keepdims=True)
    return (grad - mean_grad - normed * mean_dot) * inverse


def norm_in_kernel(tokens_ref, shift_ref, scale_ref, out_ref):
    for start in range(0, tokens_ref.shape[0], PERIOD):
        rows = pl.ds(start, PERIOD)
        normed, ignored = normalized(tokens_ref[rows, :].astype(f32))
        out_ref[rows, :] = (normed * (1.0 + scale_ref[...]) + shift_ref[...]).astype(bf16)


def norm_in(tokens, shift, scale):
    return pl.pallas_call(
        norm_in_kernel,
        out_shape=shaped(*tokens.shape, dtype=bf16),
        in_specs=[VMEM_SPEC] * 3,
        out_specs=VMEM_SPEC,
        compiler_params=params(),
        name="norm_in",
    )(tokens, shift, scale)


def project_kernel(place_ref, *refs, parts):
    count = len(parts)
    weight_ref, window_ref = refs[-2], refs[-1]
    q_ref, kv_ref = refs[-4], refs[-3]
    window_parts = refs[count:-4]
    fill(weight_ref, place_ref, refs[:count], parts)
    tokens = q_ref.shape[0]
    for index, part in enumerate(window_parts):
        window_ref[pl.ds(index * tokens, tokens), :] = part[...]
    for start in range(0, 2 * D, 768):
        kv_ref[:, pl.ds(start, 768)] = dot_nn(
            window_ref[...], weight_ref[:, pl.ds(D + start, 768)]
        ).astype(bf16)
    for start in range(0, D, 384):
        q_ref[:, pl.ds(start, 384)] = dot_nn(
            window_parts[0][...], weight_ref[:, pl.ds(start, 384)]
        ).astype(bf16)


def project(place, sources, window_parts):
    tokens = window_parts[0].shape[0]
    keys = tokens * len(window_parts)
    return staged_call(
        project_kernel,
        place,
        sources,
        window_parts,
        [shaped(tokens, D, dtype=bf16), shaped(keys, 2 * D, dtype=bf16)],
        [pltpu.VMEM((D, 3 * D), bf16), pltpu.VMEM((keys, D), bf16)],
        "project",
    )


def head_window(head):
    start = head * HD
    low = start // 128 * 128
    width = 128 if start + HD - low <= 128 else 256
    return low, min(width, D - low), start - low


def head_lanes(rows, width, first):
    lane = lax.broadcasted_iota(jnp.int32, (rows, width), 1)
    return (lane >= first) & (lane < first + HD)


def attend_kernel(place_ref, *refs, parts):
    count = len(parts)
    q_ref, kv_ref, bias_ref, mask_ref, tokens_ref, gate_ref, shift_ref, scale_ref = refs[
        count : count + 8
    ]
    merged_ref, proj_ref, mid_ref, normed_ref, acc_ref, weight_ref = refs[count + 8 :]
    tokens = q_ref.shape[0]
    fill(weight_ref, place_ref, refs[:count], parts)
    acc_ref[...] = jnp.zeros_like(acc_ref)
    for head in range(H):
        low, width, first = head_window(head)
        window = pl.ds(low, width)
        lanes = head_lanes(tokens, width, first)
        query = jnp.where(lanes, q_ref[:, window], jnp.zeros((), bf16))
        scores = dot_nt(query, kv_ref[:, window]) * score_scale + bias_ref[...]
        top = jnp.max(scores, axis=1, keepdims=True)
        weights = jnp.exp(scores - top)
        probs = (weights * (1.0 / jnp.sum(weights, axis=1, keepdims=True))).astype(bf16)
        out = dot_nn(probs, kv_ref[:, pl.ds(D + low, width)])
        acc_ref[:, window] += jnp.where(lanes, out, 0.0)
    for start in range(0, tokens, PERIOD):
        rows = pl.ds(start, PERIOD)
        merged_ref[rows, :] = (acc_ref[rows, :] * mask_ref[...]).astype(bf16)
    proj_ref[...] = dot_nn(merged_ref[...], weight_ref[...])
    for start in range(0, tokens, PERIOD):
        rows = pl.ds(start, PERIOD)
        mid = tokens_ref[rows, :].astype(f32) + gate_ref[...] * proj_ref[rows, :]
        mid_ref[rows, :] = mid
        normed, ignored = normalized(mid)
        normed_ref[rows, :] = (normed * (1.0 + scale_ref[...]) + shift_ref[...]).astype(bf16)


def attend(place, sources, *inputs):
    tokens = inputs[0].shape[0]
    return staged_call(
        attend_kernel,
        place,
        sources,
        inputs,
        [
            shaped(tokens, D, dtype=bf16),
            shaped(tokens, D),
            shaped(tokens, D),
            shaped(tokens, D, dtype=bf16),
        ],
        [pltpu.VMEM((tokens, D), f32), pltpu.VMEM((D, D), bf16)],
        "attend",
    )


def attend_back_kernel(
    q_ref, kv_ref, bias_ref, grad_ref, dq_ref, dkv_ref, dq_acc, dk_acc, dv_acc
):
    tokens = q_ref.shape[0]
    dq_acc[...] = jnp.zeros_like(dq_acc)
    dk_acc[...] = jnp.zeros_like(dk_acc)
    dv_acc[...] = jnp.zeros_like(dv_acc)
    for head in range(H):
        low, width, first = head_window(head)
        window = pl.ds(low, width)
        lanes = head_lanes(tokens, width, first)
        query = jnp.where(lanes, q_ref[:, window], jnp.zeros((), bf16))
        grad = jnp.where(lanes, grad_ref[:, window], jnp.zeros((), bf16))
        keys = kv_ref[:, window]
        scores = dot_nt(keys, query) * score_scale + bias_ref[...]
        top = jnp.max(scores, axis=0, keepdims=True)
        weights = jnp.exp(scores - top)
        probs = weights * (1.0 / jnp.sum(weights, axis=0, keepdims=True))
        probs_low = probs.astype(bf16)
        grad_probs = dot_nt(kv_ref[:, pl.ds(D + low, width)], grad)
        row_dot = jnp.sum(probs_low.astype(f32) * grad_probs, axis=0, keepdims=True)
        grad_scores = (probs * (grad_probs - row_dot)).astype(bf16)
        dk_acc[:, window] += dot_nn(grad_scores, query)
        dv_acc[:, window] += dot_nn(probs_low, grad)
        dq_acc[:, window] += jnp.where(lanes, dot_tn(grad_scores, keys), 0.0)
    dq_ref[...] = (dq_acc[...] * score_scale).astype(bf16)
    for index in range(dkv_ref.shape[0]):
        rows = pl.ds(index * tokens, tokens)
        dkv_ref[index, :, pl.ds(0, D)] = (dk_acc[rows, :] * score_scale).astype(bf16)
        dkv_ref[index, :, pl.ds(D, D)] = dv_acc[rows, :].astype(bf16)


def attend_back(queries, kv_window, bias_t, grad_heads):
    tokens = queries.shape[0]
    keys = kv_window.shape[0]
    return pl.pallas_call(
        attend_back_kernel,
        out_shape=(
            shaped(tokens, D, dtype=bf16),
            shaped(keys // tokens, tokens, 2 * D, dtype=bf16),
        ),
        in_specs=[VMEM_SPEC] * 4,
        out_specs=(VMEM_SPEC,) * 2,
        scratch_shapes=[
            pltpu.VMEM((tokens, D), f32),
            pltpu.VMEM((keys, D), f32),
            pltpu.VMEM((keys, D), f32),
        ],
        compiler_params=params(),
        name="attend_back",
    )(queries, kv_window, bias_t, grad_heads)


def feed_kernel(place_ref, *refs, parts, own_rows):
    count = len(parts)
    mid_ref, grad_ref, channel_ref, down_ref = refs[count : count + 4]
    act_ref, pre_ref, grad_own, grad_low, out_own, out_low = refs[count + 4 : count + 10]
    weight_ref, grad_acc, out_acc = refs[count + 10 :]
    step, steps = pl.program_id(0), pl.num_programs(0)
    rows, cols = act_ref.shape
    groups = channel_ref.shape[0]
    tokens = rows // groups

    @pl.when(step == 0)
    def _():
        grad_acc[...] = jnp.zeros_like(grad_acc)
        out_acc[...] = jnp.zeros_like(out_acc)

    fill(weight_ref, place_ref, refs[:count], parts)
    root = 0.7978845608028654
    for group in range(groups):
        span = pl.ds(group * tokens, tokens)
        channels = jnp.concatenate([channel_ref[group]] * (tokens // PERIOD), axis=0)
        pre = dot_nn(mid_ref[span, :], weight_ref[...])
        grad_act = dot_nt(grad_ref[span, :], down_ref[...])
        square = pre * pre
        inner = jnp.tanh(root * (pre + 0.044715 * (square * pre)))
        half_sum = 0.5 + 0.5 * inner
        act_ref[span, :] = (pre * half_sum * channels).astype(bf16)
        slope = half_sum + (0.5 * pre) * (1.0 - inner * inner) * (
            root + (3.0 * 0.044715 * root) * square
        )
        pre_ref[span, :] = (grad_act * channels * slope).astype(bf16)
    grad_acc[...] += dot_nt(pre_ref[...], weight_ref[...])
    out_acc[...] += dot_nn(act_ref[...], down_ref[...])

    @pl.when(step == steps - 1)
    def _():
        skip = rows - grad_low.shape[0]
        grad_own[...] = grad_acc[pl.ds(0, own_rows), :]
        out_own[...] = out_acc[pl.ds(0, own_rows), :]
        grad_low[...] = grad_acc[pl.ds(skip, rows - skip), :].astype(bf16)
        out_low[...] = out_acc[pl.ds(skip, rows - skip), :].astype(bf16)


def feed(place, sources, mid_rows, grad_rows, channels, down, chunk, tokens, low_rows):
    arrays, specs, parts = source_inputs(sources)
    rows = mid_rows.shape[0]
    width = down.shape[0]
    by_chunk = pl.BlockSpec((rows, chunk), lambda i, place: (0, i))
    own, low = (tokens, D), (low_rows, D)
    return pl.pallas_call(
        functools.partial(feed_kernel, parts=parts, own_rows=tokens),
        out_shape=[
            shaped(rows, width, dtype=bf16),
            shaped(rows, width, dtype=bf16),
            shaped(*own),
            shaped(*low, dtype=bf16),
            shaped(*own),
            shaped(*low, dtype=bf16),
        ],
        grid_spec=pltpu.PrefetchScalarGridSpec(
            num_scalar_prefetch=1,
            grid=(width // chunk,),
            in_specs=specs
            + [
                whole((rows, D)),
                whole((rows, D)),
                pl.BlockSpec(
                    (channels.shape[0], PERIOD, chunk), lambda i, place: (0, 0, i)
                ),
                pl.BlockSpec((chunk, D), lambda i, place: (i, 0)),
            ],
            out_specs=[by_chunk, by_chunk, whole(own), whole(low), whole(own), whole(low)],
            scratch_shapes=[
                pltpu.VMEM((D, chunk), bf16),
                pltpu.VMEM((rows, D), f32),
                pltpu.VMEM((rows, D), f32),
            ],
        ),
        compiler_params=params(),
        name="feed",
    )(place, *arrays, mid_rows, grad_rows, channels, down)


def mid_back_kernel(place_ref, *refs, parts):
    count = len(parts)
    own_ref, other_ref, mid_ref, proj_ref, late_ref, scale_ref, gate_ref, mask_ref = refs[
        count : count + 8
    ]
    grad_mid_ref, grad_attn_ref, heads_ref, sums_ref, weight_ref, merged_ref = refs[count + 8 :]
    tokens = own_ref.shape[0]
    fill(weight_ref, place_ref, refs[:count], parts)
    gate_sum = jnp.zeros((PERIOD, D), f32)
    shift_sum = jnp.zeros((PERIOD, D), f32)
    scale_sum = jnp.zeros((PERIOD, D), f32)
    for start in range(0, tokens, PERIOD):
        rows = pl.ds(start, PERIOD)
        normed, inverse = normalized(mid_ref[rows, :])
        grad = own_ref[rows, :] + other_ref[rows, :].astype(f32)
        grad_mid = late_ref[rows, pl.ds(0, D)].astype(f32) + normalized_back(
            grad * (1.0 + scale_ref[...]), normed, inverse
        )
        grad_mid_ref[rows, :] = grad_mid
        grad_attn_ref[rows, :] = (grad_mid * gate_ref[...]).astype(bf16)
        gate_sum += grad_mid * proj_ref[rows, :]
        shift_sum += grad
        scale_sum += grad * normed
    sums_ref[0] = gate_sum
    sums_ref[1] = shift_sum
    sums_ref[2] = scale_sum
    merged_ref[...] = dot_nt(grad_attn_ref[...], weight_ref[...])
    for start in range(0, tokens, PERIOD):
        rows = pl.ds(start, PERIOD)
        heads_ref[rows, :] = (merged_ref[rows, :] * mask_ref[...]).astype(bf16)


def mid_back(place, sources, *inputs):
    tokens = inputs[0].shape[0]
    return staged_call(
        mid_back_kernel,
        place,
        sources,
        inputs,
        [
            shaped(tokens, D),
            shaped(tokens, D, dtype=bf16),
            shaped(tokens, D, dtype=bf16),
            shaped(3, PERIOD, D),
        ],
        [pltpu.VMEM((D, D), bf16), pltpu.VMEM((tokens, D), f32)],
        "mid_back",
    )


def in_back_kernel(place_ref, *refs, parts):
    count = len(parts)
    dq_ref, dkv_ref, tokens_ref, scale_ref, grad_mid_ref = refs[count : count + 5]
    grad_in_ref, sums_ref, weight_ref, grad_ref = refs[count + 5 :]
    tokens = dq_ref.shape[0]
    fill(weight_ref, place_ref, refs[:count], parts)
    grad_ref[...] = dot_nt(dkv_ref[...], weight_ref[:, pl.ds(D, 2 * D)]) + dot_nt(
        dq_ref[...], weight_ref[:, pl.ds(0, D)]
    )
    shift_sum = jnp.zeros((PERIOD, D), f32)
    scale_sum = jnp.zeros((PERIOD, D), f32)
    for start in range(0, tokens, PERIOD):
        rows = pl.ds(start, PERIOD)
        normed, inverse = normalized(tokens_ref[rows, :].astype(f32))
        grad = grad_ref[rows, :]
        back = normalized_back(grad * (1.0 + scale_ref[...]), normed, inverse)
        grad_in_ref[rows, :] = (grad_mid_ref[rows, :] + back).astype(bf16)
        shift_sum += grad
        scale_sum += grad * normed
    sums_ref[0] = shift_sum
    sums_ref[1] = scale_sum


def in_back(place, sources, *inputs):
    tokens = inputs[0].shape[0]
    return staged_call(
        in_back_kernel,
        place,
        sources,
        inputs,
        [shaped(tokens, D, dtype=bf16), shaped(2, PERIOD, D)],
        [pltpu.VMEM((D, 3 * D), bf16), pltpu.VMEM((tokens, D), f32)],
        "in_back",
    )


def term_kernel(place_ref, *refs, pairs, chunk, plan):
    acc_ref = refs[-1]
    for index in range(pairs):
        value = None
        grads, acts = refs[2 * index], refs[2 * index + 1]
        width = acts.shape[1]
        for start in range(0, width, 576):
            span = pl.ds(start, 576)
            value = dot_tn(grads[...], acts[:, span])
            acc_ref[:, span] = value if index == 0 else acc_ref[:, span] + value
    core = place_ref[2]
    outs = refs[2 * pairs : -1]
    for out_index, (first, count, axis) in enumerate(plan):
        send_ref, keep_ref = outs[2 * out_index], outs[2 * out_index + 1]
        at = place_ref[3 + axis]
        width = send_ref.shape[-1]
        for target, side in ((send_ref, 1 - at), (keep_ref, at)):
            blocks = target.shape[0]
            for block in range(blocks):
                pieces = acc_ref.shape[1] // width
                lane, rest = block // (blocks // pieces), block % (blocks // pieces)
                if axis == 0:
                    line = rest * 4 + side * 2 + core
                else:
                    line = (rest // 2) * 8 + side * 4 + (rest % 2) * 2 + core
                start = pl.multiple_of(line * chunk + first, 8)
                target[block] = acc_ref[pl.ds(start, count), pl.ds(lane * width, width)].astype(
                    bf16
                )


def term(place, pairs, plan, blocks, width):
    columns = pairs[0][0].shape[1]
    rows = pairs[0][1].shape[1]
    chunk = columns // (4 * blocks * width // rows)
    flat = [value for pair in pairs for value in pair]
    outs = []
    for first, count, axis in plan:
        outs += [shaped(blocks, count, width, dtype=bf16)] * 2
    return pl.pallas_call(
        functools.partial(term_kernel, pairs=len(pairs), chunk=chunk, plan=plan),
        out_shape=outs,
        in_specs=[pl.BlockSpec(memory_space=pltpu.SMEM)] + [VMEM_SPEC] * len(flat),
        out_specs=[VMEM_SPEC] * len(outs),
        scratch_shapes=[pltpu.VMEM((columns, rows), f32)],
        compiler_params=params(),
        name="term",
    )(place, *flat)


def running_ends(pieces):
    index = jnp.arange(pieces.shape[0], dtype=jnp.int32)
    return jnp.sum(jnp.where(index[None, :] <= index[:, None], pieces[None, :], 0), axis=1)


def crop_of(slots, ends):
    return jnp.sum((slots[..., None] >= ends[:-1]).astype(jnp.int32), axis=-1)


def one_hot(crops, count):
    return (crops[..., None] == jnp.arange(count, dtype=jnp.int32)).astype(f32)


def block_order(size):
    def device(block):
        chip, core = block // 2, block % 2
        return 2 * (chip ^ ((chip >> 1) & 1)) + core if size % 8 == 0 else block

    return [device(block) for block in range(size)]


def local(
    tokens_in,
    condition,
    crop_pieces,
    pad_counts,
    head_mask,
    channel_mask,
    keep_mask,
    qkv_weight,
    out_weight,
    up_weight,
    down_weight,
    ada_weight,
    cotangent,
):
    seq = lax.axis_size("seq")
    rows = lax.axis_size("fsdp")
    tokens = tokens_in.shape[1]
    slots = tokens // seq
    repeats = PERIOD // slots
    crops = crop_pieces.shape[1]
    hidden = up_weight.shape[1]
    hidden_part = hidden // rows
    half = D // rows
    seq_at = lax.axis_index("seq")
    row_at = lax.axis_index("fsdp")
    fast = rows == 2 and seq == 16
    order = block_order(seq)
    core = seq_at % 2
    if seq % 8 == 0:
        chip = seq_at // 2
        block_at = 2 * (chip ^ ((chip >> 1) & 1)) + core
    else:
        block_at = seq_at
    place = jnp.stack(
        [row_at, seq_at & 3, core, (seq_at // 2) % 2, (seq_at // 4) % 2]
    ).astype(jnp.int32)

    def flip(value, bit):
        return lax.ppermute(value, "seq", [(i, i ^ bit) for i in range(seq)])

    def cross(value):
        return lax.ppermute(value, "fsdp", [(0, 1), (1, 0)])

    def shift(value, distance):
        pairs = [
            (order[b], order[b + distance]) for b in range(seq) if 0 <= b + distance < seq
        ]
        return lax.ppermute(value, "seq", pairs)

    swap_rows = jnp.asarray(
        np.kron(np.eye(seq)[np.array(order)], np.eye(slots)), bf16
    )

    def to_slots(value):
        moved = jnp.dot(swap_rows, value, preferred_element_type=f32).astype(bf16)
        moved = lax.all_to_all(moved.reshape(seq, slots, -1), "seq", 0, 0)
        return moved.reshape(tokens, -1)

    def from_slots(value, dtype):
        value = lax.all_to_all(value.reshape(seq, slots, -1), "seq", 0, 0)
        value = value.reshape(tokens, -1)
        return jnp.dot(swap_rows, value, preferred_element_type=f32).astype(dtype)

    def after(value, *earlier):
        return lax.optimization_barrier((value, *earlier))[0]

    def gather_rows(value):
        if rows == 2:
            return jnp.stack([value, cross(value)])
        return lax.all_gather(value, "fsdp", axis=0)

    def pick(low_part, high_part):
        return jnp.where(row_at == 0, low_part, high_part)

    def tiled(value):
        return jnp.concatenate([value] * repeats, axis=-2) if repeats > 1 else value

    slot_index = block_at * slots + jnp.arange(slots, dtype=jnp.int32)
    ends = running_ends(crop_pieces[0])
    crop_here = crop_of(slot_index, ends)
    selector = one_hot(crop_here, crops)
    pads = pad_counts[0]

    cond_act = jax.nn.silu(condition[0]).astype(bf16)
    extra = jnp.concatenate(
        [channel_mask[0].astype(bf16), crop_pieces[0].astype(bf16)[:, None]], axis=1
    )
    extra = jnp.pad(extra, ((0, 0), (0, 128 - extra.shape[1])))
    packed = gather_rows(jnp.concatenate([cond_act, extra], axis=1))
    groups = channel_mask.shape[2]
    cond_rows = packed[:, :, :D].reshape(rows * crops, D)
    group_rows = packed[:, :, D : D + groups].astype(f32)
    ends_rows = jax.vmap(running_ends)(packed[:, :, D + groups].astype(jnp.int32))
    selector_rows = jax.vmap(lambda own: one_hot(crop_of(slot_index, own), crops))(ends_rows)

    columns = ada_weight.shape[1]
    mod_rows = jnp.dot(cond_rows, ada_weight, preferred_element_type=f32)
    mod_rows = mod_rows.reshape(rows, crops, columns)
    if rows == 2:
        mod_slots = jnp.einsum("rsc,rcm->rsm", selector_rows, mod_rows, precision=highest)
        arrived = cross(mod_slots[1])
        mod_attn = pick(mod_slots[0], arrived)
        mod_mlp = pick(arrived, mod_slots[0])
    else:
        mine = lax.all_to_all(mod_rows, "fsdp", 0, 0)
        mine = jnp.transpose(mine, (1, 0, 2)).reshape(crops, rows * columns)
        mine = jnp.dot(selector, mine, precision=highest)
        mod_attn, mod_mlp = mine[:, : 3 * D], mine[:, 3 * D :]
    mod_attn, mod_mlp = tiled(mod_attn), tiled(mod_mlp)
    shift_attn, scale_attn, gate_attn = (mod_attn[:, i * D : (i + 1) * D] for i in range(3))
    shift_mlp, scale_mlp, gate_mlp = (mod_mlp[:, i * D : (i + 1) * D] for i in range(3))

    def block(at):
        return lambda i, place: (0, at)

    if fast:
        quarter = half // 4
        chunk = 768

        def fetch(weight, column, cols, *earlier):
            part = lax.dynamic_slice(weight, ((seq_at & 3) * quarter, column), (quarter, cols))
            first = cross(after(part, *earlier))
            second = flip(first, 2)
            return (first, flip(first, 1), second, flip(second, 1))

        other_part = (1 - row_at) * hidden_part
        k_pieces = fetch(qkv_weight, D, D, packed)
        v_pieces = fetch(qkv_weight, 2 * D, D, k_pieces[0], mod_slots)
        q_pieces = fetch(qkv_weight, 0, D, k_pieces[0], mod_slots)
        out_pieces = fetch(out_weight, 0, D, v_pieces[0])
        up_low = fetch(up_weight, other_part, hidden_part // 2, q_pieces[0])
        up_high = fetch(
            up_weight, other_part + hidden_part // 2, hidden_part // 2, out_pieces[0]
        )
        qkv_sources = [(qkv_weight, (half, 3 * D), block(0), None, 0)]
        for column, pieces in ((0, q_pieces), (D, k_pieces), (2 * D, v_pieces)):
            qkv_sources += [
                (piece, (quarter, D), block(0), step, column)
                for step, piece in enumerate(pieces)
            ]
        out_sources = [(out_weight, (half, D), block(0), None, 0)]
        out_sources += [
            (piece, (quarter, D), block(0), step, 0) for step, piece in enumerate(out_pieces)
        ]
        chunks = hidden_part // chunk
        up_sources = [
            (up_weight, (half, chunk), lambda i, place: (0, place[0] * chunks + i), None, 0)
        ]
        up_sources += [
            (
                jnp.concatenate([low, high], axis=1),
                (quarter, chunk),
                lambda i, place: (0, i),
                step,
                0,
            )
            for step, (low, high) in enumerate(zip(up_low, up_high))
        ]
        low_rows = tokens
    else:
        chunk = hidden_part
        qkv_full = lax.all_gather(qkv_weight, "fsdp", axis=0, tiled=True)
        out_full = lax.all_gather(out_weight, "fsdp", axis=0, tiled=True)
        up_part = lax.all_to_all(up_weight, "fsdp", 1, 0, tiled=True)
        qkv_sources = [(qkv_full, (D, 3 * D), block(0), "all", 0)]
        out_sources = [(out_full, (D, D), block(0), "all", 0)]
        up_sources = [(up_part, (D, hidden_part), block(0), "all", 0)]
        low_rows = rows * tokens

    tokens_here = to_slots(tokens_in[0])
    kept = jnp.broadcast_to(keep_mask[0].astype(bf16)[:, None], (tokens, 128))
    normed_in = norm_in(tokens_here, shift_attn, scale_attn)

    reach = -(-(PIECE_MAX - 1) // slots)
    paired = reach == 2 and seq % 2 == 0
    if paired:
        below, above = shift(normed_in, 2), shift(normed_in, -2)
        passed = flip(jnp.where(core == 0, above, below), 1)
        near = [normed_in, flip(normed_in, 1), below, above, passed]
        near_at = [
            block_at,
            block_at ^ 1,
            block_at - 2,
            block_at + 2,
            block_at - 1 + 2 * core,
        ]
    else:
        near, near_at = [normed_in], [block_at]
        for distance in range(1, reach + 1):
            near += [shift(normed_in, distance), shift(normed_in, -distance)]
            near_at += [block_at - distance, block_at + distance]
    late_in = to_slots(after(jnp.concatenate([cotangent[0], kept], axis=1), normed_in))
    near_at = jnp.stack(near_at)
    key_slots = near_at[:, None] * slots + jnp.arange(slots, dtype=jnp.int32)[None, :]
    inside = (near_at >= 0) & (near_at < seq)
    key_crop = jnp.where(inside[:, None], crop_of(key_slots, ends), -1)
    key_crop = jnp.where(
        key_slots[:, None, :] < tokens - pads[None, :, None], key_crop[:, None, :], -1
    ).reshape(-1)
    query_crop = jnp.broadcast_to(crop_here[None, :], (seq, slots)).reshape(tokens)
    bias = jnp.where(query_crop[:, None] == key_crop[None, :], 0.0, masked_score).astype(f32)
    bias_t = jnp.where(key_crop[:, None] == query_crop[None, :], 0.0, masked_score).astype(f32)
    head_slots = tiled(
        jnp.repeat(jnp.dot(selector, head_mask[0].astype(f32), precision=highest), HD, axis=1)
    )

    def by_slot(value):
        return value.reshape(tokens // PERIOD, PERIOD, -1)

    queries, kv_window = project(place, qkv_sources, near)
    grad_mlp = by_slot(late_in[:, :D].astype(f32)) * gate_mlp
    grad_mlp = (grad_mlp * by_slot(late_in[:, D : D + 1].astype(f32))).reshape(tokens, D)
    grad_mlp_rows = gather_rows(grad_mlp.astype(bf16)).reshape(rows * tokens, D)
    queries = after(queries, grad_mlp)
    merged, attn_proj, mid_state, normed_mid = attend(
        place,
        out_sources,
        queries,
        kv_window,
        bias,
        head_slots,
        tokens_here,
        gate_attn,
        shift_mlp,
        scale_mlp,
    )

    mid_rows = gather_rows(normed_mid).reshape(rows * tokens, D)
    channels = jnp.einsum("rsc,rcg->rsg", selector_rows, group_rows, precision=highest)
    channels = lax.dynamic_slice_in_dim(
        jnp.repeat(tiled(channels), CHAN_GROUP, axis=2), row_at * hidden_part, hidden_part, 2
    )
    hidden_act, grad_pre, grad_own, grad_low, out_own, out_low = feed(
        place,
        up_sources,
        mid_rows,
        grad_mlp_rows,
        channels,
        down_weight,
        chunk,
        tokens,
        low_rows,
    )

    def own_sum(own, low):
        if rows == 2:
            return own, cross(low)
        low = low.reshape(rows, tokens, D)
        low = lax.psum_scatter(low, "fsdp", scatter_dimension=0, tiled=True)
        return jnp.zeros_like(own), low.reshape(tokens, D)

    grad_own, grad_other = own_sum(grad_own, grad_low)
    out_own, out_other = own_sum(out_own, out_low)
    mlp_out = out_own + out_other.astype(f32)
    kept_out = by_slot(mlp_out * late_in[:, D : D + 1].astype(f32))
    block_out = (by_slot(mid_state) + gate_mlp * kept_out).reshape(tokens, D)
    block_out = block_out.astype(bf16)
    gate_mlp_sum = jnp.sum(by_slot(late_in[:, :D].astype(f32)) * kept_out, axis=0)

    if fast:

        def pooled(grads, acts):
            return [(grads, acts), (flip(grads, 1), flip(acts, 1))]

        down_pairs = pooled(grad_mlp_rows, hidden_act)
        up_pairs = pooled(grad_pre, mid_rows)
        down_sent, down_kept = term(place, down_pairs, [(0, D // seq, 0)], 4, hidden_part)
        grad_own = after(grad_own, down_sent)

    grad_mid, grad_attn, grad_heads, mid_sums = mid_back(
        place,
        out_sources,
        grad_own,
        grad_other,
        mid_state,
        attn_proj,
        late_in,
        scale_mlp,
        gate_attn,
        head_slots,
    )
    if fast:

        def own_half(value):
            return pick(value[:, :half], value[:, half:])

        def other_half(value):
            return pick(value[:, half:], value[:, :half])

        crossing = jnp.concatenate(
            [other_half(merged), other_half(normed_in), grad_attn], axis=1
        )
        crossed = cross(crossing)
        grad_heads = after(grad_heads, crossing, up_pairs)
    grad_queries, parts = attend_back(queries, kv_window, bias_t, grad_heads)
    grad_kv = parts[0].astype(f32)
    if paired:
        handed = flip(parts[4], 1).astype(f32)
        down_part = (parts[2].astype(f32) + jnp.where(core == 1, handed, 0.0)).astype(bf16)
        up_side = (parts[3].astype(f32) + jnp.where(core == 0, handed, 0.0)).astype(bf16)
        grad_kv = grad_kv + flip(parts[1], 1).astype(f32)
        if fast:
            block_out, ignored, ignored = lax.optimization_barrier(
                (block_out, down_part, up_side)
            )
            up_ready, ignored, ignored = lax.optimization_barrier(
                (up_pairs, down_part, up_side)
            )
            up_sent, up_kept = term(place, up_ready, [(0, hidden // seq, 0)], 4, half)
            grad_kv = after(grad_kv, up_sent)
        grad_kv = grad_kv + shift(down_part, -2).astype(f32) + shift(up_side, 2).astype(f32)
    else:
        for distance in range(1, reach + 1):
            grad_kv = grad_kv + shift(parts[2 * distance - 1], -distance).astype(f32)
            grad_kv = grad_kv + shift(parts[2 * distance], distance).astype(f32)
    grad_kv = grad_kv.astype(bf16)
    block_out = from_slots(block_out, bf16)
    input_grad, in_sums = in_back(
        place, qkv_sources, grad_queries, grad_kv, tokens_here, scale_attn, grad_mid
    )
    input_grad = from_slots(input_grad, f32)

    def by_crop(sums):
        sums = sums.reshape(-1, repeats, slots, D)
        sums = jnp.sum(sums, axis=1) if repeats > 1 else sums[:, 0]
        return jnp.einsum("sc,nsd->cnd", selector, sums, precision=highest).astype(bf16)

    def all_sum(value):
        if not fast:
            return lax.psum(value, "seq")
        for bit in (1, 2, 4, 8):
            value = (value.astype(f32) + flip(value, bit).astype(f32)).astype(bf16)
        return value

    mod_grads = jnp.concatenate([in_sums, mid_sums, gate_mlp_sum[None]], axis=0)
    mod_grads = all_sum(by_crop(mod_grads).reshape(crops, 6 * D))
    if rows == 2:
        own = pick(mod_grads[:, : 3 * D], mod_grads[:, 3 * D :])
        other = cross(pick(mod_grads[:, 3 * D :], mod_grads[:, : 3 * D]))
        mod_grads = jnp.concatenate([own, other], axis=0)
    else:
        split = jnp.transpose(mod_grads.reshape(crops, rows, columns), (1, 0, 2))
        mod_grads = lax.all_to_all(split, "fsdp", 0, 0).reshape(rows * crops, columns)
    ada_grad = lax.dot_general(
        cond_rows, mod_grads, (((0,), (0,)), ((), ())), preferred_element_type=f32
    )

    if not fast:

        def product(acts, grads):
            return lax.dot_general(
                acts, grads, (((0,), (0,)), ((), ())), preferred_element_type=f32
            ).astype(bf16)

        def both(value):
            value = lax.psum_scatter(value, "fsdp", scatter_dimension=0, tiled=True)
            return lax.psum_scatter(value, "seq", scatter_dimension=1, tiled=True).astype(f32)

        grad_qkv = jnp.concatenate([grad_queries, grad_kv], axis=1)
        qkv_grad = both(product(normed_in, grad_qkv))
        out_grad = both(product(merged, grad_attn))
        up_cols = lax.all_to_all(product(mid_rows, grad_pre), "fsdp", 0, 1, tiled=True)
        up_grad = lax.psum_scatter(up_cols, "seq", scatter_dimension=1, tiled=True).astype(f32)
        down_cols = product(hidden_act, grad_mlp_rows)
        down_grad = lax.psum_scatter(
            down_cols, "seq", scatter_dimension=1, tiled=True
        ).astype(f32)
    else:

        def scatter(sent, kept, bits):
            value = kept.astype(f32) + flip(sent, bits[0]).astype(f32)
            shape = value.shape[1:]
            value = value.reshape(2, 2, *shape).astype(bf16)
            at = (seq_at // bits[2]) % 2
            send = lax.dynamic_index_in_dim(value, 1 - at, 1, keepdims=False)
            keep = lax.dynamic_index_in_dim(value, at, 1, keepdims=False)
            value = (keep.astype(f32) + flip(send, bits[2]).astype(f32)).astype(bf16)
            at = (seq_at // bits[1]) % 2
            send = lax.dynamic_index_in_dim(value, 1 - at, 0, keepdims=False)
            keep = lax.dynamic_index_in_dim(value, at, 0, keepdims=False)
            return keep.astype(f32) + flip(send, bits[1]).astype(f32)

        down_grad = jnp.transpose(scatter(down_sent, down_kept, (2, 8, 4)))
        up_mine = scatter(up_sent, up_kept, (2, 8, 4)).astype(bf16)
        pairs = []
        for place_seq in range(seq):
            for place_row in range(2):
                high = (place_seq // 8) % 2
                target_seq = (place_seq & 7) | (place_row * 8)
                pairs.append((place_seq * 2 + place_row, target_seq * 2 + high))
        up_grad = jnp.transpose(lax.ppermute(up_mine, ("seq", "fsdp"), pairs)).astype(f32)

        out_acts = jnp.concatenate([own_half(merged), crossed[:, :half]], axis=0)
        out_grads = jnp.concatenate([grad_attn, crossed[:, D:]], axis=0)
        out_sent, out_kept = term(
            place,
            pooled(out_grads, out_acts),
            [(0, D // seq, 0)],
            4,
            half,
        )
        out_grad = jnp.transpose(scatter(out_sent, out_kept, (2, 8, 4)))

        q_crossed, kv_crossed = cross(grad_queries), cross(grad_kv)
        qkv_grads = jnp.concatenate(
            [
                jnp.concatenate([grad_queries, q_crossed], axis=0),
                jnp.concatenate([grad_kv, kv_crossed], axis=0),
            ],
            axis=1,
        )
        qkv_acts = jnp.concatenate([own_half(normed_in), crossed[:, half:D]], axis=0)
        first = 3 * D // seq // 16 * 8
        sent_a, kept_a, sent_b, kept_b = term(
            place,
            pooled(qkv_grads, qkv_acts),
            [(0, first, 0), (first, 3 * D // seq - first, 1)],
            4,
            half,
        )
        qkv_grad = jnp.transpose(
            jnp.concatenate(
                [
                    scatter(sent_a, kept_a, (2, 8, 4)),
                    scatter(sent_b, kept_b, (4, 8, 2)),
                ],
                axis=0,
            )
        )

    return (
        block_out[None],
        input_grad[None],
        qkv_grad,
        out_grad,
        up_grad,
        down_grad,
        ada_grad,
    )


def solution(mesh):
    in_specs = (
        P("fsdp", "seq", None),
        P("fsdp", None, None),
        P("fsdp", None),
        P("fsdp", None),
        P("fsdp", None, None),
        P("fsdp", None, None),
        P("fsdp", "seq"),
        P("fsdp", None),
        P("fsdp", None),
        P("fsdp", None),
        P("fsdp", None),
        P(None, "fsdp"),
        P("fsdp", "seq", None),
    )
    out_specs = (
        P("fsdp", "seq", None),
        P("fsdp", "seq", None),
        P("fsdp", "seq"),
        P("fsdp", "seq"),
        P("fsdp", "seq"),
        P("fsdp", "seq"),
        P(None, "fsdp"),
    )
    return jax.shard_map(local, mesh=mesh, in_specs=in_specs, out_specs=out_specs, check_vma=False)
```

```python
import functools

import jax
import jax.numpy as jnp
import numpy as np
from jax import lax
from jax.experimental import pallas as pl
from jax.experimental.pallas import tpu as pltpu
from jax.sharding import PartitionSpec as P

D = 1152
H = 16
HD = 72
CHAN_GROUP = 128
PIECE_MAX = 16
PERIOD = 16

bf16 = jnp.bfloat16
f32 = jnp.float32
highest = lax.Precision.HIGHEST
norm_epsilon = 1e-06
masked_score = -1e30
score_scale = HD ** (-0.5)
VMEM_LIMIT = 56 * 1024 * 1024
VMEM_SPEC = pl.BlockSpec(memory_space=pltpu.VMEM)
COST = pl.CostEstimate(flops=1, transcendentals=0, bytes_accessed=1)


def params():
    return pltpu.CompilerParams(vmem_limit_bytes=VMEM_LIMIT)


def dot_nt(a, b):
    return lax.dot_general(a, b, (((1,), (1,)), ((), ())), preferred_element_type=f32)


def dot_nn(a, b):
    return lax.dot_general(a, b, (((1,), (0,)), ((), ())), preferred_element_type=f32)


def dot_tn(a, b):
    return lax.dot_general(a, b, (((0,), (0,)), ((), ())), preferred_element_type=f32)


def source_inputs(sources):
    arrays = [source[0] for source in sources]
    specs = [pl.BlockSpec(source[1], source[2]) for source in sources]
    parts = [(source[3], source[4]) for source in sources]
    return arrays, specs, parts


def fill(target_ref, place_ref, refs, parts):
    half = target_ref.shape[0] // 2
    mine = place_ref[0]
    for ref, (step, column) in zip(refs, parts):
        rows, cols = ref.shape
        if step == "all":
            start = 0
        elif step is None:
            start = pl.multiple_of(mine * half, 16)
        else:
            quarter = place_ref[step[0]] ^ step[1]
            start = pl.multiple_of((1 - mine) * half + quarter * rows, 16)
        target_ref[pl.ds(start, rows), pl.ds(column, cols)] = ref[...]


def whole(shape):
    return pl.BlockSpec(shape, lambda i, place: (0,) * len(shape))


def staged_call(kernel, place, sources, inputs, out_shapes, scratch, name):
    arrays, specs, parts = source_inputs(sources)
    return pl.pallas_call(
        functools.partial(kernel, parts=parts),
        out_shape=out_shapes,
        grid_spec=pltpu.PrefetchScalarGridSpec(
            num_scalar_prefetch=1,
            grid=(1,),
            in_specs=specs + [whole(value.shape) for value in inputs],
            out_specs=[whole(out.shape) for out in out_shapes],
            scratch_shapes=scratch,
        ),
        compiler_params=params(),
        cost_estimate=COST,
        name=name,
    )(place, *arrays, *inputs)


def shaped(*shape, dtype=f32):
    return jax.ShapeDtypeStruct(shape, dtype)


def normalized(values):
    centred = values - jnp.mean(values, axis=1, keepdims=True)
    inverse = lax.rsqrt(jnp.mean(centred * centred, axis=1, keepdims=True) + norm_epsilon)
    return centred * inverse, inverse


def normalized_back(grad, normed, inverse):
    mean_grad = jnp.mean(grad, axis=1, keepdims=True)
    mean_dot = jnp.mean(grad * normed, axis=1, keepdims=True)
    return (grad - mean_grad - normed * mean_dot) * inverse


def slot_rows(value):
    repeats = PERIOD // value.shape[0]
    return jnp.concatenate([value] * repeats, axis=0) if repeats > 1 else value


def norm_in_kernel(place_ref, tokens_ref, own_ref, other_ref, out_ref):
    first = place_ref[0] == 0
    shift = slot_rows(jnp.where(first, own_ref[:, pl.ds(0, D)], other_ref[:, pl.ds(0, D)]))
    scale = slot_rows(jnp.where(first, own_ref[:, pl.ds(D, D)], other_ref[:, pl.ds(D, D)]))
    for start in range(0, tokens_ref.shape[0], PERIOD):
        rows = pl.ds(start, PERIOD)
        normed, ignored = normalized(tokens_ref[rows, pl.ds(0, D)].astype(f32))
        out_ref[rows, :] = (normed * (1.0 + scale) + shift).astype(bf16)


def norm_in(place, tokens, own, other):
    return pl.pallas_call(
        norm_in_kernel,
        out_shape=shaped(tokens.shape[0], D, dtype=bf16),
        in_specs=[pl.BlockSpec(memory_space=pltpu.SMEM)] + [VMEM_SPEC] * 3,
        out_specs=VMEM_SPEC,
        compiler_params=params(),
        cost_estimate=COST,
        name="norm_in",
    )(place, tokens, own, other)


def project_kernel(place_ref, *refs, parts):
    count = len(parts)
    weight_ref, window_ref = refs[-2], refs[-1]
    q_ref, kv_ref = refs[-4], refs[-3]
    window_parts = refs[count:-4]
    fill(weight_ref, place_ref, refs[:count], parts)
    tokens = q_ref.shape[0]
    for index, part in enumerate(window_parts):
        window_ref[pl.ds(index * tokens, tokens), :] = part[...]
    for start in range(0, 2 * D, 768):
        kv_ref[:, pl.ds(start, 768)] = dot_nn(
            window_ref[...], weight_ref[:, pl.ds(D + start, 768)]
        ).astype(bf16)
    for start in range(0, D, 384):
        q_ref[:, pl.ds(start, 384)] = dot_nn(
            window_parts[0][...], weight_ref[:, pl.ds(start, 384)]
        ).astype(bf16)


def project(place, sources, window_parts):
    tokens = window_parts[0].shape[0]
    keys = tokens * len(window_parts)
    return staged_call(
        project_kernel,
        place,
        sources,
        window_parts,
        [shaped(tokens, D, dtype=bf16), shaped(keys, 2 * D, dtype=bf16)],
        [pltpu.VMEM((D, 3 * D), bf16), pltpu.VMEM((keys, D), bf16)],
        "project",
    )


def head_window(head):
    start = head * HD
    low = start // 128 * 128
    width = 128 if start + HD - low <= 128 else 256
    return low, min(width, D - low), start - low


def head_lanes(rows, width, first):
    lane = lax.broadcasted_iota(jnp.int32, (rows, width), 1)
    return (lane >= first) & (lane < first + HD)


def attend_kernel(place_ref, *refs, parts):
    count = len(parts)
    q_ref, kv_ref, bias_ref, mask_ref, tokens_ref, gate_ref, shift_ref, scale_ref = refs[
        count : count + 8
    ]
    merged_ref, proj_ref, mid_ref, normed_ref, acc_ref, weight_ref = refs[count + 8 :]
    tokens = q_ref.shape[0]
    fill(weight_ref, place_ref, refs[:count], parts)
    acc_ref[...] = jnp.zeros_like(acc_ref)
    for head in range(H):
        low, width, first = head_window(head)
        window = pl.ds(low, width)
        lanes = head_lanes(tokens, width, first)
        query = jnp.where(lanes, q_ref[:, window], jnp.zeros((), bf16))
        scores = dot_nt(query, kv_ref[:, window]) * score_scale + bias_ref[...]
        top = jnp.max(scores, axis=1, keepdims=True)
        weights = jnp.exp(scores - top)
        probs = (weights * (1.0 / jnp.sum(weights, axis=1, keepdims=True))).astype(bf16)
        out = dot_nn(probs, kv_ref[:, pl.ds(D + low, width)])
        acc_ref[:, window] += jnp.where(lanes, out, 0.0)
    for start in range(0, tokens, PERIOD):
        rows = pl.ds(start, PERIOD)
        merged_ref[rows, :] = (acc_ref[rows, :] * mask_ref[...]).astype(bf16)
    proj_ref[...] = dot_nn(merged_ref[...], weight_ref[...])
    for start in range(0, tokens, PERIOD):
        rows = pl.ds(start, PERIOD)
        mid = tokens_ref[rows, pl.ds(0, D)].astype(f32) + gate_ref[...] * proj_ref[rows, :]
        mid_ref[rows, :] = mid
        normed, ignored = normalized(mid)
        normed_ref[rows, :] = (normed * (1.0 + scale_ref[...]) + shift_ref[...]).astype(bf16)


def attend(place, sources, *inputs):
    tokens = inputs[0].shape[0]
    return staged_call(
        attend_kernel,
        place,
        sources,
        inputs,
        [
            shaped(tokens, D, dtype=bf16),
            shaped(tokens, D),
            shaped(tokens, D),
            shaped(tokens, D, dtype=bf16),
        ],
        [pltpu.VMEM((tokens, D), f32), pltpu.VMEM((D, D), bf16)],
        "attend",
    )


def attend_back_kernel(
    q_ref, kv_ref, bias_ref, grad_ref, dq_ref, *refs
):
    tokens = q_ref.shape[0]
    dkv_refs, (dq_acc, dk_acc, dv_acc) = refs[:-3], refs[-3:]
    dq_acc[...] = jnp.zeros_like(dq_acc)
    dk_acc[...] = jnp.zeros_like(dk_acc)
    dv_acc[...] = jnp.zeros_like(dv_acc)
    for head in range(H):
        low, width, first = head_window(head)
        window = pl.ds(low, width)
        lanes = head_lanes(tokens, width, first)
        query = jnp.where(lanes, q_ref[:, window], jnp.zeros((), bf16))
        grad = jnp.where(lanes, grad_ref[:, window], jnp.zeros((), bf16))
        keys = kv_ref[:, window]
        scores = dot_nt(keys, query) * score_scale + bias_ref[...]
        top = jnp.max(scores, axis=0, keepdims=True)
        weights = jnp.exp(scores - top)
        probs = weights * (1.0 / jnp.sum(weights, axis=0, keepdims=True))
        probs_low = probs.astype(bf16)
        grad_probs = dot_nt(kv_ref[:, pl.ds(D + low, width)], grad)
        row_dot = jnp.sum(probs_low.astype(f32) * grad_probs, axis=0, keepdims=True)
        grad_scores = (probs * (grad_probs - row_dot)).astype(bf16)
        dk_acc[:, window] += dot_nn(grad_scores, query)
        dv_acc[:, window] += dot_nn(probs_low, grad)
        dq_acc[:, window] += jnp.where(lanes, dot_tn(grad_scores, keys), 0.0)
    dq_ref[...] = (dq_acc[...] * score_scale).astype(bf16)
    for index, dkv_ref in enumerate(dkv_refs):
        rows = pl.ds(index * tokens, tokens)
        dkv_ref[:, pl.ds(0, D)] = (dk_acc[rows, :] * score_scale).astype(bf16)
        dkv_ref[:, pl.ds(D, D)] = dv_acc[rows, :].astype(bf16)


def attend_back(queries, kv_window, bias_t, grad_heads):
    tokens = queries.shape[0]
    keys = kv_window.shape[0]
    outs = [shaped(tokens, D, dtype=bf16)]
    outs += [shaped(tokens, 2 * D, dtype=bf16)] * (keys // tokens)
    return pl.pallas_call(
        attend_back_kernel,
        out_shape=outs,
        in_specs=[VMEM_SPEC] * 4,
        out_specs=[VMEM_SPEC] * len(outs),
        scratch_shapes=[
            pltpu.VMEM((tokens, D), f32),
            pltpu.VMEM((keys, D), f32),
            pltpu.VMEM((keys, D), f32),
        ],
        compiler_params=params(),
        cost_estimate=COST,
        name="attend_back",
    )(queries, kv_window, bias_t, grad_heads)


def feed_kernel(place_ref, *refs, parts, arrays):
    count = len(parts)
    mid_refs, grad_refs = refs[count : count + arrays], refs[count + arrays : count + 2 * arrays]
    channel_ref, down_ref = refs[count + 2 * arrays : count + 2 * arrays + 2]
    act_ref, pre_ref, grad_own, grad_low, out_own, out_low = refs[-9:-3]
    weight_ref, grad_acc, out_acc = refs[-3:]
    own_rows = grad_own.shape[0]
    step, steps = pl.program_id(0), pl.num_programs(0)
    rows, cols = act_ref.shape
    groups = channel_ref.shape[0]
    tokens = rows // groups

    @pl.when(step == 0)
    def _():
        grad_acc[...] = jnp.zeros_like(grad_acc)
        out_acc[...] = jnp.zeros_like(out_acc)

    fill(weight_ref, place_ref, refs[:count], parts)
    root = 0.7978845608028654
    for group in range(groups):
        span = pl.ds(group * tokens, tokens)
        source, at = (group, 0) if arrays > 1 else (0, group * tokens)
        part = pl.ds(at, tokens)
        channels = jnp.concatenate([channel_ref[group]] * (tokens // PERIOD), axis=0)
        pre = dot_nn(mid_refs[source][part, :], weight_ref[...])
        grad_act = dot_nt(grad_refs[source][part, :], down_ref[...])
        square = pre * pre
        inner = jnp.tanh(root * (pre + 0.044715 * (square * pre)))
        half_sum = 0.5 + 0.5 * inner
        act_ref[span, :] = (pre * half_sum * channels).astype(bf16)
        slope = half_sum + (0.5 * pre) * (1.0 - inner * inner) * (
            root + (3.0 * 0.044715 * root) * square
        )
        pre_ref[span, :] = (grad_act * channels * slope).astype(bf16)
    grad_acc[...] += dot_nt(pre_ref[...], weight_ref[...])
    out_acc[...] += dot_nn(act_ref[...], down_ref[...])

    @pl.when(step == steps - 1)
    def _():
        skip = rows - grad_low.shape[0]
        grad_own[...] = grad_acc[pl.ds(0, own_rows), :]
        out_own[...] = out_acc[pl.ds(0, own_rows), :]
        grad_low[...] = grad_acc[pl.ds(skip, rows - skip), :].astype(bf16)
        out_low[...] = out_acc[pl.ds(skip, rows - skip), :].astype(bf16)


def feed(place, sources, mids, grads, channels, down, chunk, tokens, low_rows):
    arrays, specs, parts = source_inputs(sources)
    rows = sum(mid.shape[0] for mid in mids)
    width = down.shape[0]
    by_chunk = pl.BlockSpec((rows, chunk), lambda i, place: (0, i))
    own, low = (tokens, D), (low_rows, D)
    return pl.pallas_call(
        functools.partial(feed_kernel, parts=parts, arrays=len(mids)),
        out_shape=[
            shaped(rows, width, dtype=bf16),
            shaped(rows, width, dtype=bf16),
            shaped(*own),
            shaped(*low, dtype=bf16),
            shaped(*own),
            shaped(*low, dtype=bf16),
        ],
        grid_spec=pltpu.PrefetchScalarGridSpec(
            num_scalar_prefetch=1,
            grid=(width // chunk,),
            in_specs=specs
            + [whole(value.shape) for value in (*mids, *grads)]
            + [
                pl.BlockSpec(
                    (channels.shape[0], PERIOD, chunk), lambda i, place: (0, 0, i)
                ),
                pl.BlockSpec((chunk, D), lambda i, place: (i, 0)),
            ],
            out_specs=[by_chunk, by_chunk, whole(own), whole(low), whole(own), whole(low)],
            scratch_shapes=[
                pltpu.VMEM((D, chunk), bf16),
                pltpu.VMEM((rows, D), f32),
                pltpu.VMEM((rows, D), f32),
            ],
        ),
        compiler_params=params(),
        cost_estimate=COST,
        name="feed",
    )(place, *arrays, *mids, *grads, channels, down)


def mid_back_kernel(place_ref, *refs, parts):
    count = len(parts)
    own_ref, other_ref, mid_ref, proj_ref, late_ref, scale_ref, gate_ref, mask_ref = refs[
        count : count + 8
    ]
    attn_ref, normed_ref = refs[count + 8 : count + 10]
    grad_mid_ref, own_pack_ref, pack_ref, heads_ref, sums_ref, weight_ref, merged_ref = refs[
        count + 10 :
    ]
    first = place_ref[0] == 0
    half = D // 2
    for index, ref in enumerate((attn_ref, normed_ref)):
        low, high = ref[:, pl.ds(0, half)], ref[:, pl.ds(half, half)]
        own_pack_ref[:, pl.ds(index * half, half)] = jnp.where(first, low, high)
        pack_ref[:, pl.ds(index * half, half)] = jnp.where(first, high, low)
    tokens = own_ref.shape[0]
    fill(weight_ref, place_ref, refs[:count], parts)
    gate_sum = jnp.zeros((PERIOD, D), f32)
    shift_sum = jnp.zeros((PERIOD, D), f32)
    scale_sum = jnp.zeros((PERIOD, D), f32)
    for start in range(0, tokens, PERIOD):
        rows = pl.ds(start, PERIOD)
        normed, inverse = normalized(mid_ref[rows, :])
        grad = own_ref[rows, :] + other_ref[rows, :].astype(f32)
        grad_mid = late_ref[rows, pl.ds(D, D)].astype(f32) + normalized_back(
            grad * (1.0 + scale_ref[...]), normed, inverse
        )
        grad_mid_ref[rows, :] = grad_mid
        grad_attn = (grad_mid * gate_ref[...]).astype(bf16)
        own_pack_ref[rows, pl.ds(D, D)] = grad_attn
        pack_ref[rows, pl.ds(D, D)] = grad_attn
        gate_sum += grad_mid * proj_ref[rows, :]
        shift_sum += grad
        scale_sum += grad * normed
    sums_ref[0] = gate_sum
    sums_ref[1] = shift_sum
    sums_ref[2] = scale_sum
    merged_ref[...] = dot_nt(pack_ref[:, pl.ds(D, D)], weight_ref[...])
    for start in range(0, tokens, PERIOD):
        rows = pl.ds(start, PERIOD)
        heads_ref[rows, :] = (merged_ref[rows, :] * mask_ref[...]).astype(bf16)


def mid_back(place, sources, *inputs):
    tokens = inputs[0].shape[0]
    return staged_call(
        mid_back_kernel,
        place,
        sources,
        inputs,
        [
            shaped(tokens, D),
            shaped(tokens, 2 * D, dtype=bf16),
            shaped(tokens, 2 * D, dtype=bf16),
            shaped(tokens, D, dtype=bf16),
            shaped(3, PERIOD, D),
        ],
        [pltpu.VMEM((D, D), bf16), pltpu.VMEM((tokens, D), f32)],
        "mid_back",
    )


def in_back_kernel(place_ref, *refs, parts):
    count = len(parts)
    dq_ref, dkv_ref, tokens_ref, scale_ref, grad_mid_ref = refs[count : count + 5]
    grad_in_ref, sums_ref, weight_ref, grad_ref = refs[count + 5 :]
    tokens = dq_ref.shape[0]
    fill(weight_ref, place_ref, refs[:count], parts)
    grad_ref[...] = dot_nt(dkv_ref[...], weight_ref[:, pl.ds(D, 2 * D)]) + dot_nt(
        dq_ref[...], weight_ref[:, pl.ds(0, D)]
    )
    shift_sum = jnp.zeros((PERIOD, D), f32)
    scale_sum = jnp.zeros((PERIOD, D), f32)
    for start in range(0, tokens, PERIOD):
        rows = pl.ds(start, PERIOD)
        normed, inverse = normalized(tokens_ref[rows, pl.ds(0, D)].astype(f32))
        grad = grad_ref[rows, :]
        back = normalized_back(grad * (1.0 + scale_ref[...]), normed, inverse)
        grad_in_ref[rows, :] = (grad_mid_ref[rows, :] + back).astype(bf16)
        shift_sum += grad
        scale_sum += grad * normed
    sums_ref[0] = shift_sum
    sums_ref[1] = scale_sum


def in_back(place, sources, *inputs):
    tokens = inputs[0].shape[0]
    return staged_call(
        in_back_kernel,
        place,
        sources,
        inputs,
        [shaped(tokens, D, dtype=bf16), shaped(2, PERIOD, D)],
        [pltpu.VMEM((D, 3 * D), bf16), pltpu.VMEM((tokens, D), f32)],
        "in_back",
    )


def term_kernel(place_ref, *refs, layout, outputs):
    joined = refs[-3 * len(layout) :]
    place_at = {0: place_ref[3], 1: place_ref[4]}
    core = place_ref[2]
    first_out = len(refs) - 3 * len(layout) - 2 * outputs
    for index, (pieces, chunk, plan) in enumerate(layout):
        grads_ref, acts_ref, acc_ref = joined[3 * index : 3 * index + 3]
        for target, ref_at, column, cols, row_to, col_to in pieces:
            value = refs[ref_at][:, pl.ds(column, cols)]
            into = grads_ref if target == 0 else acts_ref
            into[pl.ds(row_to, value.shape[0]), pl.ds(col_to, cols)] = value
        width = acts_ref.shape[1]
        for start in range(0, width, 576):
            span = pl.ds(start, 576)
            acc_ref[:, span] = dot_tn(grads_ref[...], acts_ref[:, span])
        for out_index, (first, count, into_row, axis) in enumerate(plan):
            at = place_at[axis]
            for side_at, side in ((0, 1 - at), (1, at)):
                out_ref = refs[first_out + 2 * out_index + side_at]
                blocks, lanes = out_ref.shape[0], out_ref.shape[2]
                lane_blocks = width // lanes
                for block in range(blocks):
                    lane, rest = divmod(block, blocks // lane_blocks)
                    if axis == 0:
                        line = rest * 4 + side * 2 + core
                    else:
                        line = (rest // 2) * 8 + side * 4 + (rest % 2) * 2 + core
                    start = pl.multiple_of(line * chunk + first, 8)
                    out_ref[block, pl.ds(into_row, count), :] = acc_ref[
                        pl.ds(start, count), pl.ds(lane * lanes, lanes)
                    ].astype(bf16)


def term(place, weights, width):
    arrays, layout, scratch, rows_out = [], [], [], [0, 0]
    for grads, acts in weights:
        pieces, shapes = [], []
        for target, value in ((0, grads), (1, acts)):
            row_to = 0
            for group in value:
                col_to = 0
                for array, column, cols in group:
                    pieces.append((target, len(arrays), column, cols, row_to, col_to))
                    arrays.append(array)
                    col_to += cols
                row_to += group[0][0].shape[0]
            shapes.append((row_to, col_to))
        (depth, columns), (_, rows) = shapes
        chunk = columns // (16 * width // rows)
        first = chunk // 16 * 8
        plan = [(0, first, rows_out[0], 0), (first, chunk - first, rows_out[1], 1)]
        rows_out = [rows_out[0] + first, rows_out[1] + chunk - first]
        layout.append((pieces, chunk, plan))
        scratch += [
            pltpu.VMEM((depth, columns), bf16),
            pltpu.VMEM((depth, rows), bf16),
            pltpu.VMEM((columns, rows), f32),
        ]
    outs = [shaped(4, rows_out[axis], width, dtype=bf16) for axis in (0, 0, 1, 1)]
    return pl.pallas_call(
        functools.partial(term_kernel, layout=layout, outputs=2),
        out_shape=outs,
        in_specs=[pl.BlockSpec(memory_space=pltpu.SMEM)] + [VMEM_SPEC] * len(arrays),
        out_specs=[VMEM_SPEC] * len(outs),
        scratch_shapes=scratch,
        compiler_params=params(),
        cost_estimate=COST,
        name="term",
    )(place, *arrays)


def running_ends(pieces):
    index = jnp.arange(pieces.shape[0], dtype=jnp.int32)
    return jnp.sum(jnp.where(index[None, :] <= index[:, None], pieces[None, :], 0), axis=1)


def crop_of(slots, ends):
    return jnp.sum((slots[..., None] >= ends[:-1]).astype(jnp.int32), axis=-1)


def one_hot(crops, count):
    return (crops[..., None] == jnp.arange(count, dtype=jnp.int32)).astype(f32)


def block_order(size):
    def device(block):
        chip, core = block // 2, block % 2
        return 2 * (chip ^ ((chip >> 1) & 1)) + core if size % 8 == 0 else block

    return [device(block) for block in range(size)]


def local(
    tokens_in,
    condition,
    crop_pieces,
    pad_counts,
    head_mask,
    channel_mask,
    keep_mask,
    qkv_weight,
    out_weight,
    up_weight,
    down_weight,
    ada_weight,
    cotangent,
):
    seq = lax.axis_size("seq")
    rows = lax.axis_size("fsdp")
    tokens = tokens_in.shape[1]
    slots = tokens // seq
    repeats = PERIOD // slots
    crops = crop_pieces.shape[1]
    hidden = up_weight.shape[1]
    hidden_part = hidden // rows
    half = D // rows
    seq_at = lax.axis_index("seq")
    row_at = lax.axis_index("fsdp")
    fast = rows == 2 and seq == 16
    order = block_order(seq)
    core = seq_at % 2
    if seq % 8 == 0:
        chip = seq_at // 2
        block_at = 2 * (chip ^ ((chip >> 1) & 1)) + core
    else:
        block_at = seq_at
    place = jnp.stack(
        [
            row_at,
            seq_at & 3,
            core,
            (seq_at // 2) % 2,
            (seq_at // 4) % 2,
            (seq_at // 4) % 2 * 2 + core,
        ]
    ).astype(jnp.int32)

    def flip(value, bit):
        return lax.ppermute(value, "seq", [(i, i ^ bit) for i in range(seq)])

    def cross(value):
        return lax.ppermute(value, "fsdp", [(0, 1), (1, 0)])

    def shift(value, distance):
        pairs = [
            (order[b], order[b + distance]) for b in range(seq) if 0 <= b + distance < seq
        ]
        return lax.ppermute(value, "seq", pairs)

    swap_rows = jnp.asarray(
        np.kron(np.eye(seq)[np.array(order)], np.eye(slots)), bf16
    )

    def to_slots(value):
        moved = jnp.dot(swap_rows, value, preferred_element_type=f32).astype(bf16)
        moved = lax.all_to_all(moved.reshape(seq, slots, -1), "seq", 0, 0)
        return moved.reshape(tokens, -1)

    def from_slots(value, dtype):
        value = lax.all_to_all(value.reshape(seq, slots, -1), "seq", 0, 0)
        value = value.reshape(tokens, -1)
        return jnp.dot(swap_rows, value, preferred_element_type=f32).astype(dtype)

    def after(value, *earlier):
        return lax.optimization_barrier((value, *earlier))[0]

    def fetch_first(weight, column, cols, bit, *earlier):
        row = after(((seq_at // bit) % 2 * 2 + core) * (half // 4), *earlier)
        return cross(lax.dynamic_slice(weight, (row, column), (half // 4, cols)))

    def gather_rows(value):
        if rows == 2:
            return jnp.stack([value, cross(value)])
        return lax.all_gather(value, "fsdp", axis=0)

    def pick(low_part, high_part):
        return jnp.where(row_at == 0, low_part, high_part)

    def tiled(value):
        return jnp.concatenate([value] * repeats, axis=-2) if repeats > 1 else value

    slot_index = block_at * slots + jnp.arange(slots, dtype=jnp.int32)
    ends = running_ends(crop_pieces[0])
    crop_here = crop_of(slot_index, ends)
    selector = one_hot(crop_here, crops)
    pads = pad_counts[0]

    cond_act = jax.nn.silu(condition[0]).astype(bf16)
    extra = jnp.concatenate(
        [channel_mask[0].astype(bf16), crop_pieces[0].astype(bf16)[:, None]], axis=1
    )
    extra = jnp.pad(extra, ((0, 0), (0, 128 - extra.shape[1])))
    packed = gather_rows(jnp.concatenate([cond_act, extra], axis=1))
    groups = channel_mask.shape[2]
    cond_rows = packed[:, :, :D].reshape(rows * crops, D)
    group_rows = packed[:, :, D : D + groups].astype(f32)
    ends_rows = jax.vmap(running_ends)(packed[:, :, D + groups].astype(jnp.int32))
    selector_rows = jax.vmap(lambda own: one_hot(crop_of(slot_index, own), crops))(ends_rows)

    columns = ada_weight.shape[1]
    quarter = half // 4
    if fast:
        k_first = fetch_first(qkv_weight, D, D, 2, seq_at)
        v_first = fetch_first(qkv_weight, 2 * D, D, 4, k_first)
        k_second = flip(k_first, 2)
        cond_rows = after(cond_rows, k_first)
    mod_rows = jnp.dot(cond_rows, ada_weight, preferred_element_type=f32)
    mod_rows = mod_rows.reshape(rows, crops, columns)
    if rows == 2:
        mod_slots = jnp.einsum("rsc,rcm->rsm", selector_rows, mod_rows, precision=highest)
        if fast:
            mod_slots = after(mod_slots, v_first, k_second)
        arrived = cross(mod_slots[1])
        mod_attn = pick(mod_slots[0], arrived)
        mod_mlp = pick(arrived, mod_slots[0])
        norm_mods = (mod_slots[0], arrived)
    else:
        mine = lax.all_to_all(mod_rows, "fsdp", 0, 0)
        mine = jnp.transpose(mine, (1, 0, 2)).reshape(crops, rows * columns)
        mine = jnp.dot(selector, mine, precision=highest)
        mod_attn, mod_mlp = mine[:, : 3 * D], mine[:, 3 * D :]
        norm_mods = (mod_attn, mod_attn)
    mod_attn, mod_mlp = tiled(mod_attn), tiled(mod_mlp)
    ignored, scale_attn, gate_attn = (mod_attn[:, i * D : (i + 1) * D] for i in range(3))
    shift_mlp, scale_mlp, gate_mlp = (mod_mlp[:, i * D : (i + 1) * D] for i in range(3))

    def block(at):
        return lambda i, place: (0, at)

    if fast:
        chunk = 768

        def spread(first, second):
            return (first, flip(first, 1), second, flip(second, 1))

        other_part = (1 - row_at) * hidden_part
        q_first = fetch_first(qkv_weight, 0, D, 2, arrived)
        out_first = fetch_first(out_weight, 0, D, 4, q_first)
        up_first_piece = fetch_first(up_weight, other_part, hidden_part, 2, out_first)
        v_second, q_second, out_second = flip(v_first, 4), flip(q_first, 2), flip(out_first, 4)
        k_pieces, v_pieces = spread(k_first, k_second), spread(v_first, v_second)
        q_pieces, out_pieces = spread(q_first, q_second), spread(out_first, out_second)
        qkv_sources = [(qkv_weight, (half, 3 * D), block(0), None, 0)]
        for at, column, pieces in ((1, 0, q_pieces), (1, D, k_pieces), (5, 2 * D, v_pieces)):
            qkv_sources += [
                (piece, (quarter, D), block(0), (at, step), column)
                for step, piece in enumerate(pieces)
            ]
        out_sources = [(out_weight, (half, D), block(0), None, 0)]
        out_sources += [
            (piece, (quarter, D), block(0), (5, step), 0)
            for step, piece in enumerate(out_pieces)
        ]
        low_rows = tokens
    else:
        chunk = hidden_part
        qkv_full = lax.all_gather(qkv_weight, "fsdp", axis=0, tiled=True)
        out_full = lax.all_gather(out_weight, "fsdp", axis=0, tiled=True)
        up_part = lax.all_to_all(up_weight, "fsdp", 1, 0, tiled=True)
        qkv_sources = [(qkv_full, (D, 3 * D), block(0), "all", 0)]
        out_sources = [(out_full, (D, D), block(0), "all", 0)]
        up_sources = [(up_part, (D, hidden_part), block(0), "all", 0)]
        low_rows = rows * tokens

    kept = jnp.broadcast_to(keep_mask[0].astype(bf16)[:, None], (tokens, 128))
    tokens_here = to_slots(jnp.concatenate([tokens_in[0], cotangent[0], kept], axis=1))
    if fast:
        tokens_here = after(tokens_here, v_second)
    normed_in = norm_in(place, tokens_here, *norm_mods)

    reach = -(-(PIECE_MAX - 1) // slots)
    paired = reach == 2 and seq % 2 == 0
    if paired:
        below, above = shift(normed_in, 2), shift(normed_in, -2)
        if fast:
            above = after(above, q_second)
        passed = flip(jnp.where(core == 0, above, below), 1)
        near = [normed_in, flip(normed_in, 1), below, above, passed]
        near_at = [
            block_at,
            block_at ^ 1,
            block_at - 2,
            block_at + 2,
            block_at - 1 + 2 * core,
        ]
    else:
        near, near_at = [normed_in], [block_at]
        for distance in range(1, reach + 1):
            near += [shift(normed_in, distance), shift(normed_in, -distance)]
            near_at += [block_at - distance, block_at + distance]
    near_at = after(jnp.stack(near_at), normed_in)
    key_slots = near_at[:, None] * slots + jnp.arange(slots, dtype=jnp.int32)[None, :]
    inside = (near_at >= 0) & (near_at < seq)
    key_crop = jnp.where(inside[:, None], crop_of(key_slots, ends), -1)
    key_crop = jnp.where(
        key_slots[:, None, :] < tokens - pads[None, :, None], key_crop[:, None, :], -1
    ).reshape(-1)
    query_crop = jnp.broadcast_to(crop_here[None, :], (seq, slots)).reshape(tokens)
    bias = jnp.where(query_crop[:, None] == key_crop[None, :], 0.0, masked_score).astype(f32)
    bias_t = jnp.where(key_crop[:, None] == query_crop[None, :], 0.0, masked_score).astype(f32)
    head_slots = tiled(
        jnp.repeat(jnp.dot(selector, head_mask[0].astype(f32), precision=highest), HD, axis=1)
    )

    def by_slot(value):
        return value.reshape(tokens // PERIOD, PERIOD, -1)

    if fast:
        near[-1] = after(near[-1], out_second)
    queries, kv_window = project(place, qkv_sources, near)
    if fast:
        up_second_piece = flip(after(up_first_piece, queries), 2)
    grad_out = by_slot(tokens_here[:, D : 2 * D].astype(f32))
    keep = by_slot(tokens_here[:, 2 * D : 2 * D + 1].astype(f32))
    grad_mlp = grad_out * gate_mlp * keep
    grad_mlp = grad_mlp.reshape(tokens, D).astype(bf16)

    def row_list(value):
        if rows == 2:
            return [value, cross(value)]
        return [lax.all_gather(value, "fsdp", axis=0, tiled=True)]

    grad_mlps = row_list(grad_mlp)
    queries = after(queries, grad_mlp)
    merged, attn_proj, mid_state, normed_mid = attend(
        place,
        out_sources,
        queries,
        kv_window,
        bias,
        head_slots,
        tokens_here,
        gate_attn,
        shift_mlp,
        scale_mlp,
    )

    mids = row_list(normed_mid)
    if fast:
        up_pieces = spread(up_first_piece, after(up_second_piece, merged))
        chunks = hidden_part // chunk
        up_sources = [
            (up_weight, (half, chunk), lambda i, place: (0, place[0] * chunks + i), None, 0)
        ]
        up_sources += [
            (piece, (quarter, chunk), lambda i, place: (0, i), (1, step), 0)
            for step, piece in enumerate(up_pieces)
        ]
        grad_mlps_side = [flip(value, 1) for value in grad_mlps]
        mids_side = [flip(value, 1) for value in mids]
        mids[1] = after(mids[1], grad_mlps_side)
    channels = jnp.einsum("rsc,rcg->rsg", selector_rows, group_rows, precision=highest)
    channels = lax.dynamic_slice_in_dim(
        jnp.repeat(tiled(channels), CHAN_GROUP, axis=2), row_at * hidden_part, hidden_part, 2
    )
    hidden_act, grad_pre, grad_own, grad_low, out_own, out_low = feed(
        place,
        up_sources,
        mids,
        grad_mlps,
        channels,
        down_weight,
        chunk,
        tokens,
        low_rows,
    )

    def own_sum(own, low):
        if rows == 2:
            return own, cross(low)
        low = low.reshape(rows, tokens, D)
        low = lax.psum_scatter(low, "fsdp", scatter_dimension=0, tiled=True)
        return jnp.zeros_like(own), low.reshape(tokens, D)

    grad_own, grad_other = own_sum(grad_own, grad_low)
    out_own, out_other = own_sum(out_own, out_low)
    mlp_out = out_own + out_other.astype(f32)
    kept_out = by_slot(mlp_out) * keep
    block_out = (by_slot(mid_state) + gate_mlp * kept_out).reshape(tokens, D)
    block_out = block_out.astype(bf16)
    gate_mlp_sum = jnp.sum(grad_out * kept_out, axis=0)

    if fast:

        def columns_of(array, column=0, cols=None):
            return [(array, column, array.shape[1] if cols is None else cols)]

        act_side, pre_side = flip(hidden_act, 1), flip(grad_pre, 1)
        down_parts = term(
            place,
            [
                (
                    [columns_of(value) for value in (*grad_mlps, *grad_mlps_side)],
                    [columns_of(value) for value in (hidden_act, act_side)],
                )
            ],
            hidden_part,
        )
        grad_own = after(grad_own, down_parts)
        down_first = (flip(down_parts[0], 2), flip(down_parts[2], 4))

    grad_mid, own_pack, pack, grad_heads, mid_sums = mid_back(
        place,
        out_sources,
        grad_own,
        grad_other,
        mid_state,
        attn_proj,
        tokens_here,
        scale_mlp,
        gate_attn,
        head_slots,
        merged,
        normed_in,
    )
    if fast:

        crossed = cross(pack)
        own_side = flip(own_pack, 1)
        grad_heads = after(grad_heads, pack, own_side, pre_side, mids_side)
    grad_queries, *parts = attend_back(queries, kv_window, bias_t, grad_heads)
    if fast:
        parts[4], down_first = lax.optimization_barrier((parts[4], down_first))
    if paired:
        handed = flip(parts[4], 1)
        near_side = flip(parts[1], 1)
        zero = jnp.zeros((), bf16)
        down_part = parts[2] + jnp.where(core == 1, handed, zero)
        up_side = parts[3] + jnp.where(core == 0, handed, zero)
        from_above, from_below = shift(down_part, -2), shift(up_side, 2)
        arrivals = [near_side, from_above, from_below]
    else:
        arrivals = []
        for distance in range(1, reach + 1):
            arrivals += [
                shift(parts[2 * distance - 1], -distance),
                shift(parts[2 * distance], distance),
            ]
    if fast:
        q_crossed = cross(grad_queries)
        q_side = flip(grad_queries, 1)
        crossed_side = flip(crossed, 1)
        down_first, ignored = lax.optimization_barrier((down_first, (down_part, up_side)))

        def reduced(kept, arrived_part):
            value = (kept.astype(f32) + arrived_part.astype(f32)).astype(bf16)
            return value.reshape(2, value.shape[0] // 2, *value.shape[1:])

        def second_step(values):
            steps = []
            for value, bit in zip(values, (4, 2)):
                at = (seq_at // bit) % 2
                send = lax.dynamic_index_in_dim(value, 1 - at, 1, keepdims=False)
                keep_part = lax.dynamic_index_in_dim(value, at, 1, keepdims=False)
                steps.append((send, keep_part, bit))
            return steps

        def third_step(kept_parts, arrived_parts):
            value = jnp.concatenate(
                [
                    (kept_part.astype(f32) + arrived_part.astype(f32)).astype(bf16)
                    for kept_part, arrived_part in zip(kept_parts, arrived_parts)
                ],
                axis=1,
            )
            at = (seq_at // 8) % 2
            send = lax.dynamic_index_in_dim(value, 1 - at, 0, keepdims=False)
            return send, lax.dynamic_index_in_dim(value, at, 0, keepdims=False)

        down_values = [reduced(down_parts[1], down_first[0]), reduced(down_parts[3], down_first[1])]
        down_steps = second_step(down_values)
        down_second = [flip(send, bit) for send, ignored, bit in down_steps]
        up_parts = term(
            place,
            [
                (
                    [columns_of(value) for value in (grad_pre, pre_side)],
                    [columns_of(value) for value in (*mids, *mids_side)],
                ),
                (
                    [columns_of(value, D, D) for value in (own_pack, crossed, own_side, crossed_side)],
                    [
                        columns_of(value, 0, half)
                        for value in (own_pack, crossed, own_side, crossed_side)
                    ],
                ),
            ],
            half,
        )
        up_first = (flip(up_parts[0], 2), flip(up_parts[2], 4))
        arrivals[0] = after(arrivals[0], up_parts, q_crossed, q_side, out_other)
    grad_kv = parts[0].astype(f32)
    for arrival in arrivals:
        grad_kv = grad_kv + arrival.astype(f32)
    grad_kv = grad_kv.astype(bf16)
    if fast:
        grad_queries, down_second = lax.optimization_barrier((grad_queries, down_second))
    input_grad, in_sums = in_back(
        place, qkv_sources, grad_queries, grad_kv, tokens_here, scale_attn, grad_mid
    )

    if fast:
        kv_crossed = cross(grad_kv)
        down_second = after(down_second, in_sums)
        down_send, down_keep = third_step([step[1] for step in down_steps], down_second)
        down_last = flip(down_send, 8)
        kv_crossed, in_sums, down_last = lax.optimization_barrier(
            (kv_crossed, in_sums, down_last)
        )
        up_first, grad_kv, q_crossed_late, ignored = lax.optimization_barrier(
            (up_first, grad_kv, q_crossed, kv_crossed)
        )

    def by_crop(sums):
        sums = sums.reshape(-1, repeats, slots, D)
        sums = jnp.sum(sums, axis=1) if repeats > 1 else sums[:, 0]
        return jnp.einsum("sc,nsd->cnd", selector, sums, precision=highest).astype(bf16)

    mod_grads = jnp.concatenate([in_sums, mid_sums, gate_mlp_sum[None]], axis=0)
    if not fast:

        def product(acts, grads):
            return lax.dot_general(
                acts, grads, (((0,), (0,)), ((), ())), preferred_element_type=f32
            ).astype(bf16)

        def both(value):
            value = lax.psum_scatter(value, "fsdp", scatter_dimension=0, tiled=True)
            return lax.psum_scatter(value, "seq", scatter_dimension=1, tiled=True).astype(f32)

        grad_qkv = jnp.concatenate([grad_queries, grad_kv], axis=1)
        qkv_grad = both(product(normed_in, grad_qkv))
        out_grad = both(product(merged, own_pack[:, D:]))
        up_cols = lax.all_to_all(product(mids[0], grad_pre), "fsdp", 0, 1, tiled=True)
        up_grad = lax.psum_scatter(up_cols, "seq", scatter_dimension=1, tiled=True).astype(f32)
        down_cols = product(hidden_act, grad_mlps[0])
        down_grad = lax.psum_scatter(
            down_cols, "seq", scatter_dimension=1, tiled=True
        ).astype(f32)
    else:

        kv_side = flip(grad_kv, 1)
        kv_crossed_side, q_crossed_side = flip(kv_crossed, 1), flip(q_crossed_late, 1)

        def joined(first_part, second_part):
            return columns_of(first_part) + columns_of(second_part)

        up_steps = second_step([reduced(up_parts[1], up_first[0]), reduced(up_parts[3], up_first[1])])
        up_second = [flip(send, bit) for send, ignored, bit in up_steps]
        qkv_parts = term(
            place,
            [
                (
                    [
                        joined(grad_queries, grad_kv),
                        joined(q_crossed, kv_crossed),
                        joined(q_side, kv_side),
                        joined(q_crossed_side, kv_crossed_side),
                    ],
                    [
                        columns_of(value, half, half)
                        for value in (own_pack, crossed, own_side, crossed_side)
                    ],
                )
            ],
            half,
        )
        qkv_first = (flip(qkv_parts[0], 2), flip(qkv_parts[2], 4))
        qkv_steps = second_step(
            [reduced(qkv_parts[1], qkv_first[0]), reduced(qkv_parts[3], qkv_first[1])]
        )
        qkv_second = [flip(send, bit) for send, ignored, bit in qkv_steps]
        up_second, block_out, input_grad, mod_grads, ignored = lax.optimization_barrier(
            (up_second, block_out, input_grad, mod_grads, qkv_parts)
        )
        up_send, up_keep = third_step([step[1] for step in up_steps], up_second)
        qkv_send, qkv_keep = third_step([step[1] for step in qkv_steps], qkv_second)
        up_last, ignored = lax.optimization_barrier(
            (flip(up_send, 8), [send for send, ignored, ignored in qkv_steps])
        )
        down_grad = jnp.transpose(down_keep.astype(f32) + down_last.astype(f32))
        qkv_grad = jnp.transpose(qkv_keep.astype(f32) + flip(qkv_send, 8).astype(f32))
        mixed = up_keep.astype(f32) + up_last.astype(f32)
        up_rows, out_rows = hidden // seq, D // seq
        up_low, out_low = up_rows // 16 * 8, out_rows // 16 * 8
        parted = up_low + out_low
        rest = parted + up_rows - up_low
        up_mine = jnp.concatenate([mixed[:up_low], mixed[parted:rest]], axis=0).astype(bf16)
        out_grad = jnp.transpose(jnp.concatenate([mixed[up_low:parted], mixed[rest:]], axis=0))
        pairs = []
        for place_seq in range(seq):
            for place_row in range(2):
                high = (place_seq // 8) % 2
                target_seq = (place_seq & 7) | (place_row * 8)
                pairs.append((place_seq * 2 + place_row, target_seq * 2 + high))
        up_grad = jnp.transpose(lax.ppermute(up_mine, ("seq", "fsdp"), pairs)).astype(f32)
    mod_grads = by_crop(mod_grads).reshape(crops, 6 * D)
    if fast:
        share = columns // 2
        quarters = [mod_grads[:, i * share : (i + 1) * share] for i in range(4)]
        first_core = core == 0
        kept_sum = [jnp.where(first_core, quarters[i], quarters[i + 1]) for i in (0, 2)]
        sent_sum = [jnp.where(first_core, quarters[i + 1], quarters[i]) for i in (0, 2)]
        kept_sum, sent_sum = (jnp.stack(value) for value in (kept_sum, sent_sum))
        mod_grads = (kept_sum.astype(f32) + flip(sent_sum, 1).astype(f32)).astype(bf16)
        for bit, ahead in ((2, [send for send, ignored, ignored in qkv_steps]), (4, qkv_send), (8, ())):
            mod_grads = (mod_grads.astype(f32) + flip(mod_grads, bit).astype(f32)).astype(bf16)
            mod_grads = after(mod_grads, ahead)
        own = pick(mod_grads[0], mod_grads[1])
        other = cross(pick(mod_grads[1], mod_grads[0]))
        own = jnp.concatenate([own, other], axis=0)
        other = flip(own, 1)
        mod_grads = jnp.concatenate(
            [jnp.where(first_core, own, other), jnp.where(first_core, other, own)], axis=1
        )
    else:
        mod_grads = lax.psum(mod_grads, "seq")
        split = jnp.transpose(mod_grads.reshape(crops, rows, columns), (1, 0, 2))
        mod_grads = lax.all_to_all(split, "fsdp", 0, 0).reshape(rows * crops, columns)
    ada_grad = lax.dot_general(
        cond_rows, mod_grads, (((0,), (0,)), ((), ())), preferred_element_type=f32
    )

    both_out = from_slots(jnp.concatenate([block_out, input_grad], axis=1), f32)
    block_out, input_grad = both_out[:, :D].astype(bf16), both_out[:, D:]
    return (
        block_out[None],
        input_grad[None],
        qkv_grad,
        out_grad,
        up_grad,
        down_grad,
        ada_grad,
    )


def solution(mesh):
    in_specs = (
        P("fsdp", "seq", None),
        P("fsdp", None, None),
        P("fsdp", None),
        P("fsdp", None),
        P("fsdp", None, None),
        P("fsdp", None, None),
        P("fsdp", "seq"),
        P("fsdp", None),
        P("fsdp", None),
        P("fsdp", None),
        P("fsdp", None),
        P(None, "fsdp"),
        P("fsdp", "seq", None),
    )
    out_specs = (
        P("fsdp", "seq", None),
        P("fsdp", "seq", None),
        P("fsdp", "seq"),
        P("fsdp", "seq"),
        P("fsdp", "seq"),
        P("fsdp", "seq"),
        P(None, "fsdp"),
    )
    return jax.shard_map(local, mesh=mesh, in_specs=in_specs, out_specs=out_specs, check_vma=False)
```

```python
import functools

import jax
import jax.numpy as jnp
import numpy as np
from jax import lax
from jax.experimental import pallas as pl
from jax.experimental.pallas import tpu as pltpu
from jax.sharding import PartitionSpec as P

D = 1152
H = 16
HD = 72
CHAN_GROUP = 128
PIECE_MAX = 16
PERIOD = 16

bf16 = jnp.bfloat16
f32 = jnp.float32
highest = lax.Precision.HIGHEST
norm_epsilon = 1e-06
masked_score = -1e30
score_scale = HD ** (-0.5)
VMEM_LIMIT = 56 * 1024 * 1024
VMEM_SPEC = pl.BlockSpec(memory_space=pltpu.VMEM)
COST = pl.CostEstimate(flops=1, transcendentals=0, bytes_accessed=1)


def params():
    return pltpu.CompilerParams(vmem_limit_bytes=VMEM_LIMIT)


def dot_nt(a, b):
    return lax.dot_general(a, b, (((1,), (1,)), ((), ())), preferred_element_type=f32)


def dot_nn(a, b):
    return lax.dot_general(a, b, (((1,), (0,)), ((), ())), preferred_element_type=f32)


def dot_tn(a, b):
    return lax.dot_general(a, b, (((0,), (0,)), ((), ())), preferred_element_type=f32)


def source_inputs(sources):
    arrays = [source[0] for source in sources]
    specs = [pl.BlockSpec(source[1], source[2]) for source in sources]
    parts = [(source[3], source[4]) for source in sources]
    return arrays, specs, parts


def fill(target_ref, place_ref, refs, parts):
    half = target_ref.shape[0] // 2
    mine = place_ref[0]
    for ref, (step, column) in zip(refs, parts):
        rows, cols = ref.shape
        if step == "all":
            start = 0
        elif step is None:
            start = pl.multiple_of(mine * half, 16)
        else:
            part = place_ref[step[0]] ^ step[1]
            start = pl.multiple_of((1 - mine) * half + part * rows, 16)
        target_ref[pl.ds(start, rows), pl.ds(column, cols)] = ref[...]


def whole(shape):
    return pl.BlockSpec(shape, lambda i, place: (0,) * len(shape))


def staged_call(kernel, place, sources, inputs, out_shapes, scratch, name):
    arrays, specs, parts = source_inputs(sources)
    return pl.pallas_call(
        functools.partial(kernel, parts=parts),
        out_shape=out_shapes,
        grid_spec=pltpu.PrefetchScalarGridSpec(
            num_scalar_prefetch=1,
            grid=(1,),
            in_specs=specs + [whole(value.shape) for value in inputs],
            out_specs=[whole(out.shape) for out in out_shapes],
            scratch_shapes=scratch,
        ),
        compiler_params=params(),
        cost_estimate=COST,
        name=name,
    )(place, *arrays, *inputs)


def shaped(*shape, dtype=f32):
    return jax.ShapeDtypeStruct(shape, dtype)


def normalized(values):
    centred = values - jnp.mean(values, axis=1, keepdims=True)
    inverse = lax.rsqrt(jnp.mean(centred * centred, axis=1, keepdims=True) + norm_epsilon)
    return centred * inverse, inverse


def normalized_back(grad, normed, inverse):
    mean_grad = jnp.mean(grad, axis=1, keepdims=True)
    mean_dot = jnp.mean(grad * normed, axis=1, keepdims=True)
    return (grad - mean_grad - normed * mean_dot) * inverse


def slot_rows(value):
    repeats = PERIOD // value.shape[0]
    return jnp.concatenate([value] * repeats, axis=0) if repeats > 1 else value


def mod_attn(place_ref, own_ref, other_ref, index):
    columns = pl.ds(index * D, D)
    return slot_rows(jnp.where(place_ref[6] == 0, own_ref[:, columns], other_ref[:, columns]))


def mod_mlp(place_ref, own_ref, other_ref, index):
    return mod_attn(place_ref, other_ref, own_ref, index)


def norm_in_kernel(place_ref, tokens_ref, own_ref, other_ref, out_ref, grad_ref):
    shift = mod_attn(place_ref, own_ref, other_ref, 0)
    scale = 1.0 + mod_attn(place_ref, own_ref, other_ref, 1)
    gate = mod_mlp(place_ref, own_ref, other_ref, 2)
    for start in range(0, tokens_ref.shape[0], PERIOD):
        rows = pl.ds(start, PERIOD)
        normed, ignored = normalized(tokens_ref[rows, pl.ds(0, D)].astype(f32))
        out_ref[rows, :] = (normed * scale + shift).astype(bf16)
        keep = tokens_ref[rows, pl.ds(2 * D, 128)].astype(f32)[:, :1]
        grad = tokens_ref[rows, pl.ds(D, D)].astype(f32)
        grad_ref[rows, :] = (grad * gate * keep).astype(bf16)


def norm_in(place, tokens, own, other):
    return pl.pallas_call(
        norm_in_kernel,
        out_shape=[shaped(tokens.shape[0], D, dtype=bf16)] * 2,
        in_specs=[pl.BlockSpec(memory_space=pltpu.SMEM)] + [VMEM_SPEC] * 3,
        out_specs=[VMEM_SPEC] * 2,
        compiler_params=params(),
        cost_estimate=COST,
        name="norm_in",
    )(place, tokens, own, other)


def project_kernel(place_ref, *refs, parts):
    count = len(parts)
    weight_ref, window_ref = refs[-2], refs[-1]
    q_ref, kv_ref = refs[-4], refs[-3]
    window_parts = refs[count:-4]
    fill(weight_ref, place_ref, refs[:count], parts)
    tokens = q_ref.shape[0]
    for index, part in enumerate(window_parts):
        window_ref[pl.ds(index * tokens, tokens), :] = part[...]
    for start in range(0, 2 * D, 768):
        kv_ref[:, pl.ds(start, 768)] = dot_nn(
            window_ref[...], weight_ref[:, pl.ds(D + start, 768)]
        ).astype(bf16)
    for start in range(0, D, 384):
        q_ref[:, pl.ds(start, 384)] = dot_nn(
            window_parts[0][...], weight_ref[:, pl.ds(start, 384)]
        ).astype(bf16)


def project(place, sources, window_parts):
    tokens = window_parts[0].shape[0]
    keys = tokens * len(window_parts)
    return staged_call(
        project_kernel,
        place,
        sources,
        window_parts,
        [shaped(tokens, D, dtype=bf16), shaped(keys, 2 * D, dtype=bf16)],
        [pltpu.VMEM((D, 3 * D), bf16), pltpu.VMEM((keys, D), bf16)],
        "project",
    )


def head_window(head):
    start = head * HD
    low = start // 128 * 128
    width = 128 if start + HD - low <= 128 else 256
    return low, min(width, D - low), start - low


def head_lanes(rows, width, first):
    lane = lax.broadcasted_iota(jnp.int32, (rows, width), 1)
    return (lane >= first) & (lane < first + HD)


def attend_kernel(place_ref, *refs, parts):
    count = len(parts)
    q_ref, kv_ref, bias_ref, mask_ref, tokens_ref, own_ref, other_ref = refs[count : count + 7]
    merged_ref, proj_ref, mid_ref, normed_ref, acc_ref, weight_ref = refs[count + 7 :]
    gate = mod_attn(place_ref, own_ref, other_ref, 2)
    shift = mod_mlp(place_ref, own_ref, other_ref, 0)
    scale = 1.0 + mod_mlp(place_ref, own_ref, other_ref, 1)
    tokens = q_ref.shape[0]
    fill(weight_ref, place_ref, refs[:count], parts)
    acc_ref[...] = jnp.zeros_like(acc_ref)
    for head in range(H):
        low, width, first = head_window(head)
        window = pl.ds(low, width)
        lanes = head_lanes(tokens, width, first)
        query = jnp.where(lanes, q_ref[:, window], jnp.zeros((), bf16))
        scores = dot_nt(query, kv_ref[:, window]) * score_scale + bias_ref[...]
        top = jnp.max(scores, axis=1, keepdims=True)
        weights = jnp.exp(scores - top)
        probs = (weights * (1.0 / jnp.sum(weights, axis=1, keepdims=True))).astype(bf16)
        out = dot_nn(probs, kv_ref[:, pl.ds(D + low, width)])
        acc_ref[:, window] += jnp.where(lanes, out, 0.0)
    for start in range(0, tokens, PERIOD):
        rows = pl.ds(start, PERIOD)
        merged_ref[rows, :] = (acc_ref[rows, :] * mask_ref[...]).astype(bf16)
    proj_ref[...] = dot_nn(merged_ref[...], weight_ref[...])
    for start in range(0, tokens, PERIOD):
        rows = pl.ds(start, PERIOD)
        mid = tokens_ref[rows, pl.ds(0, D)].astype(f32) + gate * proj_ref[rows, :]
        mid_ref[rows, :] = mid
        normed, ignored = normalized(mid)
        normed_ref[rows, :] = (normed * scale + shift).astype(bf16)


def attend(place, sources, *inputs):
    tokens = inputs[0].shape[0]
    return staged_call(
        attend_kernel,
        place,
        sources,
        inputs,
        [
            shaped(tokens, D, dtype=bf16),
            shaped(tokens, D),
            shaped(tokens, D),
            shaped(tokens, D, dtype=bf16),
        ],
        [pltpu.VMEM((tokens, D), f32), pltpu.VMEM((D, D), bf16)],
        "attend",
    )


def attend_back_kernel(
    q_ref, kv_ref, bias_ref, grad_ref, dq_ref, *refs
):
    tokens = q_ref.shape[0]
    dkv_refs, (dq_acc, dk_acc, dv_acc) = refs[:-3], refs[-3:]
    dq_acc[...] = jnp.zeros_like(dq_acc)
    dk_acc[...] = jnp.zeros_like(dk_acc)
    dv_acc[...] = jnp.zeros_like(dv_acc)
    for head in range(H):
        low, width, first = head_window(head)
        window = pl.ds(low, width)
        lanes = head_lanes(tokens, width, first)
        query = jnp.where(lanes, q_ref[:, window], jnp.zeros((), bf16))
        grad = jnp.where(lanes, grad_ref[:, window], jnp.zeros((), bf16))
        keys = kv_ref[:, window]
        scores = dot_nt(keys, query) * score_scale + bias_ref[...]
        top = jnp.max(scores, axis=0, keepdims=True)
        weights = jnp.exp(scores - top)
        probs = weights * (1.0 / jnp.sum(weights, axis=0, keepdims=True))
        probs_low = probs.astype(bf16)
        grad_probs = dot_nt(kv_ref[:, pl.ds(D + low, width)], grad)
        row_dot = jnp.sum(probs_low.astype(f32) * grad_probs, axis=0, keepdims=True)
        grad_scores = (probs * (grad_probs - row_dot)).astype(bf16)
        dk_acc[:, window] += dot_nn(grad_scores, query)
        dv_acc[:, window] += dot_nn(probs_low, grad)
        dq_acc[:, window] += jnp.where(lanes, dot_tn(grad_scores, keys), 0.0)
    dq_ref[...] = (dq_acc[...] * score_scale).astype(bf16)
    for index, dkv_ref in enumerate(dkv_refs):
        rows = pl.ds(index * tokens, tokens)
        dkv_ref[:, pl.ds(0, D)] = (dk_acc[rows, :] * score_scale).astype(bf16)
        dkv_ref[:, pl.ds(D, D)] = dv_acc[rows, :].astype(bf16)


def attend_back(queries, kv_window, bias_t, grad_heads):
    tokens = queries.shape[0]
    keys = kv_window.shape[0]
    outs = [shaped(tokens, D, dtype=bf16)]
    outs += [shaped(tokens, 2 * D, dtype=bf16)] * (keys // tokens)
    return pl.pallas_call(
        attend_back_kernel,
        out_shape=outs,
        in_specs=[VMEM_SPEC] * 4,
        out_specs=[VMEM_SPEC] * len(outs),
        scratch_shapes=[
            pltpu.VMEM((tokens, D), f32),
            pltpu.VMEM((keys, D), f32),
            pltpu.VMEM((keys, D), f32),
        ],
        compiler_params=params(),
        cost_estimate=COST,
        name="attend_back",
    )(queries, kv_window, bias_t, grad_heads)


def feed_kernel(place_ref, *refs, parts, arrays):
    count = len(parts)
    mid_refs, grad_refs = refs[count : count + arrays], refs[count + arrays : count + 2 * arrays]
    channel_ref, down_ref = refs[count + 2 * arrays : count + 2 * arrays + 2]
    act_ref, pre_ref, grad_own, out_own, low_ref = refs[-8:-3]
    weight_ref, grad_acc, out_acc = refs[-3:]
    own_rows = grad_own.shape[0]
    step, steps = pl.program_id(0), pl.num_programs(0)
    rows, cols = act_ref.shape
    groups = channel_ref.shape[0]
    tokens = rows // groups

    @pl.when(step == 0)
    def _():
        grad_acc[...] = jnp.zeros_like(grad_acc)
        out_acc[...] = jnp.zeros_like(out_acc)

    fill(weight_ref, place_ref, refs[:count], parts)
    root = 0.7978845608028654
    for group in range(groups):
        span = pl.ds(group * tokens, tokens)
        source, at = (group, 0) if arrays > 1 else (0, group * tokens)
        part = pl.ds(at, tokens)
        channels = jnp.concatenate([channel_ref[group]] * (tokens // PERIOD), axis=0)
        pre = dot_nn(mid_refs[source][part, :], weight_ref[...])
        grad_act = dot_nt(grad_refs[source][part, :], down_ref[...])
        square = pre * pre
        inner = jnp.tanh(root * (pre + 0.044715 * (square * pre)))
        half_sum = 0.5 + 0.5 * inner
        act_ref[span, :] = (pre * half_sum * channels).astype(bf16)
        slope = half_sum + (0.5 * pre) * (1.0 - inner * inner) * (
            root + (3.0 * 0.044715 * root) * square
        )
        pre_ref[span, :] = (grad_act * channels * slope).astype(bf16)
    grad_acc[...] += dot_nt(pre_ref[...], weight_ref[...])
    out_acc[...] += dot_nn(act_ref[...], down_ref[...])

    @pl.when(step == steps - 1)
    def _():
        skip = rows - low_ref.shape[0]
        grad_own[...] = grad_acc[pl.ds(0, own_rows), :]
        out_own[...] = out_acc[pl.ds(0, own_rows), :]
        low_ref[:, pl.ds(0, D)] = grad_acc[pl.ds(skip, rows - skip), :].astype(bf16)
        low_ref[:, pl.ds(D, D)] = out_acc[pl.ds(skip, rows - skip), :].astype(bf16)


def feed(place, sources, mids, grads, channels, down, chunk, tokens, low_rows):
    arrays, specs, parts = source_inputs(sources)
    rows = sum(mid.shape[0] for mid in mids)
    width = down.shape[0]
    by_chunk = pl.BlockSpec((rows, chunk), lambda i, place: (0, i))
    own, low = (tokens, D), (low_rows, 2 * D)
    return pl.pallas_call(
        functools.partial(feed_kernel, parts=parts, arrays=len(mids)),
        out_shape=[
            shaped(rows, width, dtype=bf16),
            shaped(rows, width, dtype=bf16),
            shaped(*own),
            shaped(*own),
            shaped(*low, dtype=bf16),
        ],
        grid_spec=pltpu.PrefetchScalarGridSpec(
            num_scalar_prefetch=1,
            grid=(width // chunk,),
            in_specs=specs
            + [whole(value.shape) for value in (*mids, *grads)]
            + [
                pl.BlockSpec(
                    (channels.shape[0], PERIOD, chunk), lambda i, place: (0, 0, i)
                ),
                pl.BlockSpec((chunk, D), lambda i, place: (i, 0)),
            ],
            out_specs=[by_chunk, by_chunk, whole(own), whole(own), whole(low)],
            scratch_shapes=[
                pltpu.VMEM((D, chunk), bf16),
                pltpu.VMEM((rows, D), f32),
                pltpu.VMEM((rows, D), f32),
            ],
        ),
        compiler_params=params(),
        cost_estimate=COST,
        name="feed",
    )(place, *arrays, *mids, *grads, channels, down)


def mid_back_kernel(place_ref, *refs, parts):
    count = len(parts)
    own_ref, out_ref, other_ref, mid_ref, proj_ref, late_ref = refs[count : count + 6]
    mod_own, mod_other, mask_ref, attn_ref, normed_ref = refs[count + 6 : count + 11]
    grad_mid_ref, own_pack_ref, pack_ref, heads_ref, block_ref, sums_ref = refs[
        count + 11 : count + 17
    ]
    weight_ref, merged_ref = refs[count + 17 :]
    scale = 1.0 + mod_mlp(place_ref, mod_own, mod_other, 1)
    gate = mod_attn(place_ref, mod_own, mod_other, 2)
    out_gate = mod_mlp(place_ref, mod_own, mod_other, 2)
    first = place_ref[0] == 0
    half = D // 2
    for index, ref in enumerate((attn_ref, normed_ref)):
        low, high = ref[:, pl.ds(0, half)], ref[:, pl.ds(half, half)]
        own_pack_ref[:, pl.ds(index * half, half)] = jnp.where(first, low, high)
        pack_ref[:, pl.ds(index * half, half)] = jnp.where(first, high, low)
    tokens = own_ref.shape[0]
    fill(weight_ref, place_ref, refs[:count], parts)
    sums = [jnp.zeros((PERIOD, D), f32) for ignored in range(4)]
    for start in range(0, tokens, PERIOD):
        rows = pl.ds(start, PERIOD)
        normed, inverse = normalized(mid_ref[rows, :])
        grad = own_ref[rows, :] + other_ref[rows, pl.ds(0, D)].astype(f32)
        grad_out = late_ref[rows, pl.ds(D, D)].astype(f32)
        grad_mid = grad_out + normalized_back(grad * scale, normed, inverse)
        grad_mid_ref[rows, :] = grad_mid
        grad_attn = (grad_mid * gate).astype(bf16)
        own_pack_ref[rows, pl.ds(D, D)] = grad_attn
        pack_ref[rows, pl.ds(D, D)] = grad_attn
        out = out_ref[rows, :] + other_ref[rows, pl.ds(D, D)].astype(f32)
        out = out * late_ref[rows, pl.ds(2 * D, 128)].astype(f32)[:, :1]
        block_ref[rows, :] = (mid_ref[rows, :] + out_gate * out).astype(bf16)
        for index, value in enumerate(
            (grad_mid * proj_ref[rows, :], grad, grad * normed, grad_out * out)
        ):
            sums[index] += value
    for index in range(4):
        sums_ref[index] = sums[index]
    merged_ref[...] = dot_nt(pack_ref[:, pl.ds(D, D)], weight_ref[...])
    for start in range(0, tokens, PERIOD):
        rows = pl.ds(start, PERIOD)
        heads_ref[rows, :] = (merged_ref[rows, :] * mask_ref[...]).astype(bf16)


def mid_back(place, sources, *inputs):
    tokens = inputs[0].shape[0]
    return staged_call(
        mid_back_kernel,
        place,
        sources,
        inputs,
        [
            shaped(tokens, D),
            shaped(tokens, 2 * D, dtype=bf16),
            shaped(tokens, 2 * D, dtype=bf16),
            shaped(tokens, D, dtype=bf16),
            shaped(tokens, D, dtype=bf16),
            shaped(4, PERIOD, D),
        ],
        [pltpu.VMEM((D, D), bf16), pltpu.VMEM((tokens, D), f32)],
        "mid_back",
    )


def in_back_kernel(place_ref, *refs, parts):
    count = len(parts)
    dq_ref, dkv_ref, tokens_ref, mod_own, mod_other = refs[count : count + 5]
    grad_mid_ref, block_ref = refs[count + 5 : count + 7]
    both_ref, sums_ref, weight_ref, grad_ref = refs[count + 7 :]
    tokens = dq_ref.shape[0]
    fill(weight_ref, place_ref, refs[:count], parts)
    grad_ref[...] = dot_nt(dkv_ref[...], weight_ref[:, pl.ds(D, 2 * D)]) + dot_nt(
        dq_ref[...], weight_ref[:, pl.ds(0, D)]
    )
    scale = 1.0 + mod_attn(place_ref, mod_own, mod_other, 1)
    shift_sum = jnp.zeros((PERIOD, D), f32)
    scale_sum = jnp.zeros((PERIOD, D), f32)
    both_ref[:, pl.ds(0, D)] = block_ref[...]
    for start in range(0, tokens, PERIOD):
        rows = pl.ds(start, PERIOD)
        normed, inverse = normalized(tokens_ref[rows, pl.ds(0, D)].astype(f32))
        grad = grad_ref[rows, :]
        back = normalized_back(grad * scale, normed, inverse)
        both_ref[rows, pl.ds(D, D)] = (grad_mid_ref[rows, :] + back).astype(bf16)
        shift_sum += grad
        scale_sum += grad * normed
    sums_ref[0] = shift_sum
    sums_ref[1] = scale_sum


def in_back(place, sources, *inputs):
    tokens = inputs[0].shape[0]
    return staged_call(
        in_back_kernel,
        place,
        sources,
        inputs,
        [shaped(tokens, 2 * D, dtype=bf16), shaped(2, PERIOD, D)],
        [pltpu.VMEM((D, 3 * D), bf16), pltpu.VMEM((tokens, D), f32)],
        "in_back",
    )


def term_kernel(place_ref, *refs, layout, outputs):
    joined = refs[-3 * len(layout) :]
    place_at = {0: place_ref[3], 1: place_ref[4]}
    core = place_ref[2]
    first_out = len(refs) - 3 * len(layout) - 2 * outputs
    for index, (pieces, chunk, plan) in enumerate(layout):
        grads_ref, acts_ref, acc_ref = joined[3 * index : 3 * index + 3]
        for target, ref_at, column, cols, row_to, col_to in pieces:
            value = refs[ref_at][:, pl.ds(column, cols)]
            into = grads_ref if target == 0 else acts_ref
            into[pl.ds(row_to, value.shape[0]), pl.ds(col_to, cols)] = value
        width = acts_ref.shape[1]
        for start in range(0, width, 576):
            span = pl.ds(start, 576)
            acc_ref[:, span] = dot_tn(grads_ref[...], acts_ref[:, span])
        for out_index, (first, count, into_row, axis) in enumerate(plan):
            at = place_at[axis]
            for side_at, side in ((0, 1 - at), (1, at)):
                out_ref = refs[first_out + 2 * out_index + side_at]
                blocks, lanes = out_ref.shape[0], out_ref.shape[2]
                lane_blocks = width // lanes
                for block in range(blocks):
                    lane, rest = divmod(block, blocks // lane_blocks)
                    if axis == 0:
                        line = rest * 4 + side * 2 + core
                    else:
                        line = (rest // 2) * 8 + side * 4 + (rest % 2) * 2 + core
                    start = pl.multiple_of(line * chunk + first, 8)
                    out_ref[block, pl.ds(into_row, count), :] = acc_ref[
                        pl.ds(start, count), pl.ds(lane * lanes, lanes)
                    ].astype(bf16)


def term(place, weights, width):
    arrays, layout, scratch, rows_out = [], [], [], [0, 0]
    for grads, acts in weights:
        pieces, shapes = [], []
        for target, value in ((0, grads), (1, acts)):
            row_to = 0
            for group in value:
                col_to = 0
                for array, column, cols in group:
                    pieces.append((target, len(arrays), column, cols, row_to, col_to))
                    arrays.append(array)
                    col_to += cols
                row_to += group[0][0].shape[0]
            shapes.append((row_to, col_to))
        (depth, columns), (_, rows) = shapes
        chunk = columns // (16 * width // rows)
        first = chunk // 16 * 8
        plan = [(0, first, rows_out[0], 0), (first, chunk - first, rows_out[1], 1)]
        rows_out = [rows_out[0] + first, rows_out[1] + chunk - first]
        layout.append((pieces, chunk, plan))
        scratch += [
            pltpu.VMEM((depth, columns), bf16),
            pltpu.VMEM((depth, rows), bf16),
            pltpu.VMEM((columns, rows), f32),
        ]
    outs = [shaped(4, rows_out[axis], width, dtype=bf16) for axis in (0, 0, 1, 1)]
    return pl.pallas_call(
        functools.partial(term_kernel, layout=layout, outputs=2),
        out_shape=outs,
        in_specs=[pl.BlockSpec(memory_space=pltpu.SMEM)] + [VMEM_SPEC] * len(arrays),
        out_specs=[VMEM_SPEC] * len(outs),
        scratch_shapes=scratch,
        compiler_params=params(),
        cost_estimate=COST,
        name="term",
    )(place, *arrays)


def outer_kernel(left_ref, right_ref, out_ref):
    out_ref[...] = dot_tn(left_ref[...], right_ref[...])


def outer(left, right):
    depth, rows = left.shape
    columns = right.shape[1]
    return pl.pallas_call(
        outer_kernel,
        out_shape=shaped(rows, columns),
        grid=(rows // 128,),
        in_specs=[
            pl.BlockSpec((depth, 128), lambda i: (0, i)),
            pl.BlockSpec((depth, columns), lambda i: (0, 0)),
        ],
        out_specs=pl.BlockSpec((128, columns), lambda i: (i, 0)),
        compiler_params=params(),
        cost_estimate=COST,
        name="outer",
    )(left, right)


def running_ends(pieces):
    index = jnp.arange(pieces.shape[0], dtype=jnp.int32)
    return jnp.sum(jnp.where(index[None, :] <= index[:, None], pieces[None, :], 0), axis=1)


def crop_of(slots, ends):
    return jnp.sum((slots[..., None] >= ends[:-1]).astype(jnp.int32), axis=-1)


def one_hot(crops, count):
    return (crops[..., None] == jnp.arange(count, dtype=jnp.int32)).astype(f32)


def block_order(size):
    def device(block):
        chip, core = block // 2, block % 2
        return 2 * (chip ^ ((chip >> 1) & 1)) + core if size % 8 == 0 else block

    return [device(block) for block in range(size)]


def local(
    tokens_in,
    condition,
    crop_pieces,
    pad_counts,
    head_mask,
    channel_mask,
    keep_mask,
    qkv_weight,
    out_weight,
    up_weight,
    down_weight,
    ada_weight,
    cotangent,
):
    seq = lax.axis_size("seq")
    rows = lax.axis_size("fsdp")
    tokens = tokens_in.shape[1]
    slots = tokens // seq
    repeats = PERIOD // slots
    crops = crop_pieces.shape[1]
    hidden = up_weight.shape[1]
    hidden_part = hidden // rows
    half = D // rows
    seq_at = lax.axis_index("seq")
    row_at = lax.axis_index("fsdp")
    fast = rows == 2 and seq == 16
    order = block_order(seq)
    core = seq_at % 2
    if seq % 8 == 0:
        chip = seq_at // 2
        block_at = 2 * (chip ^ ((chip >> 1) & 1)) + core
    else:
        block_at = seq_at
    place = jnp.stack(
        [
            row_at,
            seq_at & 3,
            core,
            (seq_at // 2) % 2,
            (seq_at // 4) % 2,
            (seq_at // 4) % 2 * 2 + core,
            row_at if fast else jnp.zeros_like(row_at),
            (seq_at // 8) % 2,
        ]
    ).astype(jnp.int32)

    def flip(value, bit):
        return lax.ppermute(value, "seq", [(i, i ^ bit) for i in range(seq)])

    def cross(value):
        return lax.ppermute(value, "fsdp", [(0, 1), (1, 0)])

    def shift(value, distance):
        pairs = [
            (order[b], order[b + distance]) for b in range(seq) if 0 <= b + distance < seq
        ]
        return lax.ppermute(value, "seq", pairs)

    swap_rows = jnp.asarray(
        np.kron(np.eye(seq)[np.array(order)], np.eye(slots)), bf16
    )

    def to_slots(value):
        moved = jnp.dot(swap_rows, value, preferred_element_type=f32).astype(bf16)
        moved = lax.all_to_all(moved.reshape(seq, slots, -1), "seq", 0, 0)
        return moved.reshape(tokens, -1)

    def from_slots(value, dtype, *earlier):
        value = lax.all_to_all(value.reshape(seq, slots, -1), "seq", 0, 0)
        value = after(value, *earlier) if earlier else value
        value = value.reshape(tokens, -1)
        return jnp.dot(swap_rows, value, preferred_element_type=f32).astype(dtype)

    def after(value, *earlier):
        return lax.optimization_barrier((value, *earlier))[0]

    def fetch_first(slices, bit, *earlier):
        count = 2 if bit is None else 4
        part = core if bit is None else (seq_at // bit) % 2 * 2 + core
        row = after(part * (half // count), *earlier)
        parts = [
            lax.dynamic_slice(weight, (row, column), (half // count, cols))
            for weight, column, cols in slices
        ]
        return cross(jnp.concatenate(parts, axis=1) if len(parts) > 1 else parts[0])

    def gather_rows(value):
        if rows == 2:
            return jnp.stack([value, cross(value)])
        return lax.all_gather(value, "fsdp", axis=0)

    def pick(low_part, high_part):
        return jnp.where(row_at == 0, low_part, high_part)

    def tiled(value):
        return jnp.concatenate([value] * repeats, axis=-2) if repeats > 1 else value

    slot_index = block_at * slots + jnp.arange(slots, dtype=jnp.int32)
    ends = running_ends(crop_pieces[0])
    crop_here = crop_of(slot_index, ends)
    selector = one_hot(crop_here, crops)
    pads = pad_counts[0]

    cond_act = jax.nn.silu(condition[0]).astype(bf16)
    extra = jnp.concatenate(
        [channel_mask[0].astype(bf16), crop_pieces[0].astype(bf16)[:, None]], axis=1
    )
    extra = jnp.pad(extra, ((0, 0), (0, 128 - extra.shape[1])))
    packed = gather_rows(jnp.concatenate([cond_act, extra], axis=1))
    groups = channel_mask.shape[2]
    cond_rows = packed[:, :, :D].reshape(rows * crops, D)
    group_rows = packed[:, :, D : D + groups].astype(f32)
    ends_rows = jax.vmap(running_ends)(packed[:, :, D + groups].astype(jnp.int32))
    selector_rows = jax.vmap(lambda own: one_hot(crop_of(slot_index, own), crops))(ends_rows)

    columns = ada_weight.shape[1]
    quarter = half // 4
    if fast:
        k_first = fetch_first([(qkv_weight, D, D), (out_weight, 0, D)], 2, seq_at)
        k_second = flip(k_first, 2)
    mod_rows = jnp.dot(cond_rows, ada_weight, preferred_element_type=f32)
    mod_rows = mod_rows.reshape(rows, crops, columns)
    if rows == 2:
        mod_slots = jnp.einsum("rsc,rcm->rsm", selector_rows, mod_rows, precision=highest)
        if fast:
            mod_slots = after(mod_slots, k_first)
        arrived = cross(mod_slots[1])
        mods = (mod_slots[0], arrived)
    else:
        mine = lax.all_to_all(mod_rows, "fsdp", 0, 0)
        mine = jnp.transpose(mine, (1, 0, 2)).reshape(crops, rows * columns)
        mine = jnp.dot(selector, mine, precision=highest)
        mods = (mine[:, : 3 * D], mine[:, 3 * D :])

    kept = jnp.broadcast_to(keep_mask[0].astype(bf16)[:, None], (tokens, 128))
    tokens_here = to_slots(jnp.concatenate([tokens_in[0], cotangent[0], kept], axis=1))
    def block(at):
        return lambda i, place: (0, at)

    if fast:
        chunk = 768

        def spread(first, second):
            return (first, flip(first, 1), second, flip(second, 1))

        other_part = (1 - row_at) * hidden_part
        v_first = fetch_first([(qkv_weight, 2 * D, D)], 4, mod_slots)
        q_first = fetch_first([(qkv_weight, 0, D)], None, arrived)
        tokens_here = after(tokens_here, k_second)
        normed_in, grad_mlp = norm_in(place, tokens_here, *mods)
        up_first_piece = fetch_first(
            [(up_weight, other_part, hidden_part)], 2, q_first, normed_in
        )
        v_second = flip(v_first, 4)
        k_pieces, v_pieces = spread(k_first, k_second), spread(v_first, v_second)
        q_pieces = (q_first, flip(q_first, 1))
        qkv_sources = [(qkv_weight, (half, 3 * D), block(0), None, 0)]
        for at, column, pieces in ((2, 0, q_pieces), (1, D, k_pieces), (5, 2 * D, v_pieces)):
            qkv_sources += [
                (piece, (piece.shape[0], D), block(0), (at, step), column)
                for step, piece in enumerate(pieces)
            ]
        out_sources = [(out_weight, (half, D), block(0), None, 0)]
        out_sources += [
            (piece, (quarter, D), block(1), (1, step), 0)
            for step, piece in enumerate(k_pieces)
        ]
        low_rows = tokens
    else:
        chunk = hidden_part
        qkv_full = lax.all_gather(qkv_weight, "fsdp", axis=0, tiled=True)
        out_full = lax.all_gather(out_weight, "fsdp", axis=0, tiled=True)
        up_part = lax.all_to_all(up_weight, "fsdp", 1, 0, tiled=True)
        qkv_sources = [(qkv_full, (D, 3 * D), block(0), "all", 0)]
        out_sources = [(out_full, (D, D), block(0), "all", 0)]
        up_sources = [(up_part, (D, hidden_part), block(0), "all", 0)]
        low_rows = rows * tokens

    if not fast:
        normed_in, grad_mlp = norm_in(place, tokens_here, *mods)

    reach = -(-(PIECE_MAX - 1) // slots)
    paired = reach == 2 and seq % 2 == 0
    if paired:
        below, above = shift(normed_in, 2), shift(normed_in, -2)
        if fast:
            above = after(above, v_second, q_first)
        passed = flip(jnp.where(core == 0, above, below), 1)
        near = [normed_in, flip(normed_in, 1), below, above, passed]
        near_at = [
            block_at,
            block_at ^ 1,
            block_at - 2,
            block_at + 2,
            block_at - 1 + 2 * core,
        ]
    else:
        near, near_at = [normed_in], [block_at]
        for distance in range(1, reach + 1):
            near += [shift(normed_in, distance), shift(normed_in, -distance)]
            near_at += [block_at - distance, block_at + distance]
    near_at = after(jnp.stack(near_at), normed_in)
    key_slots = near_at[:, None] * slots + jnp.arange(slots, dtype=jnp.int32)[None, :]
    inside = (near_at >= 0) & (near_at < seq)
    key_crop = jnp.where(inside[:, None], crop_of(key_slots, ends), -1)
    key_crop = jnp.where(
        key_slots[:, None, :] < tokens - pads[None, :, None], key_crop[:, None, :], -1
    ).reshape(-1)
    query_crop = jnp.broadcast_to(crop_here[None, :], (seq, slots)).reshape(tokens)
    bias = jnp.where(query_crop[:, None] == key_crop[None, :], 0.0, masked_score).astype(f32)
    bias_t = jnp.where(key_crop[:, None] == query_crop[None, :], 0.0, masked_score).astype(f32)
    head_slots = tiled(
        jnp.repeat(jnp.dot(selector, head_mask[0].astype(f32), precision=highest), HD, axis=1)
    )

    queries, kv_window = project(place, qkv_sources, near)
    if fast:
        up_second_piece = flip(after(up_first_piece, queries), 2)

    def row_list(value):
        if rows == 2:
            return [value, cross(value)]
        return [lax.all_gather(value, "fsdp", axis=0, tiled=True)]

    grad_mlps = row_list(grad_mlp)
    merged, attn_proj, mid_state, normed_mid = attend(
        place,
        out_sources,
        queries,
        kv_window,
        bias,
        head_slots,
        tokens_here,
        *mods,
    )

    mids = row_list(normed_mid)
    if fast:
        up_pieces = spread(up_first_piece, after(up_second_piece, mids[1]))
        chunks = hidden_part // chunk
        up_sources = [
            (up_weight, (half, chunk), lambda i, place: (0, place[0] * chunks + i), None, 0)
        ]
        up_sources += [
            (piece, (quarter, chunk), lambda i, place: (0, i), (1, step), 0)
            for step, piece in enumerate(up_pieces)
        ]
        grad_mlps_side = [flip(value, 1) for value in grad_mlps]
        mids_side = [flip(value, 1) for value in mids]
        mids[1] = after(mids[1], grad_mlps_side)
    channels = jnp.einsum("rsc,rcg->rsg", selector_rows, group_rows, precision=highest)
    channels = lax.dynamic_slice_in_dim(
        jnp.repeat(tiled(channels), CHAN_GROUP, axis=2), row_at * hidden_part, hidden_part, 2
    )
    hidden_act, grad_pre, grad_own, out_own, low = feed(
        place,
        up_sources,
        mids,
        grad_mlps,
        channels,
        down_weight,
        chunk,
        tokens,
        low_rows,
    )

    if rows == 2:
        low = cross(low)
    else:
        low = low.reshape(rows, tokens, 2 * D)
        low = lax.psum_scatter(low, "fsdp", scatter_dimension=0, tiled=True)
        low = low.reshape(tokens, 2 * D)
        grad_own, out_own = jnp.zeros_like(grad_own), jnp.zeros_like(out_own)

    if fast:

        def columns_of(array, column=0, cols=None):
            return [(array, column, array.shape[1] if cols is None else cols)]

        act_side, pre_side = flip(hidden_act, 1), flip(grad_pre, 1)
        down_parts = term(
            place,
            [
                (
                    [columns_of(value) for value in (*grad_mlps, *grad_mlps_side)],
                    [columns_of(value) for value in (hidden_act, act_side)],
                )
            ],
            hidden_part,
        )
        grad_own = after(grad_own, down_parts)
        down_first = (flip(down_parts[0], 2), flip(down_parts[2], 4))

    grad_mid, own_pack, pack, grad_heads, block_out, mid_sums = mid_back(
        place,
        out_sources,
        grad_own,
        out_own,
        low,
        mid_state,
        attn_proj,
        tokens_here,
        *mods,
        head_slots,
        merged,
        normed_in,
    )
    if fast:

        crossed = cross(pack)
        own_side = flip(own_pack, 1)
        grad_heads = after(grad_heads, pack, own_side, pre_side, mids_side)
    grad_queries, *parts = attend_back(queries, kv_window, bias_t, grad_heads)
    if fast:
        parts[4], down_first = lax.optimization_barrier((parts[4], down_first))
    if paired:
        handed = flip(parts[4], 1)
        near_side = flip(parts[1], 1)
        zero = jnp.zeros((), bf16)
        down_part = parts[2] + jnp.where(core == 1, handed, zero)
        up_side = parts[3] + jnp.where(core == 0, handed, zero)
        from_above, from_below = shift(down_part, -2), shift(up_side, 2)
        arrivals = [near_side, from_above, from_below]
    else:
        arrivals = []
        for distance in range(1, reach + 1):
            arrivals += [
                shift(parts[2 * distance - 1], -distance),
                shift(parts[2 * distance], distance),
            ]
    if fast:
        q_crossed = cross(grad_queries)
        q_side = flip(grad_queries, 1)
        crossed_side = flip(crossed, 1)
        down_first, ignored = lax.optimization_barrier((down_first, (down_part, up_side)))

        def reduced(kept, arrived_part):
            value = (kept.astype(f32) + arrived_part.astype(f32)).astype(bf16)
            return value.reshape(2, value.shape[0] // 2, *value.shape[1:])

        def second_step(values):
            steps = []
            for value, bit in zip(values, (4, 2)):
                at = (seq_at // bit) % 2
                send = lax.dynamic_index_in_dim(value, 1 - at, 1, keepdims=False)
                keep_part = lax.dynamic_index_in_dim(value, at, 1, keepdims=False)
                steps.append((send, keep_part, bit))
            return steps

        def third_step(kept_parts, arrived_parts):
            value = jnp.concatenate(
                [
                    (kept_part.astype(f32) + arrived_part.astype(f32)).astype(bf16)
                    for kept_part, arrived_part in zip(kept_parts, arrived_parts)
                ],
                axis=1,
            )
            at = (seq_at // 8) % 2
            send = lax.dynamic_index_in_dim(value, 1 - at, 0, keepdims=False)
            return send, lax.dynamic_index_in_dim(value, at, 0, keepdims=False)

        down_values = [reduced(down_parts[1], down_first[0]), reduced(down_parts[3], down_first[1])]
        down_steps = second_step(down_values)
        down_second = [flip(send, bit) for send, ignored, bit in down_steps]
        up_parts = term(
            place,
            [
                (
                    [columns_of(value) for value in (grad_pre, pre_side)],
                    [columns_of(value) for value in (*mids, *mids_side)],
                ),
                (
                    [columns_of(value, D, D) for value in (own_pack, crossed, own_side, crossed_side)],
                    [
                        columns_of(value, 0, half)
                        for value in (own_pack, crossed, own_side, crossed_side)
                    ],
                ),
            ],
            half,
        )
        up_first = (flip(up_parts[0], 2), flip(up_parts[2], 4))
        arrivals[0] = after(arrivals[0], up_parts, q_side)
    grad_kv = parts[0].astype(f32)
    for arrival in arrivals:
        grad_kv = grad_kv + arrival.astype(f32)
    grad_kv = grad_kv.astype(bf16)
    if fast:
        grad_queries, down_second = lax.optimization_barrier((grad_queries, down_second))
    both_out, in_sums = in_back(
        place, qkv_sources, grad_queries, grad_kv, tokens_here, *mods, grad_mid, block_out
    )
    if fast:
        kv_crossed = cross(grad_kv)
        down_second = after(down_second, in_sums)
        down_send, down_keep = third_step([step[1] for step in down_steps], down_second)
        down_last = flip(down_send, 8)
        kv_crossed, in_sums = lax.optimization_barrier((kv_crossed, in_sums))
        up_first, grad_kv, q_crossed_late, ignored = lax.optimization_barrier(
            (up_first, grad_kv, q_crossed, kv_crossed)
        )

    def by_crop(sums):
        sums = sums.reshape(-1, repeats, slots, D)
        sums = jnp.sum(sums, axis=1) if repeats > 1 else sums[:, 0]
        return jnp.einsum("sc,nsd->cnd", selector, sums, precision=highest).astype(bf16)

    mod_grads = jnp.concatenate([in_sums, mid_sums], axis=0)
    if not fast:

        def product(acts, grads):
            return lax.dot_general(
                acts, grads, (((0,), (0,)), ((), ())), preferred_element_type=f32
            ).astype(bf16)

        def both(value):
            value = lax.psum_scatter(value, "fsdp", scatter_dimension=0, tiled=True)
            return lax.psum_scatter(value, "seq", scatter_dimension=1, tiled=True).astype(f32)

        grad_qkv = jnp.concatenate([grad_queries, grad_kv], axis=1)
        qkv_grad = both(product(normed_in, grad_qkv))
        out_grad = both(product(merged, own_pack[:, D:]))
        up_cols = lax.all_to_all(product(mids[0], grad_pre), "fsdp", 0, 1, tiled=True)
        up_grad = lax.psum_scatter(up_cols, "seq", scatter_dimension=1, tiled=True).astype(f32)
        down_cols = product(hidden_act, grad_mlps[0])
        down_grad = lax.psum_scatter(
            down_cols, "seq", scatter_dimension=1, tiled=True
        ).astype(f32)
    else:

        kv_side = flip(grad_kv, 1)
        kv_crossed_side, q_crossed_side = flip(kv_crossed, 1), flip(q_crossed_late, 1)

        def joined(first_part, second_part):
            return columns_of(first_part) + columns_of(second_part)

        up_steps = second_step([reduced(up_parts[1], up_first[0]), reduced(up_parts[3], up_first[1])])
        up_second = [flip(send, bit) for send, ignored, bit in up_steps]
        qkv_parts = term(
            place,
            [
                (
                    [
                        joined(grad_queries, grad_kv),
                        joined(q_crossed, kv_crossed),
                        joined(q_side, kv_side),
                        joined(q_crossed_side, kv_crossed_side),
                    ],
                    [
                        columns_of(value, half, half)
                        for value in (own_pack, crossed, own_side, crossed_side)
                    ],
                )
            ],
            half,
        )
        qkv_first = (flip(qkv_parts[0], 2), flip(qkv_parts[2], 4))
        qkv_steps = second_step(
            [reduced(qkv_parts[1], qkv_first[0]), reduced(qkv_parts[3], qkv_first[1])]
        )
        qkv_second = [flip(send, bit) for send, ignored, bit in qkv_steps]
        up_second, mod_grads, down_last, ignored = lax.optimization_barrier(
            (up_second, mod_grads, down_last, qkv_parts)
        )
        qkv_sends = [step[0] for step in qkv_steps]
        up_send, up_keep = third_step([step[1] for step in up_steps], up_second)
        qkv_send, qkv_keep = third_step([step[1] for step in qkv_steps], qkv_second)
        down_grad = jnp.transpose(down_keep.astype(f32) + down_last.astype(f32))
        up_last, ignored = lax.optimization_barrier((flip(up_send, 8), qkv_send))
        qkv_grad = jnp.transpose(qkv_keep.astype(f32) + flip(qkv_send, 8).astype(f32))
        mixed = up_keep.astype(f32) + up_last.astype(f32)
        up_rows, out_rows = hidden // seq, D // seq
        up_low, out_low = up_rows // 16 * 8, out_rows // 16 * 8
        parted = up_low + out_low
        rest = parted + up_rows - up_low
        up_mine = jnp.concatenate([mixed[:up_low], mixed[parted:rest]], axis=0).astype(bf16)
        out_grad = jnp.transpose(jnp.concatenate([mixed[up_low:parted], mixed[rest:]], axis=0))
        pairs = []
        for place_seq in range(seq):
            for place_row in range(2):
                high = (place_seq // 8) % 2
                target_seq = (place_seq & 7) | (place_row * 8)
                pairs.append((place_seq * 2 + place_row, target_seq * 2 + high))
        up_grad = jnp.transpose(lax.ppermute(up_mine, ("seq", "fsdp"), pairs)).astype(f32)
    mod_grads = by_crop(mod_grads).reshape(crops, 6 * D)
    if fast:
        share = columns // 2
        quarters = [mod_grads[:, i * share : (i + 1) * share] for i in range(4)]
        first_core = core == 0
        kept_sum = [jnp.where(first_core, quarters[i], quarters[i + 1]) for i in (0, 2)]
        sent_sum = [jnp.where(first_core, quarters[i + 1], quarters[i]) for i in (0, 2)]
        kept_sum, sent_sum = (jnp.stack(value) for value in (kept_sum, sent_sum))
        mod_grads = (kept_sum.astype(f32) + flip(sent_sum, 1).astype(f32)).astype(bf16)
        for bit, ahead in ((8, ()), (2, qkv_sends), (4, qkv_send)):
            mod_grads = (mod_grads.astype(f32) + flip(mod_grads, bit).astype(f32)).astype(bf16)
            mod_grads = after(mod_grads, ahead)
        own = pick(mod_grads[0], mod_grads[1])
        other = cross(pick(mod_grads[1], mod_grads[0]))
        own = jnp.concatenate([own, other], axis=0)
        other = flip(own, 1)
        mod_grads = jnp.concatenate(
            [jnp.where(first_core, own, other), jnp.where(first_core, other, own)], axis=1
        )
    else:
        mod_grads = lax.psum(mod_grads, "seq")
        split = jnp.transpose(mod_grads.reshape(crops, rows, columns), (1, 0, 2))
        mod_grads = lax.all_to_all(split, "fsdp", 0, 0).reshape(rows * crops, columns)
    ada_grad = outer(cond_rows, mod_grads)

    both_out = from_slots(both_out, f32, *(qkv_sends if fast else ()))
    block_out, input_grad = both_out[:, :D].astype(bf16), both_out[:, D:]
    return (
        block_out[None],
        input_grad[None],
        qkv_grad,
        out_grad,
        up_grad,
        down_grad,
        ada_grad,
    )


def solution(mesh):
    in_specs = (
        P("fsdp", "seq", None),
        P("fsdp", None, None),
        P("fsdp", None),
        P("fsdp", None),
        P("fsdp", None, None),
        P("fsdp", None, None),
        P("fsdp", "seq"),
        P("fsdp", None),
        P("fsdp", None),
        P("fsdp", None),
        P("fsdp", None),
        P(None, "fsdp"),
        P("fsdp", "seq", None),
    )
    out_specs = (
        P("fsdp", "seq", None),
        P("fsdp", "seq", None),
        P("fsdp", "seq"),
        P("fsdp", "seq"),
        P("fsdp", "seq"),
        P("fsdp", "seq"),
        P(None, "fsdp"),
    )
    return jax.shard_map(local, mesh=mesh, in_specs=in_specs, out_specs=out_specs, check_vma=False)
```

```python
import functools

import jax
import jax.numpy as jnp
import numpy as np
from jax import lax
from jax.experimental import pallas as pl
from jax.experimental.pallas import tpu as pltpu
from jax.sharding import PartitionSpec as P

D = 1152
H = 16
HD = 72
CHAN_GROUP = 128
PIECE_MAX = 16
PERIOD = 16

bf16 = jnp.bfloat16
f32 = jnp.float32
highest = lax.Precision.HIGHEST
norm_epsilon = 1e-06
masked_score = -1e30
score_scale = HD ** (-0.5)
VMEM_LIMIT = 56 * 1024 * 1024
VMEM_SPEC = pl.BlockSpec(memory_space=pltpu.VMEM)
COST = pl.CostEstimate(flops=1, transcendentals=0, bytes_accessed=1)


def params():
    return pltpu.CompilerParams(vmem_limit_bytes=VMEM_LIMIT)


def dot_nt(a, b):
    return lax.dot_general(a, b, (((1,), (1,)), ((), ())), preferred_element_type=f32)


def dot_nn(a, b):
    return lax.dot_general(a, b, (((1,), (0,)), ((), ())), preferred_element_type=f32)


def dot_tn(a, b):
    return lax.dot_general(a, b, (((0,), (0,)), ((), ())), preferred_element_type=f32)


def source_inputs(sources):
    arrays = [source[0] for source in sources]
    specs = [pl.BlockSpec(source[1], source[2]) for source in sources]
    parts = [(source[3], source[4]) for source in sources]
    return arrays, specs, parts


def fill(target_ref, place_ref, refs, parts):
    half = target_ref.shape[0] // 2
    mine = place_ref[0]
    for ref, (step, column) in zip(refs, parts):
        rows, cols = ref.shape
        if step == "all":
            start = 0
        elif step is None:
            start = pl.multiple_of(mine * half, 16)
        else:
            part = place_ref[step[0]] ^ step[1]
            start = pl.multiple_of((1 - mine) * half + part * rows, 16)
        target_ref[pl.ds(start, rows), pl.ds(column, cols)] = ref[...]


def whole(shape):
    return pl.BlockSpec(shape, lambda i, place: (0,) * len(shape))


def copies_in(target_ref, place_ref, refs, parts, sems):
    half = target_ref.shape[0] // 2
    mine = place_ref[0]
    copies = []
    for index, (ref, (source_column, cols, step, column)) in enumerate(zip(refs, parts)):
        rows = ref.shape[0]
        if step == "all":
            start = 0
        elif step is None:
            start = pl.multiple_of(mine * half, 16)
        else:
            part = place_ref[step[0]] ^ step[1]
            start = pl.multiple_of((1 - mine) * half + part * rows, 16)
        copies.append(
            (
                column,
                pltpu.make_async_copy(
                    ref.at[:, pl.ds(source_column, cols)],
                    target_ref.at[pl.ds(start, rows), pl.ds(column, cols)],
                    sems.at[index],
                ),
            )
        )
    return copies


def wait_for(copies, column):
    for at, copy in copies:
        if at == column:
            copy.wait()


def staged_call(kernel, place, sources, inputs, out_shapes, scratch, name):
    arrays = [source[0] for source in sources]
    parts = [source[1:] for source in sources]
    return pl.pallas_call(
        functools.partial(kernel, parts=parts),
        out_shape=out_shapes,
        grid_spec=pltpu.PrefetchScalarGridSpec(
            num_scalar_prefetch=1,
            grid=(1,),
            in_specs=[pl.BlockSpec(memory_space=pl.ANY)] * len(arrays)
            + [whole(value.shape) for value in inputs],
            out_specs=[whole(out.shape) for out in out_shapes],
            scratch_shapes=scratch + [pltpu.SemaphoreType.DMA((len(arrays),))],
        ),
        compiler_params=params(),
        cost_estimate=COST,
        name=name,
    )(place, *arrays, *inputs)


def shaped(*shape, dtype=f32):
    return jax.ShapeDtypeStruct(shape, dtype)


def normalized(values):
    centred = values - jnp.mean(values, axis=1, keepdims=True)
    inverse = lax.rsqrt(jnp.mean(centred * centred, axis=1, keepdims=True) + norm_epsilon)
    return centred * inverse, inverse


def normalized_back(grad, normed, inverse):
    mean_grad = jnp.mean(grad, axis=1, keepdims=True)
    mean_dot = jnp.mean(grad * normed, axis=1, keepdims=True)
    return (grad - mean_grad - normed * mean_dot) * inverse


def slot_rows(value):
    repeats = PERIOD // value.shape[0]
    return jnp.concatenate([value] * repeats, axis=0) if repeats > 1 else value


def mod_attn(place_ref, own_ref, other_ref, index):
    columns = pl.ds(index * D, D)
    return slot_rows(jnp.where(place_ref[6] == 0, own_ref[:, columns], other_ref[:, columns]))


def mod_mlp(place_ref, own_ref, other_ref, index):
    return mod_attn(place_ref, other_ref, own_ref, index)


def norm_in_kernel(place_ref, tokens_ref, own_ref, other_ref, out_ref, grad_ref):
    shift = mod_attn(place_ref, own_ref, other_ref, 0)
    scale = 1.0 + mod_attn(place_ref, own_ref, other_ref, 1)
    gate = mod_mlp(place_ref, own_ref, other_ref, 2)
    for start in range(0, tokens_ref.shape[0], PERIOD):
        rows = pl.ds(start, PERIOD)
        normed, ignored = normalized(tokens_ref[rows, pl.ds(0, D)].astype(f32))
        out_ref[rows, :] = (normed * scale + shift).astype(bf16)
        keep = tokens_ref[rows, pl.ds(2 * D, 128)].astype(f32)[:, :1]
        grad = tokens_ref[rows, pl.ds(D, D)].astype(f32)
        grad_ref[rows, :] = (grad * gate * keep).astype(bf16)


def norm_in(place, tokens, own, other):
    return pl.pallas_call(
        norm_in_kernel,
        out_shape=[shaped(tokens.shape[0], D, dtype=bf16)] * 2,
        in_specs=[pl.BlockSpec(memory_space=pltpu.SMEM)] + [VMEM_SPEC] * 3,
        out_specs=[VMEM_SPEC] * 2,
        compiler_params=params(),
        cost_estimate=COST,
        name="norm_in",
    )(place, tokens, own, other)


def project_kernel(place_ref, *refs, parts):
    count = len(parts)
    q_ref, kv_ref, weight_ref, window_ref, sems = refs[-5:]
    window_parts = refs[count:-5]
    copies = copies_in(weight_ref, place_ref, refs[:count], parts, sems)
    for column in (D, 2 * D, 0):
        for at, copy in copies:
            if at == column:
                copy.start()
    tokens = q_ref.shape[0]
    for index, part in enumerate(window_parts):
        window_ref[pl.ds(index * tokens, tokens), :] = part[...]
    for column in (D, 2 * D):
        wait_for(copies, column)
        for start in range(0, D, 384):
            kv_ref[:, pl.ds(column - D + start, 384)] = dot_nn(
                window_ref[...], weight_ref[:, pl.ds(column + start, 384)]
            ).astype(bf16)
    wait_for(copies, 0)
    for start in range(0, D, 384):
        q_ref[:, pl.ds(start, 384)] = dot_nn(
            window_parts[0][...], weight_ref[:, pl.ds(start, 384)]
        ).astype(bf16)


def project(place, sources, window_parts):
    tokens = window_parts[0].shape[0]
    keys = tokens * len(window_parts)
    return staged_call(
        project_kernel,
        place,
        sources,
        window_parts,
        [shaped(tokens, D, dtype=bf16), shaped(keys, 2 * D, dtype=bf16)],
        [pltpu.VMEM((D, 3 * D), bf16), pltpu.VMEM((keys, D), bf16)],
        "project",
    )


def head_window(head):
    start = head * HD
    low = start // 128 * 128
    width = 128 if start + HD - low <= 128 else 256
    return low, min(width, D - low), start - low


HEAD_GROUPS = ((0, 1), (2, 3), (4, 5), (6, 7), (8,), (9, 10), (11, 12), (13, 14), (15,))


def group_window(heads):
    windows = [head_window(head) for head in heads]
    return windows[0][0], max(window[1] for window in windows), [window[2] for window in windows]


def masked_rows(value, lanes):
    zero = jnp.zeros((), value.dtype)
    parts = [jnp.where(lane, value, zero) for lane in lanes]
    return jnp.concatenate(parts, axis=0) if len(parts) > 1 else parts[0]


def head_lanes(rows, width, first):
    lane = lax.broadcasted_iota(jnp.int32, (rows, width), 1)
    return (lane >= first) & (lane < first + HD)


def attend_kernel(place_ref, *refs, parts):
    count = len(parts)
    q_ref, kv_ref, bias_ref, mask_ref, tokens_ref, own_ref, other_ref = refs[count : count + 7]
    merged_ref, proj_ref, mid_ref, normed_ref, acc_ref, weight_ref, sems = refs[count + 7 :]
    gate = mod_attn(place_ref, own_ref, other_ref, 2)
    shift = mod_mlp(place_ref, own_ref, other_ref, 0)
    scale = 1.0 + mod_mlp(place_ref, own_ref, other_ref, 1)
    tokens = q_ref.shape[0]
    copies = copies_in(weight_ref, place_ref, refs[:count], parts, sems)
    for ignored, copy in copies:
        copy.start()
    acc_ref[...] = jnp.zeros_like(acc_ref)
    for heads in HEAD_GROUPS:
        low, width, firsts = group_window(heads)
        window = pl.ds(low, width)
        lanes = [head_lanes(tokens, width, first) for first in firsts]
        bias = jnp.concatenate([bias_ref[...]] * len(heads), axis=0)
        query = masked_rows(q_ref[:, window], lanes)
        scores = dot_nt(query, kv_ref[:, window]) * score_scale + bias
        top = jnp.max(scores, axis=1, keepdims=True)
        weights = jnp.exp(scores - top)
        probs = (weights * (1.0 / jnp.sum(weights, axis=1, keepdims=True))).astype(bf16)
        out = dot_nn(probs, kv_ref[:, pl.ds(D + low, width)])
        value = acc_ref[:, window]
        for index, lane in enumerate(lanes):
            value = value + jnp.where(lane, out[index * tokens : (index + 1) * tokens], 0.0)
        acc_ref[:, window] = value
    for start in range(0, tokens, PERIOD):
        rows = pl.ds(start, PERIOD)
        merged_ref[rows, :] = (acc_ref[rows, :] * mask_ref[...]).astype(bf16)
    wait_for(copies, 0)
    proj_ref[...] = dot_nn(merged_ref[...], weight_ref[...])
    for start in range(0, tokens, PERIOD):
        rows = pl.ds(start, PERIOD)
        mid = tokens_ref[rows, pl.ds(0, D)].astype(f32) + gate * proj_ref[rows, :]
        mid_ref[rows, :] = mid
        normed, ignored = normalized(mid)
        normed_ref[rows, :] = (normed * scale + shift).astype(bf16)


def attend(place, sources, *inputs):
    tokens = inputs[0].shape[0]
    return staged_call(
        attend_kernel,
        place,
        sources,
        inputs,
        [
            shaped(tokens, D, dtype=bf16),
            shaped(tokens, D),
            shaped(tokens, D),
            shaped(tokens, D, dtype=bf16),
        ],
        [pltpu.VMEM((tokens, D), f32), pltpu.VMEM((D, D), bf16)],
        "attend",
    )


def attend_back_kernel(
    q_ref, kv_ref, bias_ref, grad_ref, dq_ref, *refs
):
    tokens = q_ref.shape[0]
    dkv_refs, (dq_acc, dk_acc, dv_acc) = refs[:-3], refs[-3:]
    dq_acc[...] = jnp.zeros_like(dq_acc)
    dk_acc[...] = jnp.zeros_like(dk_acc)
    dv_acc[...] = jnp.zeros_like(dv_acc)
    for heads in HEAD_GROUPS:
        low, width, firsts = group_window(heads)
        window = pl.ds(low, width)
        lanes = [head_lanes(tokens, width, first) for first in firsts]
        bias = jnp.concatenate([bias_ref[...]] * len(heads), axis=1)
        query = masked_rows(q_ref[:, window], lanes)
        grad = masked_rows(grad_ref[:, window], lanes)
        keys = kv_ref[:, window]
        scores = dot_nt(keys, query) * score_scale + bias
        top = jnp.max(scores, axis=0, keepdims=True)
        weights = jnp.exp(scores - top)
        probs = weights * (1.0 / jnp.sum(weights, axis=0, keepdims=True))
        probs_low = probs.astype(bf16)
        grad_probs = dot_nt(kv_ref[:, pl.ds(D + low, width)], grad)
        row_dot = jnp.sum(probs_low.astype(f32) * grad_probs, axis=0, keepdims=True)
        grad_scores = (probs * (grad_probs - row_dot)).astype(bf16)
        dk_acc[:, window] += dot_nn(grad_scores, query)
        dv_acc[:, window] += dot_nn(probs_low, grad)
        back = dot_tn(grad_scores, keys)
        value = dq_acc[:, window]
        for index, lane in enumerate(lanes):
            value = value + jnp.where(lane, back[index * tokens : (index + 1) * tokens], 0.0)
        dq_acc[:, window] = value
    dq_ref[...] = (dq_acc[...] * score_scale).astype(bf16)
    for index, dkv_ref in enumerate(dkv_refs):
        rows = pl.ds(index * tokens, tokens)
        dkv_ref[:, pl.ds(0, D)] = (dk_acc[rows, :] * score_scale).astype(bf16)
        dkv_ref[:, pl.ds(D, D)] = dv_acc[rows, :].astype(bf16)


def attend_back(queries, kv_window, bias_t, grad_heads):
    tokens = queries.shape[0]
    keys = kv_window.shape[0]
    outs = [shaped(tokens, D, dtype=bf16)]
    outs += [shaped(tokens, 2 * D, dtype=bf16)] * (keys // tokens)
    return pl.pallas_call(
        attend_back_kernel,
        out_shape=outs,
        in_specs=[VMEM_SPEC] * 4,
        out_specs=[VMEM_SPEC] * len(outs),
        scratch_shapes=[
            pltpu.VMEM((tokens, D), f32),
            pltpu.VMEM((keys, D), f32),
            pltpu.VMEM((keys, D), f32),
        ],
        compiler_params=params(),
        cost_estimate=COST,
        name="attend_back",
    )(queries, kv_window, bias_t, grad_heads)


def feed_kernel(place_ref, *refs, parts, arrays):
    count = len(parts)
    mid_refs, grad_refs = refs[count : count + arrays], refs[count + arrays : count + 2 * arrays]
    channel_ref, down_ref = refs[count + 2 * arrays : count + 2 * arrays + 2]
    act_ref, pre_ref, grad_own, out_own, low_ref = refs[-12:-7]
    weight_ref, grad_acc, out_acc, mid_all, grad_all, pre_acc, back_acc = refs[-7:]
    own_rows = grad_own.shape[0]
    step, steps = pl.program_id(0), pl.num_programs(0)
    rows, cols = act_ref.shape
    groups = channel_ref.shape[0]
    tokens = rows // groups

    @pl.when(step == 0)
    def _():
        grad_acc[...] = jnp.zeros_like(grad_acc)
        out_acc[...] = jnp.zeros_like(out_acc)
        share = rows // arrays
        for index in range(arrays):
            part = pl.ds(index * share, share)
            mid_all[part, :] = mid_refs[index][...]
            grad_all[part, :] = grad_refs[index][...]

    fill(weight_ref, place_ref, refs[:count], parts)
    root = 0.7978845608028654
    pre_acc[...] = dot_nn(mid_all[...], weight_ref[...])
    back_acc[...] = dot_nt(grad_all[...], down_ref[...])
    for group, start in [(g, t) for g in range(groups) for t in range(0, tokens, PERIOD)]:
        span = pl.ds(group * tokens + start, PERIOD)
        channels = channel_ref[group]
        pre, grad_act = pre_acc[span, :], back_acc[span, :]
        square = pre * pre
        inner = jnp.tanh(root * (pre + 0.044715 * (square * pre)))
        half_sum = 0.5 + 0.5 * inner
        act_ref[span, :] = (pre * half_sum * channels).astype(bf16)
        slope = half_sum + (0.5 * pre) * (1.0 - inner * inner) * (
            root + (3.0 * 0.044715 * root) * square
        )
        pre_ref[span, :] = (grad_act * channels * slope).astype(bf16)
    grad_acc[...] += dot_nt(pre_ref[...], weight_ref[...])
    out_acc[...] += dot_nn(act_ref[...], down_ref[...])

    @pl.when(step == steps - 1)
    def _():
        skip = rows - low_ref.shape[0]
        grad_own[...] = grad_acc[pl.ds(0, own_rows), :]
        out_own[...] = out_acc[pl.ds(0, own_rows), :]
        low_ref[:, pl.ds(0, D)] = grad_acc[pl.ds(skip, rows - skip), :].astype(bf16)
        low_ref[:, pl.ds(D, D)] = out_acc[pl.ds(skip, rows - skip), :].astype(bf16)


def feed(place, sources, mids, grads, channels, down, chunk, tokens, low_rows):
    arrays, specs, parts = source_inputs(sources)
    rows = sum(mid.shape[0] for mid in mids)
    width = down.shape[0]
    by_chunk = pl.BlockSpec((rows, chunk), lambda i, place: (0, i))
    own, low = (tokens, D), (low_rows, 2 * D)
    return pl.pallas_call(
        functools.partial(feed_kernel, parts=parts, arrays=len(mids)),
        out_shape=[
            shaped(rows, width, dtype=bf16),
            shaped(rows, width, dtype=bf16),
            shaped(*own),
            shaped(*own),
            shaped(*low, dtype=bf16),
        ],
        grid_spec=pltpu.PrefetchScalarGridSpec(
            num_scalar_prefetch=1,
            grid=(width // chunk,),
            in_specs=specs
            + [whole(value.shape) for value in (*mids, *grads)]
            + [
                pl.BlockSpec(
                    (channels.shape[0], PERIOD, chunk), lambda i, place: (0, 0, i)
                ),
                pl.BlockSpec((chunk, D), lambda i, place: (i, 0)),
            ],
            out_specs=[by_chunk, by_chunk, whole(own), whole(own), whole(low)],
            scratch_shapes=[
                pltpu.VMEM((D, chunk), bf16),
                pltpu.VMEM((rows, D), f32),
                pltpu.VMEM((rows, D), f32),
                pltpu.VMEM((rows, D), bf16),
                pltpu.VMEM((rows, D), bf16),
                pltpu.VMEM((rows, chunk), f32),
                pltpu.VMEM((rows, chunk), f32),
            ],
        ),
        compiler_params=params(),
        cost_estimate=COST,
        name="feed",
    )(place, *arrays, *mids, *grads, channels, down)


def mid_back_kernel(place_ref, *refs, parts):
    count = len(parts)
    own_ref, out_ref, other_ref, mid_ref, proj_ref, late_ref = refs[count : count + 6]
    mod_own, mod_other, mask_ref, attn_ref, normed_ref = refs[count + 6 : count + 11]
    grad_mid_ref, own_pack_ref, pack_ref, heads_ref, block_ref, sums_ref = refs[
        count + 11 : count + 17
    ]
    weight_ref, merged_ref, sems = refs[count + 17 :]
    copies = copies_in(weight_ref, place_ref, refs[:count], parts, sems)
    for ignored, copy in copies:
        copy.start()
    scale = 1.0 + mod_mlp(place_ref, mod_own, mod_other, 1)
    gate = mod_attn(place_ref, mod_own, mod_other, 2)
    out_gate = mod_mlp(place_ref, mod_own, mod_other, 2)
    first = place_ref[0] == 0
    half = D // 2
    for index, ref in enumerate((attn_ref, normed_ref)):
        low, high = ref[:, pl.ds(0, half)], ref[:, pl.ds(half, half)]
        own_pack_ref[:, pl.ds(index * half, half)] = jnp.where(first, low, high)
        pack_ref[:, pl.ds(index * half, half)] = jnp.where(first, high, low)
    tokens = own_ref.shape[0]
    sums = [jnp.zeros((PERIOD, D), f32) for ignored in range(4)]
    for start in range(0, tokens, PERIOD):
        rows = pl.ds(start, PERIOD)
        normed, inverse = normalized(mid_ref[rows, :])
        grad = own_ref[rows, :] + other_ref[rows, pl.ds(0, D)].astype(f32)
        grad_out = late_ref[rows, pl.ds(D, D)].astype(f32)
        grad_mid = grad_out + normalized_back(grad * scale, normed, inverse)
        grad_mid_ref[rows, :] = grad_mid
        grad_attn = (grad_mid * gate).astype(bf16)
        own_pack_ref[rows, pl.ds(D, D)] = grad_attn
        pack_ref[rows, pl.ds(D, D)] = grad_attn
        out = out_ref[rows, :] + other_ref[rows, pl.ds(D, D)].astype(f32)
        out = out * late_ref[rows, pl.ds(2 * D, 128)].astype(f32)[:, :1]
        block_ref[rows, :] = (mid_ref[rows, :] + out_gate * out).astype(bf16)
        for index, value in enumerate(
            (grad_mid * proj_ref[rows, :], grad, grad * normed, grad_out * out)
        ):
            sums[index] += value
    for index in range(4):
        sums_ref[index] = sums[index]
    wait_for(copies, 0)
    merged_ref[...] = dot_nt(pack_ref[:, pl.ds(D, D)], weight_ref[...])
    for start in range(0, tokens, PERIOD):
        rows = pl.ds(start, PERIOD)
        heads_ref[rows, :] = (merged_ref[rows, :] * mask_ref[...]).astype(bf16)


def mid_back(place, sources, *inputs):
    tokens = inputs[0].shape[0]
    return staged_call(
        mid_back_kernel,
        place,
        sources,
        inputs,
        [
            shaped(tokens, D),
            shaped(tokens, 2 * D, dtype=bf16),
            shaped(tokens, 2 * D, dtype=bf16),
            shaped(tokens, D, dtype=bf16),
            shaped(tokens, D, dtype=bf16),
            shaped(4, PERIOD, D),
        ],
        [pltpu.VMEM((D, D), bf16), pltpu.VMEM((tokens, D), f32)],
        "mid_back",
    )


def in_back_kernel(place_ref, *refs, parts):
    count = len(parts)
    dq_ref, dkv_ref, tokens_ref, mod_own, mod_other = refs[count : count + 5]
    grad_mid_ref, block_ref = refs[count + 5 : count + 7]
    both_ref, sums_ref, weight_ref, grad_ref, sems = refs[count + 7 :]
    tokens = dq_ref.shape[0]
    copies = copies_in(weight_ref, place_ref, refs[:count], parts, sems)
    for column in (D, 2 * D, 0):
        for at, copy in copies:
            if at == column:
                copy.start()
    both_ref[:, pl.ds(0, D)] = block_ref[...]
    wait_for(copies, D)
    grad_ref[...] = dot_nt(dkv_ref[:, pl.ds(0, D)], weight_ref[:, pl.ds(D, D)])
    wait_for(copies, 2 * D)
    grad_ref[...] += dot_nt(dkv_ref[:, pl.ds(D, D)], weight_ref[:, pl.ds(2 * D, D)])
    wait_for(copies, 0)
    grad_ref[...] += dot_nt(dq_ref[...], weight_ref[:, pl.ds(0, D)])
    scale = 1.0 + mod_attn(place_ref, mod_own, mod_other, 1)
    shift_sum = jnp.zeros((PERIOD, D), f32)
    scale_sum = jnp.zeros((PERIOD, D), f32)
    for start in range(0, tokens, PERIOD):
        rows = pl.ds(start, PERIOD)
        normed, inverse = normalized(tokens_ref[rows, pl.ds(0, D)].astype(f32))
        grad = grad_ref[rows, :]
        back = normalized_back(grad * scale, normed, inverse)
        both_ref[rows, pl.ds(D, D)] = (grad_mid_ref[rows, :] + back).astype(bf16)
        shift_sum += grad
        scale_sum += grad * normed
    sums_ref[0] = shift_sum
    sums_ref[1] = scale_sum


def in_back(place, sources, *inputs):
    tokens = inputs[0].shape[0]
    return staged_call(
        in_back_kernel,
        place,
        sources,
        inputs,
        [shaped(tokens, 2 * D, dtype=bf16), shaped(2, PERIOD, D)],
        [pltpu.VMEM((D, 3 * D), bf16), pltpu.VMEM((tokens, D), f32)],
        "in_back",
    )


def term_kernel(place_ref, *refs, layout, outputs):
    joined = refs[-3 * len(layout) :]
    place_at = {0: place_ref[3], 1: place_ref[4]}
    core = place_ref[2]
    first_out = len(refs) - 3 * len(layout) - 2 * outputs
    for index, (pieces, chunk, plan) in enumerate(layout):
        grads_ref, acts_ref, acc_ref = joined[3 * index : 3 * index + 3]
        for target, ref_at, column, cols, row_to, col_to in pieces:
            value = refs[ref_at][:, pl.ds(column, cols)]
            into = grads_ref if target == 0 else acts_ref
            into[pl.ds(row_to, value.shape[0]), pl.ds(col_to, cols)] = value
        width = acts_ref.shape[1]
        for start in range(0, width, 576):
            span = pl.ds(start, 576)
            acc_ref[:, span] = dot_tn(grads_ref[...], acts_ref[:, span])
        for out_index, (first, count, into_row, axis) in enumerate(plan):
            at = place_at[axis]
            for side_at, side in ((0, 1 - at), (1, at)):
                out_ref = refs[first_out + 2 * out_index + side_at]
                blocks, lanes = out_ref.shape[0], out_ref.shape[2]
                lane_blocks = width // lanes
                for block in range(blocks):
                    lane, rest = divmod(block, blocks // lane_blocks)
                    if axis == 0:
                        line = rest * 4 + side * 2 + core
                    else:
                        line = (rest // 2) * 8 + side * 4 + (rest % 2) * 2 + core
                    start = pl.multiple_of(line * chunk + first, 8)
                    out_ref[block, pl.ds(into_row, count), :] = acc_ref[
                        pl.ds(start, count), pl.ds(lane * lanes, lanes)
                    ].astype(bf16)


def term(place, weights, width):
    arrays, layout, scratch, rows_out = [], [], [], [0, 0]
    for grads, acts in weights:
        pieces, shapes = [], []
        for target, value in ((0, grads), (1, acts)):
            row_to = 0
            for group in value:
                col_to = 0
                for array, column, cols in group:
                    pieces.append((target, len(arrays), column, cols, row_to, col_to))
                    arrays.append(array)
                    col_to += cols
                row_to += group[0][0].shape[0]
            shapes.append((row_to, col_to))
        (depth, columns), (_, rows) = shapes
        chunk = columns // (16 * width // rows)
        first = chunk // 16 * 8
        plan = [(0, first, rows_out[0], 0), (first, chunk - first, rows_out[1], 1)]
        rows_out = [rows_out[0] + first, rows_out[1] + chunk - first]
        layout.append((pieces, chunk, plan))
        scratch += [
            pltpu.VMEM((depth, columns), bf16),
            pltpu.VMEM((depth, rows), bf16),
            pltpu.VMEM((columns, rows), f32),
        ]
    outs = [shaped(4, rows_out[axis], width, dtype=bf16) for axis in (0, 0, 1, 1)]
    return pl.pallas_call(
        functools.partial(term_kernel, layout=layout, outputs=2),
        out_shape=outs,
        in_specs=[pl.BlockSpec(memory_space=pltpu.SMEM)] + [VMEM_SPEC] * len(arrays),
        out_specs=[VMEM_SPEC] * len(outs),
        scratch_shapes=scratch,
        compiler_params=params(),
        cost_estimate=COST,
        name="term",
    )(place, *arrays)


def outer_kernel(left_ref, right_ref, out_ref, value_ref, sems):
    copies = []
    for index in range(value_ref.shape[0] // 128):
        rows = pl.ds(index * 128, 128)
        value_ref[rows, :] = dot_tn(left_ref[:, rows], right_ref[...])
        copies.append(
            pltpu.make_async_copy(value_ref.at[rows, :], out_ref.at[rows, :], sems.at[index])
        )
        copies[-1].start()
    for copy in copies:
        copy.wait()


def outer(left, right):
    depth, rows = left.shape
    columns = right.shape[1]
    return pl.pallas_call(
        outer_kernel,
        out_shape=shaped(rows, columns),
        in_specs=[VMEM_SPEC] * 2,
        out_specs=pl.BlockSpec(memory_space=pl.ANY),
        scratch_shapes=[
            pltpu.VMEM((rows, columns), f32),
            pltpu.SemaphoreType.DMA((rows // 128,)),
        ],
        compiler_params=params(),
        cost_estimate=COST,
        name="outer",
    )(left, right)


def running_ends(pieces):
    index = jnp.arange(pieces.shape[0], dtype=jnp.int32)
    return jnp.sum(jnp.where(index[None, :] <= index[:, None], pieces[None, :], 0), axis=1)


def crop_of(slots, ends):
    return jnp.sum((slots[..., None] >= ends[:-1]).astype(jnp.int32), axis=-1)


def one_hot(crops, count):
    return (crops[..., None] == jnp.arange(count, dtype=jnp.int32)).astype(f32)


def block_order(size):
    def device(block):
        chip, core = block // 2, block % 2
        return 2 * (chip ^ ((chip >> 1) & 1)) + core if size % 8 == 0 else block

    return [device(block) for block in range(size)]


def local(
    tokens_in,
    condition,
    crop_pieces,
    pad_counts,
    head_mask,
    channel_mask,
    keep_mask,
    qkv_weight,
    out_weight,
    up_weight,
    down_weight,
    ada_weight,
    cotangent,
):
    seq = lax.axis_size("seq")
    rows = lax.axis_size("fsdp")
    tokens = tokens_in.shape[1]
    slots = tokens // seq
    repeats = PERIOD // slots
    crops = crop_pieces.shape[1]
    hidden = up_weight.shape[1]
    hidden_part = hidden // rows
    half = D // rows
    seq_at = lax.axis_index("seq")
    row_at = lax.axis_index("fsdp")
    fast = rows == 2 and seq == 16
    order = block_order(seq)
    core = seq_at % 2
    if seq % 8 == 0:
        chip = seq_at // 2
        block_at = 2 * (chip ^ ((chip >> 1) & 1)) + core
    else:
        block_at = seq_at
    place = jnp.stack(
        [
            row_at,
            seq_at & 3,
            core,
            (seq_at // 2) % 2,
            (seq_at // 4) % 2,
            (seq_at // 4) % 2 * 2 + core,
            row_at if fast else jnp.zeros_like(row_at),
            (seq_at // 8) % 2,
        ]
    ).astype(jnp.int32)

    def flip(value, bit):
        return lax.ppermute(value, "seq", [(i, i ^ bit) for i in range(seq)])

    def cross(value):
        return lax.ppermute(value, "fsdp", [(0, 1), (1, 0)])

    def shift(value, distance):
        pairs = [
            (order[b], order[b + distance]) for b in range(seq) if 0 <= b + distance < seq
        ]
        return lax.ppermute(value, "seq", pairs)

    swap_rows = jnp.asarray(
        np.kron(np.eye(seq)[np.array(order)], np.eye(slots)), bf16
    )

    def to_slots(value):
        moved = jnp.dot(swap_rows, value, preferred_element_type=f32).astype(bf16)
        moved = lax.all_to_all(moved.reshape(seq, slots, -1), "seq", 0, 0)
        return moved.reshape(tokens, -1)

    def from_slots(value, dtype, *earlier):
        value = lax.all_to_all(value.reshape(seq, slots, -1), "seq", 0, 0)
        value = after(value, *earlier) if earlier else value
        value = value.reshape(tokens, -1)
        return jnp.dot(swap_rows, value, preferred_element_type=f32).astype(dtype)

    def after(value, *earlier):
        return lax.optimization_barrier((value, *earlier))[0]

    def fetch_first(slices, bit, *earlier):
        count = 2 if bit is None else 4
        part = core if bit is None else (seq_at // bit) % 2 * 2 + core
        row = after(part * (half // count), *earlier)
        parts = [
            lax.dynamic_slice(weight, (row, column), (half // count, cols))
            for weight, column, cols in slices
        ]
        return cross(jnp.concatenate(parts, axis=1) if len(parts) > 1 else parts[0])

    def gather_rows(value):
        if rows == 2:
            return jnp.stack([value, cross(value)])
        return lax.all_gather(value, "fsdp", axis=0)

    def pick(low_part, high_part):
        return jnp.where(row_at == 0, low_part, high_part)

    def tiled(value):
        return jnp.concatenate([value] * repeats, axis=-2) if repeats > 1 else value

    slot_index = block_at * slots + jnp.arange(slots, dtype=jnp.int32)
    ends = running_ends(crop_pieces[0])
    crop_here = crop_of(slot_index, ends)
    selector = one_hot(crop_here, crops)
    pads = pad_counts[0]

    cond_act = jax.nn.silu(condition[0]).astype(bf16)
    extra = jnp.concatenate(
        [channel_mask[0].astype(bf16), crop_pieces[0].astype(bf16)[:, None]], axis=1
    )
    extra = jnp.pad(extra, ((0, 0), (0, 128 - extra.shape[1])))
    packed = gather_rows(jnp.concatenate([cond_act, extra], axis=1))
    groups = channel_mask.shape[2]
    cond_rows = packed[:, :, :D].reshape(rows * crops, D)
    group_rows = packed[:, :, D : D + groups].astype(f32)
    ends_rows = jax.vmap(running_ends)(packed[:, :, D + groups].astype(jnp.int32))
    selector_rows = jax.vmap(lambda own: one_hot(crop_of(slot_index, own), crops))(ends_rows)

    columns = ada_weight.shape[1]
    quarter = half // 4
    if fast:
        k_first = fetch_first([(qkv_weight, D, D), (out_weight, 0, D)], 2, seq_at)
        k_second = flip(k_first, 2)
    mod_rows = jnp.dot(cond_rows, ada_weight, preferred_element_type=f32)
    mod_rows = mod_rows.reshape(rows, crops, columns)
    if rows == 2:
        mod_slots = jnp.einsum("rsc,rcm->rsm", selector_rows, mod_rows, precision=highest)
        if fast:
            mod_slots = after(mod_slots, k_first)
        arrived = cross(mod_slots[1])
        mods = (mod_slots[0], arrived)
    else:
        mine = lax.all_to_all(mod_rows, "fsdp", 0, 0)
        mine = jnp.transpose(mine, (1, 0, 2)).reshape(crops, rows * columns)
        mine = jnp.dot(selector, mine, precision=highest)
        mods = (mine[:, : 3 * D], mine[:, 3 * D :])

    kept = jnp.broadcast_to(keep_mask[0].astype(bf16)[:, None], (tokens, 128))
    tokens_here = to_slots(jnp.concatenate([tokens_in[0], cotangent[0], kept], axis=1))
    def block(at):
        return lambda i, place: (0, at)

    if fast:
        chunk = 768

        def spread(first, second):
            return (first, flip(first, 1), second, flip(second, 1))

        other_part = (1 - row_at) * hidden_part
        v_first = fetch_first([(qkv_weight, 2 * D, D)], 4, mod_slots)
        q_first = fetch_first([(qkv_weight, 0, D)], None, arrived)
        tokens_here = after(tokens_here, k_second)
        normed_in, grad_mlp = norm_in(place, tokens_here, *mods)
        up_first_piece = fetch_first(
            [(up_weight, other_part, hidden_part)], 2, q_first, normed_in
        )
        v_second = flip(v_first, 4)
        k_pieces, v_pieces = spread(k_first, k_second), spread(v_first, v_second)
        q_pieces = (q_first, flip(q_first, 1))
        qkv_sources = [(qkv_weight, column, D, None, column) for column in (0, D, 2 * D)]
        for at, column, pieces in ((2, 0, q_pieces), (1, D, k_pieces), (5, 2 * D, v_pieces)):
            qkv_sources += [
                (piece, 0, D, (at, step), column) for step, piece in enumerate(pieces)
            ]
        out_sources = [(out_weight, 0, D, None, 0)]
        out_sources += [(piece, D, D, (1, step), 0) for step, piece in enumerate(k_pieces)]
        low_rows = tokens
    else:
        chunk = hidden_part
        qkv_full = lax.all_gather(qkv_weight, "fsdp", axis=0, tiled=True)
        out_full = lax.all_gather(out_weight, "fsdp", axis=0, tiled=True)
        up_part = lax.all_to_all(up_weight, "fsdp", 1, 0, tiled=True)
        qkv_sources = [(qkv_full, column, D, "all", column) for column in (0, D, 2 * D)]
        out_sources = [(out_full, 0, D, "all", 0)]
        up_sources = [(up_part, (D, hidden_part), block(0), "all", 0)]
        low_rows = rows * tokens

    if not fast:
        normed_in, grad_mlp = norm_in(place, tokens_here, *mods)

    reach = -(-(PIECE_MAX - 1) // slots)
    paired = reach == 2 and seq % 2 == 0
    if paired:
        below, above = shift(normed_in, 2), shift(normed_in, -2)
        if fast:
            above = after(above, v_second, q_first)
        passed = flip(jnp.where(core == 0, above, below), 1)
        near = [normed_in, flip(normed_in, 1), below, above, passed]
        near_at = [
            block_at,
            block_at ^ 1,
            block_at - 2,
            block_at + 2,
            block_at - 1 + 2 * core,
        ]
    else:
        near, near_at = [normed_in], [block_at]
        for distance in range(1, reach + 1):
            near += [shift(normed_in, distance), shift(normed_in, -distance)]
            near_at += [block_at - distance, block_at + distance]
    near_at = after(jnp.stack(near_at), normed_in)
    key_slots = near_at[:, None] * slots + jnp.arange(slots, dtype=jnp.int32)[None, :]
    inside = (near_at >= 0) & (near_at < seq)
    key_crop = jnp.where(inside[:, None], crop_of(key_slots, ends), -1)
    key_crop = jnp.where(
        key_slots[:, None, :] < tokens - pads[None, :, None], key_crop[:, None, :], -1
    ).reshape(-1)
    query_crop = jnp.broadcast_to(crop_here[None, :], (seq, slots)).reshape(tokens)
    bias = jnp.where(query_crop[:, None] == key_crop[None, :], 0.0, masked_score).astype(f32)
    bias_t = jnp.where(key_crop[:, None] == query_crop[None, :], 0.0, masked_score).astype(f32)
    head_slots = tiled(
        jnp.repeat(jnp.dot(selector, head_mask[0].astype(f32), precision=highest), HD, axis=1)
    )

    def row_list(value):
        if rows == 2:
            return [value, cross(value)]
        return [lax.all_gather(value, "fsdp", axis=0, tiled=True)]

    grad_mlps = row_list(grad_mlp)
    if fast:
        near[-1] = after(near[-1], grad_mlps[1])
    queries, kv_window = project(place, qkv_sources, near)
    if fast:
        up_second_piece = flip(after(up_first_piece, queries), 2)

    merged, attn_proj, mid_state, normed_mid = attend(
        place,
        out_sources,
        queries,
        kv_window,
        bias,
        head_slots,
        tokens_here,
        *mods,
    )

    mids = row_list(normed_mid)
    if fast:
        up_pieces = spread(up_first_piece, after(up_second_piece, mids[1]))
        chunks = hidden_part // chunk
        up_sources = [
            (up_weight, (half, chunk), lambda i, place: (0, place[0] * chunks + i), None, 0)
        ]
        up_sources += [
            (piece, (quarter, chunk), lambda i, place: (0, i), (1, step), 0)
            for step, piece in enumerate(up_pieces)
        ]
        grad_mlps_side = [flip(value, 1) for value in grad_mlps]
        mids_side = [flip(value, 1) for value in mids]
        mids[1] = after(mids[1], grad_mlps_side)
    channels = jnp.einsum("rsc,rcg->rsg", selector_rows, group_rows, precision=highest)
    channels = lax.dynamic_slice_in_dim(
        jnp.repeat(tiled(channels), CHAN_GROUP, axis=2), row_at * hidden_part, hidden_part, 2
    )
    hidden_act, grad_pre, grad_own, out_own, low = feed(
        place,
        up_sources,
        mids,
        grad_mlps,
        channels,
        down_weight,
        chunk,
        tokens,
        low_rows,
    )

    if rows == 2:
        low = cross(low)
    else:
        low = low.reshape(rows, tokens, 2 * D)
        low = lax.psum_scatter(low, "fsdp", scatter_dimension=0, tiled=True)
        low = low.reshape(tokens, 2 * D)
        grad_own, out_own = jnp.zeros_like(grad_own), jnp.zeros_like(out_own)

    if fast:

        def columns_of(array, column=0, cols=None):
            return [(array, column, array.shape[1] if cols is None else cols)]

        act_side, pre_side = flip(hidden_act, 1), flip(grad_pre, 1)
        down_parts = term(
            place,
            [
                (
                    [columns_of(value) for value in (*grad_mlps, *grad_mlps_side)],
                    [columns_of(value) for value in (hidden_act, act_side)],
                )
            ],
            hidden_part,
        )
        grad_own = after(grad_own, down_parts)
        down_first = (flip(down_parts[0], 2), flip(down_parts[2], 4))

    grad_mid, own_pack, pack, grad_heads, block_out, mid_sums = mid_back(
        place,
        out_sources,
        grad_own,
        out_own,
        low,
        mid_state,
        attn_proj,
        tokens_here,
        *mods,
        head_slots,
        merged,
        normed_in,
    )
    if fast:

        crossed = cross(pack)
        own_side = flip(own_pack, 1)
        grad_heads = after(grad_heads, pack, own_side, pre_side, mids_side)
    grad_queries, *parts = attend_back(queries, kv_window, bias_t, grad_heads)
    if fast:
        parts[4], down_first = lax.optimization_barrier((parts[4], down_first))
    if paired:
        handed = flip(parts[4], 1)
        near_side = flip(parts[1], 1)
        zero = jnp.zeros((), bf16)
        down_part = parts[2] + jnp.where(core == 1, handed, zero)
        up_side = parts[3] + jnp.where(core == 0, handed, zero)
        from_above, from_below = shift(down_part, -2), shift(up_side, 2)
        arrivals = [near_side, from_above, from_below]
    else:
        arrivals = []
        for distance in range(1, reach + 1):
            arrivals += [
                shift(parts[2 * distance - 1], -distance),
                shift(parts[2 * distance], distance),
            ]
    if fast:
        q_crossed = cross(grad_queries)
        q_side = flip(grad_queries, 1)
        crossed_side = flip(crossed, 1)
        down_first, ignored = lax.optimization_barrier((down_first, (down_part, up_side)))

        def reduced(kept, arrived_part):
            value = (kept.astype(f32) + arrived_part.astype(f32)).astype(bf16)
            return value.reshape(2, value.shape[0] // 2, *value.shape[1:])

        def second_step(values):
            steps = []
            for value, bit in zip(values, (4, 2)):
                at = (seq_at // bit) % 2
                send = lax.dynamic_index_in_dim(value, 1 - at, 1, keepdims=False)
                keep_part = lax.dynamic_index_in_dim(value, at, 1, keepdims=False)
                steps.append((send, keep_part, bit))
            return steps

        def third_step(kept_parts, arrived_parts):
            value = jnp.concatenate(
                [
                    (kept_part.astype(f32) + arrived_part.astype(f32)).astype(bf16)
                    for kept_part, arrived_part in zip(kept_parts, arrived_parts)
                ],
                axis=1,
            )
            at = (seq_at // 8) % 2
            send = lax.dynamic_index_in_dim(value, 1 - at, 0, keepdims=False)
            return send, lax.dynamic_index_in_dim(value, at, 0, keepdims=False)

        down_values = [reduced(down_parts[1], down_first[0]), reduced(down_parts[3], down_first[1])]
        down_steps = second_step(down_values)
        down_second = [flip(send, bit) for send, ignored, bit in down_steps]
        up_parts = term(
            place,
            [
                (
                    [columns_of(value) for value in (grad_pre, pre_side)],
                    [columns_of(value) for value in (*mids, *mids_side)],
                ),
                (
                    [columns_of(value, D, D) for value in (own_pack, crossed, own_side, crossed_side)],
                    [
                        columns_of(value, 0, half)
                        for value in (own_pack, crossed, own_side, crossed_side)
                    ],
                ),
            ],
            half,
        )
        up_first = (flip(up_parts[0], 2), flip(up_parts[2], 4))
        arrivals[0] = after(arrivals[0], up_parts, q_side)
    grad_kv = parts[0].astype(f32)
    for arrival in arrivals:
        grad_kv = grad_kv + arrival.astype(f32)
    grad_kv = grad_kv.astype(bf16)
    if fast:
        grad_queries, down_second = lax.optimization_barrier((grad_queries, down_second))
    both_out, in_sums = in_back(
        place, qkv_sources, grad_queries, grad_kv, tokens_here, *mods, grad_mid, block_out
    )
    if fast:
        kv_crossed = cross(grad_kv)
        down_second = after(down_second, in_sums)
        down_send, down_keep = third_step([step[1] for step in down_steps], down_second)
        down_last = flip(down_send, 8)
        kv_crossed, in_sums = lax.optimization_barrier((kv_crossed, in_sums))
        up_first, grad_kv, q_crossed_late, ignored = lax.optimization_barrier(
            (up_first, grad_kv, q_crossed, kv_crossed)
        )

    def by_crop(sums):
        sums = sums.reshape(-1, repeats, slots, D)
        sums = jnp.sum(sums, axis=1) if repeats > 1 else sums[:, 0]
        return jnp.einsum("sc,nsd->cnd", selector, sums, precision=highest).astype(bf16)

    mod_grads = jnp.concatenate([in_sums, mid_sums], axis=0)
    if not fast:

        def product(acts, grads):
            return lax.dot_general(
                acts, grads, (((0,), (0,)), ((), ())), preferred_element_type=f32
            ).astype(bf16)

        def both(value):
            value = lax.psum_scatter(value, "fsdp", scatter_dimension=0, tiled=True)
            return lax.psum_scatter(value, "seq", scatter_dimension=1, tiled=True).astype(f32)

        grad_qkv = jnp.concatenate([grad_queries, grad_kv], axis=1)
        qkv_grad = both(product(normed_in, grad_qkv))
        out_grad = both(product(merged, own_pack[:, D:]))
        up_cols = lax.all_to_all(product(mids[0], grad_pre), "fsdp", 0, 1, tiled=True)
        up_grad = lax.psum_scatter(up_cols, "seq", scatter_dimension=1, tiled=True).astype(f32)
        down_cols = product(hidden_act, grad_mlps[0])
        down_grad = lax.psum_scatter(
            down_cols, "seq", scatter_dimension=1, tiled=True
        ).astype(f32)
    else:

        kv_side = flip(grad_kv, 1)
        kv_crossed_side, q_crossed_side = flip(kv_crossed, 1), flip(q_crossed_late, 1)

        def joined(first_part, second_part):
            return columns_of(first_part) + columns_of(second_part)

        up_steps = second_step([reduced(up_parts[1], up_first[0]), reduced(up_parts[3], up_first[1])])
        up_second = [flip(send, bit) for send, ignored, bit in up_steps]
        qkv_parts = term(
            place,
            [
                (
                    [
                        joined(grad_queries, grad_kv),
                        joined(q_crossed, kv_crossed),
                        joined(q_side, kv_side),
                        joined(q_crossed_side, kv_crossed_side),
                    ],
                    [
                        columns_of(value, half, half)
                        for value in (own_pack, crossed, own_side, crossed_side)
                    ],
                )
            ],
            half,
        )
        qkv_first = (flip(qkv_parts[0], 2), flip(qkv_parts[2], 4))
        qkv_steps = second_step(
            [reduced(qkv_parts[1], qkv_first[0]), reduced(qkv_parts[3], qkv_first[1])]
        )
        qkv_second = [flip(send, bit) for send, ignored, bit in qkv_steps]
        up_second, mod_grads, down_last, ignored = lax.optimization_barrier(
            (up_second, mod_grads, down_last, qkv_parts)
        )
        qkv_sends = [step[0] for step in qkv_steps]
        up_send, up_keep = third_step([step[1] for step in up_steps], up_second)
        qkv_send, qkv_keep = third_step([step[1] for step in qkv_steps], qkv_second)
        down_grad = jnp.transpose(down_keep.astype(f32) + down_last.astype(f32))
        up_last, ignored = lax.optimization_barrier((flip(up_send, 8), qkv_send))
        qkv_grad = jnp.transpose(qkv_keep.astype(f32) + flip(qkv_send, 8).astype(f32))
        mixed = up_keep.astype(f32) + up_last.astype(f32)
        up_rows, out_rows = hidden // seq, D // seq
        up_low, out_low = up_rows // 16 * 8, out_rows // 16 * 8
        parted = up_low + out_low
        rest = parted + up_rows - up_low
        up_mine = jnp.concatenate([mixed[:up_low], mixed[parted:rest]], axis=0).astype(bf16)
        out_grad = jnp.transpose(jnp.concatenate([mixed[up_low:parted], mixed[rest:]], axis=0))
        pairs = []
        for place_seq in range(seq):
            for place_row in range(2):
                high = (place_seq // 8) % 2
                target_seq = (place_seq & 7) | (place_row * 8)
                pairs.append((place_seq * 2 + place_row, target_seq * 2 + high))
        up_grad = jnp.transpose(lax.ppermute(up_mine, ("seq", "fsdp"), pairs)).astype(f32)
    mod_grads = by_crop(mod_grads).reshape(crops, 6 * D)
    if fast:
        share = columns // 2
        quarters = [mod_grads[:, i * share : (i + 1) * share] for i in range(4)]
        first_core = core == 0
        kept_sum = [jnp.where(first_core, quarters[i], quarters[i + 1]) for i in (0, 2)]
        sent_sum = [jnp.where(first_core, quarters[i + 1], quarters[i]) for i in (0, 2)]
        kept_sum, sent_sum = (jnp.stack(value) for value in (kept_sum, sent_sum))
        mod_grads = (kept_sum.astype(f32) + flip(sent_sum, 1).astype(f32)).astype(bf16)
        for bit, ahead in ((8, ()), (2, qkv_sends), (4, qkv_send)):
            mod_grads = (mod_grads.astype(f32) + flip(mod_grads, bit).astype(f32)).astype(bf16)
            mod_grads = after(mod_grads, ahead)
        own = pick(mod_grads[0], mod_grads[1])
        other = cross(pick(mod_grads[1], mod_grads[0]))
        own = jnp.concatenate([own, other], axis=0)
        other = flip(own, 1)
        mod_grads = jnp.concatenate(
            [jnp.where(first_core, own, other), jnp.where(first_core, other, own)], axis=1
        )
    else:
        mod_grads = lax.psum(mod_grads, "seq")
        split = jnp.transpose(mod_grads.reshape(crops, rows, columns), (1, 0, 2))
        mod_grads = lax.all_to_all(split, "fsdp", 0, 0).reshape(rows * crops, columns)
    ada_grad = outer(cond_rows, mod_grads)

    both_out = from_slots(both_out, f32, *(qkv_sends if fast else ()))
    block_out, input_grad = both_out[:, :D].astype(bf16), both_out[:, D:]
    return (
        block_out[None],
        input_grad[None],
        qkv_grad,
        out_grad,
        up_grad,
        down_grad,
        ada_grad,
    )


def solution(mesh):
    in_specs = (
        P("fsdp", "seq", None),
        P("fsdp", None, None),
        P("fsdp", None),
        P("fsdp", None),
        P("fsdp", None, None),
        P("fsdp", None, None),
        P("fsdp", "seq"),
        P("fsdp", None),
        P("fsdp", None),
        P("fsdp", None),
        P("fsdp", None),
        P(None, "fsdp"),
        P("fsdp", "seq", None),
    )
    out_specs = (
        P("fsdp", "seq", None),
        P("fsdp", "seq", None),
        P("fsdp", "seq"),
        P("fsdp", "seq"),
        P("fsdp", "seq"),
        P("fsdp", "seq"),
        P(None, "fsdp"),
    )
    return jax.shard_map(local, mesh=mesh, in_specs=in_specs, out_specs=out_specs, check_vma=False)
```

```python
import functools

import jax
import jax.numpy as jnp
import numpy as np
from jax import lax
from jax.experimental import pallas as pl
from jax.experimental.pallas import tpu as pltpu
from jax.sharding import PartitionSpec as P

D = 1152
H = 16
HD = 72
CHAN_GROUP = 128
PIECE_MAX = 16
PERIOD = 16

bf16 = jnp.bfloat16
f32 = jnp.float32
highest = lax.Precision.HIGHEST
norm_epsilon = 1e-06
masked_score = -1e30
score_scale = HD ** (-0.5)
VMEM_LIMIT = 56 * 1024 * 1024
VMEM_SPEC = pl.BlockSpec(memory_space=pltpu.VMEM)
COST = pl.CostEstimate(flops=1, transcendentals=0, bytes_accessed=1)


def params():
    return pltpu.CompilerParams(vmem_limit_bytes=VMEM_LIMIT)


def dot_nt(a, b):
    return lax.dot_general(a, b, (((1,), (1,)), ((), ())), preferred_element_type=f32)


def dot_nn(a, b):
    return lax.dot_general(a, b, (((1,), (0,)), ((), ())), preferred_element_type=f32)


def dot_tn(a, b):
    return lax.dot_general(a, b, (((0,), (0,)), ((), ())), preferred_element_type=f32)


def source_inputs(sources):
    arrays = [source[0] for source in sources]
    specs = [pl.BlockSpec(source[1], source[2]) for source in sources]
    parts = [(source[3], source[4]) for source in sources]
    return arrays, specs, parts


def fill(target_ref, place_ref, refs, parts):
    half = target_ref.shape[0] // 2
    mine = place_ref[0]
    for ref, (step, column) in zip(refs, parts):
        rows, cols = ref.shape
        if step == "all":
            start = 0
        elif step is None:
            start = pl.multiple_of(mine * half, 16)
        else:
            part = place_ref[step[0]] ^ step[1]
            start = pl.multiple_of((1 - mine) * half + part * rows, 16)
        target_ref[pl.ds(start, rows), pl.ds(column, cols)] = ref[...]


def whole(shape):
    return pl.BlockSpec(shape, lambda i, place: (0,) * len(shape))


def copies_in(target_ref, place_ref, refs, parts, sems):
    half = target_ref.shape[0] // 2
    mine = place_ref[0]
    copies = []
    for index, (ref, (source_column, cols, step, column)) in enumerate(zip(refs, parts)):
        rows = ref.shape[0]
        if step == "all":
            start = 0
        elif step is None:
            start = pl.multiple_of(mine * half, 16)
        else:
            part = place_ref[step[0]] ^ step[1]
            start = pl.multiple_of((1 - mine) * half + part * rows, 16)
        copies.append(
            (
                column,
                pltpu.make_async_copy(
                    ref.at[:, pl.ds(source_column, cols)],
                    target_ref.at[pl.ds(start, rows), pl.ds(column, cols)],
                    sems.at[index],
                ),
            )
        )
    return copies


def wait_for(copies, column):
    for at, copy in copies:
        if at == column:
            copy.wait()


def staged_call(kernel, place, sources, inputs, out_shapes, scratch, name):
    arrays = [source[0] for source in sources]
    parts = [source[1:] for source in sources]
    return pl.pallas_call(
        functools.partial(kernel, parts=parts),
        out_shape=out_shapes,
        grid_spec=pltpu.PrefetchScalarGridSpec(
            num_scalar_prefetch=1,
            grid=(1,),
            in_specs=[pl.BlockSpec(memory_space=pl.ANY)] * len(arrays)
            + [whole(value.shape) for value in inputs],
            out_specs=[whole(out.shape) for out in out_shapes],
            scratch_shapes=scratch + [pltpu.SemaphoreType.DMA((len(arrays),))],
        ),
        compiler_params=params(),
        cost_estimate=COST,
        name=name,
    )(place, *arrays, *inputs)


def shaped(*shape, dtype=f32):
    return jax.ShapeDtypeStruct(shape, dtype)


def normalized(values):
    centred = values - jnp.mean(values, axis=1, keepdims=True)
    inverse = lax.rsqrt(jnp.mean(centred * centred, axis=1, keepdims=True) + norm_epsilon)
    return centred * inverse, inverse


def normalized_back(grad, normed, inverse):
    mean_grad = jnp.mean(grad, axis=1, keepdims=True)
    mean_dot = jnp.mean(grad * normed, axis=1, keepdims=True)
    return (grad - mean_grad - normed * mean_dot) * inverse


def slot_rows(value):
    repeats = PERIOD // value.shape[0]
    return jnp.concatenate([value] * repeats, axis=0) if repeats > 1 else value


def mod_attn(place_ref, own_ref, other_ref, index):
    columns = pl.ds(index * D, D)
    return slot_rows(jnp.where(place_ref[6] == 0, own_ref[:, columns], other_ref[:, columns]))


def mod_mlp(place_ref, own_ref, other_ref, index):
    return mod_attn(place_ref, other_ref, own_ref, index)


def norm_in_kernel(place_ref, tokens_ref, own_ref, other_ref, out_ref, grad_ref):
    shift = mod_attn(place_ref, own_ref, other_ref, 0)
    scale = 1.0 + mod_attn(place_ref, own_ref, other_ref, 1)
    gate = mod_mlp(place_ref, own_ref, other_ref, 2)
    for start in range(0, tokens_ref.shape[0], PERIOD):
        rows = pl.ds(start, PERIOD)
        normed, ignored = normalized(tokens_ref[rows, pl.ds(0, D)].astype(f32))
        out_ref[rows, :] = (normed * scale + shift).astype(bf16)
        keep = tokens_ref[rows, pl.ds(2 * D, 128)].astype(f32)[:, :1]
        grad = tokens_ref[rows, pl.ds(D, D)].astype(f32)
        grad_ref[rows, :] = (grad * gate * keep).astype(bf16)


def norm_in(place, tokens, own, other):
    return pl.pallas_call(
        norm_in_kernel,
        out_shape=[shaped(tokens.shape[0], D, dtype=bf16)] * 2,
        in_specs=[pl.BlockSpec(memory_space=pltpu.SMEM)] + [VMEM_SPEC] * 3,
        out_specs=[VMEM_SPEC] * 2,
        compiler_params=params(),
        cost_estimate=COST,
        name="norm_in",
    )(place, tokens, own, other)


def project_kernel(place_ref, *refs, parts):
    count = len(parts)
    q_ref, kv_ref, weight_ref, window_ref, sems = refs[-5:]
    window_parts = refs[count:-5]
    copies = copies_in(weight_ref, place_ref, refs[:count], parts, sems)
    for column in (D, 2 * D, 0):
        for at, copy in copies:
            if at == column:
                copy.start()
    tokens = q_ref.shape[0]
    for index, part in enumerate(window_parts):
        window_ref[pl.ds(index * tokens, tokens), :] = part[...]
    for column in (D, 2 * D):
        wait_for(copies, column)
        for start in range(0, D, 384):
            kv_ref[:, pl.ds(column - D + start, 384)] = dot_nn(
                window_ref[...], weight_ref[:, pl.ds(column + start, 384)]
            ).astype(bf16)
    wait_for(copies, 0)
    for start in range(0, D, 384):
        q_ref[:, pl.ds(start, 384)] = dot_nn(
            window_parts[0][...], weight_ref[:, pl.ds(start, 384)]
        ).astype(bf16)


def project(place, sources, window_parts):
    tokens = window_parts[0].shape[0]
    keys = tokens * len(window_parts)
    return staged_call(
        project_kernel,
        place,
        sources,
        window_parts,
        [shaped(tokens, D, dtype=bf16), shaped(keys, 2 * D, dtype=bf16)],
        [pltpu.VMEM((D, 3 * D), bf16), pltpu.VMEM((keys, D), bf16)],
        "project",
    )


def head_window(head):
    start = head * HD
    low = start // 128 * 128
    width = 128 if start + HD - low <= 128 else 256
    return low, min(width, D - low), start - low


HEAD_GROUPS = ((0, 1), (2, 3), (4, 5), (6, 7), (8,), (9, 10), (11, 12), (13, 14), (15,))


def group_window(heads):
    windows = [head_window(head) for head in heads]
    return windows[0][0], max(window[1] for window in windows), [window[2] for window in windows]


def masked_rows(value, lanes):
    zero = jnp.zeros((), value.dtype)
    parts = [jnp.where(lane, value, zero) for lane in lanes]
    return jnp.concatenate(parts, axis=0) if len(parts) > 1 else parts[0]


def head_lanes(rows, width, first):
    lane = lax.broadcasted_iota(jnp.int32, (rows, width), 1)
    return (lane >= first) & (lane < first + HD)


def attend_kernel(place_ref, *refs, parts):
    count = len(parts)
    q_ref, kv_ref, bias_ref, mask_ref, tokens_ref, own_ref, other_ref = refs[count : count + 7]
    merged_ref, proj_ref, mid_ref, normed_ref, acc_ref, weight_ref, sems = refs[count + 7 :]
    gate = mod_attn(place_ref, own_ref, other_ref, 2)
    shift = mod_mlp(place_ref, own_ref, other_ref, 0)
    scale = 1.0 + mod_mlp(place_ref, own_ref, other_ref, 1)
    tokens = q_ref.shape[0]
    copies = copies_in(weight_ref, place_ref, refs[:count], parts, sems)
    for ignored, copy in copies:
        copy.start()
    acc_ref[...] = jnp.zeros_like(acc_ref)
    for heads in HEAD_GROUPS:
        low, width, firsts = group_window(heads)
        window = pl.ds(low, width)
        lanes = [head_lanes(tokens, width, first) for first in firsts]
        bias = jnp.concatenate([bias_ref[...]] * len(heads), axis=0)
        query = masked_rows(q_ref[:, window], lanes)
        scores = dot_nt(query, kv_ref[:, window]) * score_scale + bias
        top = jnp.max(scores, axis=1, keepdims=True)
        weights = jnp.exp(scores - top)
        probs = (weights * (1.0 / jnp.sum(weights, axis=1, keepdims=True))).astype(bf16)
        out = dot_nn(probs, kv_ref[:, pl.ds(D + low, width)])
        value = acc_ref[:, window]
        for index, lane in enumerate(lanes):
            value = value + jnp.where(lane, out[index * tokens : (index + 1) * tokens], 0.0)
        acc_ref[:, window] = value
    for start in range(0, tokens, PERIOD):
        rows = pl.ds(start, PERIOD)
        merged_ref[rows, :] = (acc_ref[rows, :] * mask_ref[...]).astype(bf16)
    wait_for(copies, 0)
    proj_ref[...] = dot_nn(merged_ref[...], weight_ref[...])
    for start in range(0, tokens, PERIOD):
        rows = pl.ds(start, PERIOD)
        mid = tokens_ref[rows, pl.ds(0, D)].astype(f32) + gate * proj_ref[rows, :]
        mid_ref[rows, :] = mid
        normed, ignored = normalized(mid)
        normed_ref[rows, :] = (normed * scale + shift).astype(bf16)


def attend(place, sources, *inputs):
    tokens = inputs[0].shape[0]
    return staged_call(
        attend_kernel,
        place,
        sources,
        inputs,
        [
            shaped(tokens, D, dtype=bf16),
            shaped(tokens, D),
            shaped(tokens, D),
            shaped(tokens, D, dtype=bf16),
        ],
        [pltpu.VMEM((tokens, D), f32), pltpu.VMEM((D, D), bf16)],
        "attend",
    )


def attend_back_kernel(
    q_ref, kv_ref, bias_ref, grad_ref, dq_ref, *refs
):
    tokens = q_ref.shape[0]
    dkv_refs, (dq_acc, dk_acc, dv_acc) = refs[:-3], refs[-3:]
    dq_acc[...] = jnp.zeros_like(dq_acc)
    dk_acc[...] = jnp.zeros_like(dk_acc)
    dv_acc[...] = jnp.zeros_like(dv_acc)
    for heads in HEAD_GROUPS:
        low, width, firsts = group_window(heads)
        window = pl.ds(low, width)
        lanes = [head_lanes(tokens, width, first) for first in firsts]
        bias = jnp.concatenate([bias_ref[...]] * len(heads), axis=1)
        query = masked_rows(q_ref[:, window], lanes)
        grad = masked_rows(grad_ref[:, window], lanes)
        keys = kv_ref[:, window]
        scores = dot_nt(keys, query) * score_scale + bias
        top = jnp.max(scores, axis=0, keepdims=True)
        weights = jnp.exp(scores - top)
        probs = weights * (1.0 / jnp.sum(weights, axis=0, keepdims=True))
        probs_low = probs.astype(bf16)
        grad_probs = dot_nt(kv_ref[:, pl.ds(D + low, width)], grad)
        row_dot = jnp.sum(probs_low.astype(f32) * grad_probs, axis=0, keepdims=True)
        grad_scores = (probs * (grad_probs - row_dot)).astype(bf16)
        dk_acc[:, window] += dot_nn(grad_scores, query)
        dv_acc[:, window] += dot_nn(probs_low, grad)
        back = dot_tn(grad_scores, keys)
        value = dq_acc[:, window]
        for index, lane in enumerate(lanes):
            value = value + jnp.where(lane, back[index * tokens : (index + 1) * tokens], 0.0)
        dq_acc[:, window] = value
    dq_ref[...] = (dq_acc[...] * score_scale).astype(bf16)
    for index, dkv_ref in enumerate(dkv_refs):
        rows = pl.ds(index * tokens, tokens)
        dkv_ref[:, pl.ds(0, D)] = (dk_acc[rows, :] * score_scale).astype(bf16)
        dkv_ref[:, pl.ds(D, D)] = dv_acc[rows, :].astype(bf16)


def attend_back(queries, kv_window, bias_t, grad_heads):
    tokens = queries.shape[0]
    keys = kv_window.shape[0]
    outs = [shaped(tokens, D, dtype=bf16)]
    outs += [shaped(tokens, 2 * D, dtype=bf16)] * (keys // tokens)
    return pl.pallas_call(
        attend_back_kernel,
        out_shape=outs,
        in_specs=[VMEM_SPEC] * 4,
        out_specs=[VMEM_SPEC] * len(outs),
        scratch_shapes=[
            pltpu.VMEM((tokens, D), f32),
            pltpu.VMEM((keys, D), f32),
            pltpu.VMEM((keys, D), f32),
        ],
        compiler_params=params(),
        cost_estimate=COST,
        name="attend_back",
    )(queries, kv_window, bias_t, grad_heads)


def feed_kernel(place_ref, *refs, parts, arrays):
    count = len(parts)
    mid_refs, grad_refs = refs[count : count + arrays], refs[count + arrays : count + 2 * arrays]
    channel_ref, down_ref = refs[count + 2 * arrays : count + 2 * arrays + 2]
    act_ref, pre_ref, grad_own, out_own, low_ref = refs[-12:-7]
    weight_ref, grad_acc, out_acc, mid_all, grad_all, pre_acc, back_acc = refs[-7:]
    own_rows = grad_own.shape[0]
    step, steps = pl.program_id(0), pl.num_programs(0)
    rows, cols = act_ref.shape
    groups = channel_ref.shape[0]
    tokens = rows // groups

    @pl.when(step == 0)
    def _():
        grad_acc[...] = jnp.zeros_like(grad_acc)
        out_acc[...] = jnp.zeros_like(out_acc)
        share = rows // arrays
        for index in range(arrays):
            part = pl.ds(index * share, share)
            mid_all[part, :] = mid_refs[index][...]
            grad_all[part, :] = grad_refs[index][...]

    fill(weight_ref, place_ref, refs[:count], parts)
    root = 0.7978845608028654
    pre_acc[...] = dot_nn(mid_all[...], weight_ref[...])
    back_acc[...] = dot_nt(grad_all[...], down_ref[...])
    for group, start in [(g, t) for g in range(groups) for t in range(0, tokens, PERIOD)]:
        span = pl.ds(group * tokens + start, PERIOD)
        channels = channel_ref[group]
        pre, grad_act = pre_acc[span, :], back_acc[span, :]
        square = pre * pre
        inner = jnp.tanh(root * (pre + 0.044715 * (square * pre)))
        half_sum = 0.5 + 0.5 * inner
        act_ref[span, :] = (pre * half_sum * channels).astype(bf16)
        slope = half_sum + (0.5 * pre) * (1.0 - inner * inner) * (
            root + (3.0 * 0.044715 * root) * square
        )
        pre_ref[span, :] = (grad_act * channels * slope).astype(bf16)
    grad_acc[...] += dot_nt(pre_ref[...], weight_ref[...])
    out_acc[...] += dot_nn(act_ref[...], down_ref[...])

    @pl.when(step == steps - 1)
    def _():
        skip = rows - low_ref.shape[0]
        grad_own[...] = grad_acc[pl.ds(0, own_rows), :]
        out_own[...] = out_acc[pl.ds(0, own_rows), :]
        low_ref[:, pl.ds(0, D)] = grad_acc[pl.ds(skip, rows - skip), :].astype(bf16)
        low_ref[:, pl.ds(D, D)] = out_acc[pl.ds(skip, rows - skip), :].astype(bf16)


def feed(place, sources, mids, grads, channels, down, chunk, tokens, low_rows):
    arrays, specs, parts = source_inputs(sources)
    rows = sum(mid.shape[0] for mid in mids)
    width = down.shape[0]
    by_chunk = pl.BlockSpec((rows, chunk), lambda i, place: (0, i))
    own, low = (tokens, D), (low_rows, 2 * D)
    return pl.pallas_call(
        functools.partial(feed_kernel, parts=parts, arrays=len(mids)),
        out_shape=[
            shaped(rows, width, dtype=bf16),
            shaped(rows, width, dtype=bf16),
            shaped(*own),
            shaped(*own),
            shaped(*low, dtype=bf16),
        ],
        grid_spec=pltpu.PrefetchScalarGridSpec(
            num_scalar_prefetch=1,
            grid=(width // chunk,),
            in_specs=specs
            + [whole(value.shape) for value in (*mids, *grads)]
            + [
                pl.BlockSpec(
                    (channels.shape[0], PERIOD, chunk), lambda i, place: (0, 0, i)
                ),
                pl.BlockSpec((chunk, D), lambda i, place: (i, 0)),
            ],
            out_specs=[by_chunk, by_chunk, whole(own), whole(own), whole(low)],
            scratch_shapes=[
                pltpu.VMEM((D, chunk), bf16),
                pltpu.VMEM((rows, D), f32),
                pltpu.VMEM((rows, D), f32),
                pltpu.VMEM((rows, D), bf16),
                pltpu.VMEM((rows, D), bf16),
                pltpu.VMEM((rows, chunk), f32),
                pltpu.VMEM((rows, chunk), f32),
            ],
        ),
        compiler_params=params(),
        cost_estimate=COST,
        name="feed",
    )(place, *arrays, *mids, *grads, channels, down)


def mid_back_kernel(place_ref, *refs, parts):
    count = len(parts)
    own_ref, out_ref, other_ref, mid_ref, proj_ref, late_ref = refs[count : count + 6]
    mod_own, mod_other, mask_ref, attn_ref, normed_ref = refs[count + 6 : count + 11]
    grad_mid_ref, own_pack_ref, pack_ref, heads_ref, block_ref, sums_ref = refs[
        count + 11 : count + 17
    ]
    weight_ref, merged_ref, sems = refs[count + 17 :]
    copies = copies_in(weight_ref, place_ref, refs[:count], parts, sems)
    for ignored, copy in copies:
        copy.start()
    scale = 1.0 + mod_mlp(place_ref, mod_own, mod_other, 1)
    gate = mod_attn(place_ref, mod_own, mod_other, 2)
    out_gate = mod_mlp(place_ref, mod_own, mod_other, 2)
    first = place_ref[0] == 0
    half = D // 2
    for index, ref in enumerate((attn_ref, normed_ref)):
        low, high = ref[:, pl.ds(0, half)], ref[:, pl.ds(half, half)]
        own_pack_ref[:, pl.ds(index * half, half)] = jnp.where(first, low, high)
        pack_ref[:, pl.ds(index * half, half)] = jnp.where(first, high, low)
    tokens = own_ref.shape[0]
    sums = [jnp.zeros((PERIOD, D), f32) for ignored in range(4)]
    for start in range(0, tokens, PERIOD):
        rows = pl.ds(start, PERIOD)
        normed, inverse = normalized(mid_ref[rows, :])
        grad = own_ref[rows, :] + other_ref[rows, pl.ds(0, D)].astype(f32)
        grad_out = late_ref[rows, pl.ds(D, D)].astype(f32)
        grad_mid = grad_out + normalized_back(grad * scale, normed, inverse)
        grad_mid_ref[rows, :] = grad_mid
        grad_attn = (grad_mid * gate).astype(bf16)
        own_pack_ref[rows, pl.ds(D, D)] = grad_attn
        pack_ref[rows, pl.ds(D, D)] = grad_attn
        out = out_ref[rows, :] + other_ref[rows, pl.ds(D, D)].astype(f32)
        out = out * late_ref[rows, pl.ds(2 * D, 128)].astype(f32)[:, :1]
        block_ref[rows, :] = (mid_ref[rows, :] + out_gate * out).astype(bf16)
        for index, value in enumerate(
            (grad_mid * proj_ref[rows, :], grad, grad * normed, grad_out * out)
        ):
            sums[index] += value
    for index in range(4):
        sums_ref[index] = sums[index]
    wait_for(copies, 0)
    merged_ref[...] = dot_nt(pack_ref[:, pl.ds(D, D)], weight_ref[...])
    for start in range(0, tokens, PERIOD):
        rows = pl.ds(start, PERIOD)
        heads_ref[rows, :] = (merged_ref[rows, :] * mask_ref[...]).astype(bf16)


def mid_back(place, sources, *inputs):
    tokens = inputs[0].shape[0]
    return staged_call(
        mid_back_kernel,
        place,
        sources,
        inputs,
        [
            shaped(tokens, D),
            shaped(tokens, 2 * D, dtype=bf16),
            shaped(tokens, 2 * D, dtype=bf16),
            shaped(tokens, D, dtype=bf16),
            shaped(tokens, D, dtype=bf16),
            shaped(4, PERIOD, D),
        ],
        [pltpu.VMEM((D, D), bf16), pltpu.VMEM((tokens, D), f32)],
        "mid_back",
    )


def in_back_kernel(place_ref, *refs, parts):
    count = len(parts)
    dq_ref, dkv_ref, tokens_ref, mod_own, mod_other = refs[count : count + 5]
    grad_mid_ref, block_ref = refs[count + 5 : count + 7]
    both_ref, sums_ref, weight_ref, grad_ref, sems = refs[count + 7 :]
    tokens = dq_ref.shape[0]
    copies = copies_in(weight_ref, place_ref, refs[:count], parts, sems)
    for column in (D, 2 * D, 0):
        for at, copy in copies:
            if at == column:
                copy.start()
    both_ref[:, pl.ds(0, D)] = block_ref[...]
    wait_for(copies, D)
    grad_ref[...] = dot_nt(dkv_ref[:, pl.ds(0, D)], weight_ref[:, pl.ds(D, D)])
    wait_for(copies, 2 * D)
    grad_ref[...] += dot_nt(dkv_ref[:, pl.ds(D, D)], weight_ref[:, pl.ds(2 * D, D)])
    wait_for(copies, 0)
    grad_ref[...] += dot_nt(dq_ref[...], weight_ref[:, pl.ds(0, D)])
    scale = 1.0 + mod_attn(place_ref, mod_own, mod_other, 1)
    shift_sum = jnp.zeros((PERIOD, D), f32)
    scale_sum = jnp.zeros((PERIOD, D), f32)
    for start in range(0, tokens, PERIOD):
        rows = pl.ds(start, PERIOD)
        normed, inverse = normalized(tokens_ref[rows, pl.ds(0, D)].astype(f32))
        grad = grad_ref[rows, :]
        back = normalized_back(grad * scale, normed, inverse)
        both_ref[rows, pl.ds(D, D)] = (grad_mid_ref[rows, :] + back).astype(bf16)
        shift_sum += grad
        scale_sum += grad * normed
    sums_ref[0] = shift_sum
    sums_ref[1] = scale_sum


def in_back(place, sources, *inputs):
    tokens = inputs[0].shape[0]
    return staged_call(
        in_back_kernel,
        place,
        sources,
        inputs,
        [shaped(tokens, 2 * D, dtype=bf16), shaped(2, PERIOD, D)],
        [pltpu.VMEM((D, 3 * D), bf16), pltpu.VMEM((tokens, D), f32)],
        "in_back",
    )


def term_kernel(place_ref, *refs, layout, outputs):
    joined = refs[-3 * len(layout) :]
    place_at = {0: place_ref[3], 1: place_ref[4]}
    core = place_ref[2]
    first_out = len(refs) - 3 * len(layout) - 2 * outputs
    for index, (pieces, chunk, plan) in enumerate(layout):
        grads_ref, acts_ref, acc_ref = joined[3 * index : 3 * index + 3]
        for target, ref_at, column, cols, row_to, col_to in pieces:
            value = refs[ref_at][:, pl.ds(column, cols)]
            into = grads_ref if target == 0 else acts_ref
            into[pl.ds(row_to, value.shape[0]), pl.ds(col_to, cols)] = value
        width = acts_ref.shape[1]
        acc_ref[...] = dot_tn(grads_ref[...], acts_ref[...])
        for out_index, (first, count, into_row, axis) in enumerate(plan):
            at = place_at[axis]
            for side_at, side in ((0, 1 - at), (1, at)):
                out_ref = refs[first_out + 2 * out_index + side_at]
                blocks, lanes = out_ref.shape[0], out_ref.shape[2]
                lane_blocks = width // lanes
                for block in range(blocks):
                    lane, rest = divmod(block, blocks // lane_blocks)
                    if axis == 0:
                        line = rest * 4 + side * 2 + core
                    else:
                        line = (rest // 2) * 8 + side * 4 + (rest % 2) * 2 + core
                    start = pl.multiple_of(line * chunk + first, 8)
                    out_ref[block, pl.ds(into_row, count), :] = acc_ref[
                        pl.ds(start, count), pl.ds(lane * lanes, lanes)
                    ].astype(bf16)


def term(place, weights, width, eighths=4):
    arrays, layout, scratch, rows_out = [], [], [], [0, 0]
    for grads, acts in weights:
        pieces, shapes = [], []
        for target, value in ((0, grads), (1, acts)):
            row_to = 0
            for group in value:
                col_to = 0
                for array, column, cols in group:
                    pieces.append((target, len(arrays), column, cols, row_to, col_to))
                    arrays.append(array)
                    col_to += cols
                row_to += group[0][0].shape[0]
            shapes.append((row_to, col_to))
        (depth, columns), (_, rows) = shapes
        chunk = columns // (16 * width // rows)
        first = chunk * eighths // 64 * 8
        plan = [(0, first, rows_out[0], 0), (first, chunk - first, rows_out[1], 1)]
        rows_out = [rows_out[0] + first, rows_out[1] + chunk - first]
        layout.append((pieces, chunk, plan))
        scratch += [
            pltpu.VMEM((depth, columns), bf16),
            pltpu.VMEM((depth, rows), bf16),
            pltpu.VMEM((columns, rows), f32),
        ]
    outs = [shaped(4, rows_out[axis], width, dtype=bf16) for axis in (0, 0, 1, 1)]
    return pl.pallas_call(
        functools.partial(term_kernel, layout=layout, outputs=2),
        out_shape=outs,
        in_specs=[pl.BlockSpec(memory_space=pltpu.SMEM)] + [VMEM_SPEC] * len(arrays),
        out_specs=[VMEM_SPEC] * len(outs),
        scratch_shapes=scratch,
        compiler_params=params(),
        cost_estimate=COST,
        name="term",
    )(place, *arrays)


def outer_kernel(left_ref, right_ref, out_ref, value_ref, sems):
    copies = []
    for index in range(value_ref.shape[0] // 128):
        rows = pl.ds(index * 128, 128)
        value_ref[rows, :] = dot_tn(left_ref[:, rows], right_ref[...])
        copies.append(
            pltpu.make_async_copy(value_ref.at[rows, :], out_ref.at[rows, :], sems.at[index])
        )
        copies[-1].start()
    for copy in copies:
        copy.wait()


def outer(left, right):
    depth, rows = left.shape
    columns = right.shape[1]
    return pl.pallas_call(
        outer_kernel,
        out_shape=shaped(rows, columns),
        in_specs=[VMEM_SPEC] * 2,
        out_specs=pl.BlockSpec(memory_space=pl.ANY),
        scratch_shapes=[
            pltpu.VMEM((rows, columns), f32),
            pltpu.SemaphoreType.DMA((rows // 128,)),
        ],
        compiler_params=params(),
        cost_estimate=COST,
        name="outer",
    )(left, right)


def running_ends(pieces):
    index = jnp.arange(pieces.shape[0], dtype=jnp.int32)
    return jnp.sum(jnp.where(index[None, :] <= index[:, None], pieces[None, :], 0), axis=1)


def crop_of(slots, ends):
    return jnp.sum((slots[..., None] >= ends[:-1]).astype(jnp.int32), axis=-1)


def one_hot(crops, count):
    return (crops[..., None] == jnp.arange(count, dtype=jnp.int32)).astype(f32)


def block_order(size):
    def device(block):
        chip, core = block // 2, block % 2
        return 2 * (chip ^ ((chip >> 1) & 1)) + core if size % 8 == 0 else block

    return [device(block) for block in range(size)]


def local(
    tokens_in,
    condition,
    crop_pieces,
    pad_counts,
    head_mask,
    channel_mask,
    keep_mask,
    qkv_weight,
    out_weight,
    up_weight,
    down_weight,
    ada_weight,
    cotangent,
):
    seq = lax.axis_size("seq")
    rows = lax.axis_size("fsdp")
    tokens = tokens_in.shape[1]
    slots = tokens // seq
    repeats = PERIOD // slots
    crops = crop_pieces.shape[1]
    hidden = up_weight.shape[1]
    hidden_part = hidden // rows
    half = D // rows
    seq_at = lax.axis_index("seq")
    row_at = lax.axis_index("fsdp")
    fast = rows == 2 and seq == 16
    order = block_order(seq)
    core = seq_at % 2
    if seq % 8 == 0:
        chip = seq_at // 2
        block_at = 2 * (chip ^ ((chip >> 1) & 1)) + core
    else:
        block_at = seq_at
    place = jnp.stack(
        [
            row_at,
            seq_at & 3,
            core,
            (seq_at // 2) % 2,
            (seq_at // 4) % 2,
            (seq_at // 4) % 2 * 2 + core,
            row_at if fast else jnp.zeros_like(row_at),
            (seq_at // 8) % 2,
        ]
    ).astype(jnp.int32)

    def flip(value, bit):
        return lax.ppermute(value, "seq", [(i, i ^ bit) for i in range(seq)])

    def cross(value):
        return lax.ppermute(value, "fsdp", [(0, 1), (1, 0)])

    def shift(value, distance):
        pairs = [
            (order[b], order[b + distance]) for b in range(seq) if 0 <= b + distance < seq
        ]
        return lax.ppermute(value, "seq", pairs)

    swap_rows = jnp.asarray(
        np.kron(np.eye(seq)[np.array(order)], np.eye(slots)), bf16
    )

    def to_slots(value):
        moved = jnp.dot(swap_rows, value, preferred_element_type=f32).astype(bf16)
        moved = lax.all_to_all(moved.reshape(seq, slots, -1), "seq", 0, 0)
        return moved.reshape(tokens, -1)

    def from_slots(value, dtype, *earlier):
        value = lax.all_to_all(value.reshape(seq, slots, -1), "seq", 0, 0)
        value = after(value, *earlier) if earlier else value
        value = value.reshape(tokens, -1)
        return jnp.dot(swap_rows, value, preferred_element_type=f32).astype(dtype)

    def after(value, *earlier):
        return lax.optimization_barrier((value, *earlier))[0]

    def fetch_first(slices, bit, *earlier):
        count = 2 if bit is None else 4
        part = core if bit is None else (seq_at // bit) % 2 * 2 + core
        row = after(part * (half // count), *earlier)
        parts = [
            lax.dynamic_slice(weight, (row, column), (half // count, cols))
            for weight, column, cols in slices
        ]
        return cross(jnp.concatenate(parts, axis=1) if len(parts) > 1 else parts[0])

    def gather_rows(value):
        if rows == 2:
            return jnp.stack([value, cross(value)])
        return lax.all_gather(value, "fsdp", axis=0)

    def pick(low_part, high_part):
        return jnp.where(row_at == 0, low_part, high_part)

    def tiled(value):
        return jnp.concatenate([value] * repeats, axis=-2) if repeats > 1 else value

    slot_index = block_at * slots + jnp.arange(slots, dtype=jnp.int32)
    ends = running_ends(crop_pieces[0])
    crop_here = crop_of(slot_index, ends)
    selector = one_hot(crop_here, crops)
    pads = pad_counts[0]

    cond_act = jax.nn.silu(condition[0]).astype(bf16)
    extra = jnp.concatenate(
        [channel_mask[0].astype(bf16), crop_pieces[0].astype(bf16)[:, None]], axis=1
    )
    extra = jnp.pad(extra, ((0, 0), (0, 128 - extra.shape[1])))
    packed = gather_rows(jnp.concatenate([cond_act, extra], axis=1))
    groups = channel_mask.shape[2]
    cond_rows = packed[:, :, :D].reshape(rows * crops, D)
    group_rows = packed[:, :, D : D + groups].astype(f32)
    ends_rows = jax.vmap(running_ends)(packed[:, :, D + groups].astype(jnp.int32))
    selector_rows = jax.vmap(lambda own: one_hot(crop_of(slot_index, own), crops))(ends_rows)

    columns = ada_weight.shape[1]
    quarter = half // 4
    if fast:
        k_first = fetch_first([(qkv_weight, D, D), (out_weight, 0, D)], 2, seq_at)
        k_second = flip(k_first, 2)
    mod_rows = jnp.dot(cond_rows, ada_weight, preferred_element_type=f32)
    mod_rows = mod_rows.reshape(rows, crops, columns)
    if rows == 2:
        mod_slots = jnp.einsum("rsc,rcm->rsm", selector_rows, mod_rows, precision=highest)
        if fast:
            mod_slots = after(mod_slots, k_first)
        arrived = cross(mod_slots[1])
        mods = (mod_slots[0], arrived)
    else:
        mine = lax.all_to_all(mod_rows, "fsdp", 0, 0)
        mine = jnp.transpose(mine, (1, 0, 2)).reshape(crops, rows * columns)
        mine = jnp.dot(selector, mine, precision=highest)
        mods = (mine[:, : 3 * D], mine[:, 3 * D :])

    kept = jnp.broadcast_to(keep_mask[0].astype(bf16)[:, None], (tokens, 128))
    tokens_here = to_slots(jnp.concatenate([tokens_in[0], cotangent[0], kept], axis=1))
    def block(at):
        return lambda i, place: (0, at)

    if fast:
        chunk = 768

        def spread(first, second):
            return (first, flip(first, 1), second, flip(second, 1))

        other_part = (1 - row_at) * hidden_part
        v_first = fetch_first([(qkv_weight, 2 * D, D)], 4, mod_slots)
        q_first = fetch_first([(qkv_weight, 0, D)], None, arrived)
        tokens_here = after(tokens_here, k_second)
        normed_in, grad_mlp = norm_in(place, tokens_here, *mods)
        up_first_piece = fetch_first(
            [(up_weight, other_part, hidden_part)], 2, q_first, normed_in
        )
        v_second = flip(v_first, 4)
        k_pieces, v_pieces = spread(k_first, k_second), spread(v_first, v_second)
        q_pieces = (q_first, flip(q_first, 1))
        qkv_sources = [(qkv_weight, column, D, None, column) for column in (0, D, 2 * D)]
        for at, column, pieces in ((2, 0, q_pieces), (1, D, k_pieces), (5, 2 * D, v_pieces)):
            qkv_sources += [
                (piece, 0, D, (at, step), column) for step, piece in enumerate(pieces)
            ]
        out_sources = [(out_weight, 0, D, None, 0)]
        out_sources += [(piece, D, D, (1, step), 0) for step, piece in enumerate(k_pieces)]
        low_rows = tokens
    else:
        chunk = hidden_part
        qkv_full = lax.all_gather(qkv_weight, "fsdp", axis=0, tiled=True)
        out_full = lax.all_gather(out_weight, "fsdp", axis=0, tiled=True)
        up_part = lax.all_to_all(up_weight, "fsdp", 1, 0, tiled=True)
        qkv_sources = [(qkv_full, column, D, "all", column) for column in (0, D, 2 * D)]
        out_sources = [(out_full, 0, D, "all", 0)]
        up_sources = [(up_part, (D, hidden_part), block(0), "all", 0)]
        low_rows = rows * tokens

    if not fast:
        normed_in, grad_mlp = norm_in(place, tokens_here, *mods)

    reach = -(-(PIECE_MAX - 1) // slots)
    paired = reach == 2 and seq % 2 == 0
    if paired:
        below, above = shift(normed_in, 2), shift(normed_in, -2)
        if fast:
            above = after(above, v_second, q_first)
        passed = flip(jnp.where(core == 0, above, below), 1)
        near = [normed_in, flip(normed_in, 1), below, above, passed]
        near_at = [
            block_at,
            block_at ^ 1,
            block_at - 2,
            block_at + 2,
            block_at - 1 + 2 * core,
        ]
    else:
        near, near_at = [normed_in], [block_at]
        for distance in range(1, reach + 1):
            near += [shift(normed_in, distance), shift(normed_in, -distance)]
            near_at += [block_at - distance, block_at + distance]
    near_at = after(jnp.stack(near_at), normed_in)
    key_slots = near_at[:, None] * slots + jnp.arange(slots, dtype=jnp.int32)[None, :]
    inside = (near_at >= 0) & (near_at < seq)
    key_crop = jnp.where(inside[:, None], crop_of(key_slots, ends), -1)
    key_crop = jnp.where(
        key_slots[:, None, :] < tokens - pads[None, :, None], key_crop[:, None, :], -1
    ).reshape(-1)
    query_crop = jnp.broadcast_to(crop_here[None, :], (seq, slots)).reshape(tokens)
    bias = jnp.where(query_crop[:, None] == key_crop[None, :], 0.0, masked_score).astype(f32)
    bias_t = jnp.where(key_crop[:, None] == query_crop[None, :], 0.0, masked_score).astype(f32)
    head_slots = tiled(
        jnp.repeat(jnp.dot(selector, head_mask[0].astype(f32), precision=highest), HD, axis=1)
    )

    def row_list(value):
        if rows == 2:
            return [value, cross(value)]
        return [lax.all_gather(value, "fsdp", axis=0, tiled=True)]

    grad_mlps = row_list(grad_mlp)
    if fast:
        near[-1] = after(near[-1], grad_mlps[1])
    queries, kv_window = project(place, qkv_sources, near)
    if fast:
        up_second_piece = flip(after(up_first_piece, queries), 2)

    merged, attn_proj, mid_state, normed_mid = attend(
        place,
        out_sources,
        queries,
        kv_window,
        bias,
        head_slots,
        tokens_here,
        *mods,
    )

    mids = row_list(normed_mid)
    if fast:
        up_pieces = spread(up_first_piece, after(up_second_piece, mids[1]))
        chunks = hidden_part // chunk
        up_sources = [
            (up_weight, (half, chunk), lambda i, place: (0, place[0] * chunks + i), None, 0)
        ]
        up_sources += [
            (piece, (quarter, chunk), lambda i, place: (0, i), (1, step), 0)
            for step, piece in enumerate(up_pieces)
        ]
        grad_mlps_side = [flip(value, 1) for value in grad_mlps]
        mids_side = [flip(value, 1) for value in mids]
        mids[1] = after(mids[1], grad_mlps_side)
    channels = jnp.einsum("rsc,rcg->rsg", selector_rows, group_rows, precision=highest)
    channels = lax.dynamic_slice_in_dim(
        jnp.repeat(tiled(channels), CHAN_GROUP, axis=2), row_at * hidden_part, hidden_part, 2
    )
    hidden_act, grad_pre, grad_own, out_own, low = feed(
        place,
        up_sources,
        mids,
        grad_mlps,
        channels,
        down_weight,
        chunk,
        tokens,
        low_rows,
    )

    if rows == 2:
        low = cross(low)
    else:
        low = low.reshape(rows, tokens, 2 * D)
        low = lax.psum_scatter(low, "fsdp", scatter_dimension=0, tiled=True)
        low = low.reshape(tokens, 2 * D)
        grad_own, out_own = jnp.zeros_like(grad_own), jnp.zeros_like(out_own)

    if fast:

        def columns_of(array, column=0, cols=None):
            return [(array, column, array.shape[1] if cols is None else cols)]

        act_side, pre_side = flip(hidden_act, 1), flip(grad_pre, 1)
        down_parts = term(
            place,
            [
                (
                    [columns_of(value) for value in (*grad_mlps, *grad_mlps_side)],
                    [columns_of(value) for value in (hidden_act, act_side)],
                )
            ],
            hidden_part,
        )
        grad_own = after(grad_own, down_parts)
        down_first = (flip(down_parts[0], 2), flip(down_parts[2], 4))

    grad_mid, own_pack, pack, grad_heads, block_out, mid_sums = mid_back(
        place,
        out_sources,
        grad_own,
        out_own,
        low,
        mid_state,
        attn_proj,
        tokens_here,
        *mods,
        head_slots,
        merged,
        normed_in,
    )
    if fast:

        crossed = cross(pack)
        own_side = flip(own_pack, 1)
        grad_heads = after(grad_heads, pack, own_side, pre_side, mids_side)
    grad_queries, *parts = attend_back(queries, kv_window, bias_t, grad_heads)
    if fast:
        parts[4], down_first = lax.optimization_barrier((parts[4], down_first))
    if paired:
        handed = flip(parts[4], 1)
        near_side = flip(parts[1], 1)
        zero = jnp.zeros((), bf16)
        down_part = parts[2] + jnp.where(core == 1, handed, zero)
        up_side = parts[3] + jnp.where(core == 0, handed, zero)
        from_above, from_below = shift(down_part, -2), shift(up_side, 2)
        arrivals = [near_side, from_above, from_below]
    else:
        arrivals = []
        for distance in range(1, reach + 1):
            arrivals += [
                shift(parts[2 * distance - 1], -distance),
                shift(parts[2 * distance], distance),
            ]
    if fast:
        q_crossed = cross(grad_queries)
        q_side = flip(grad_queries, 1)
        crossed_side = flip(crossed, 1)
        down_first, ignored = lax.optimization_barrier((down_first, (down_part, up_side)))

        def reduced(kept, arrived_part):
            value = (kept.astype(f32) + arrived_part.astype(f32)).astype(bf16)
            return value.reshape(2, value.shape[0] // 2, *value.shape[1:])

        def second_step(values):
            steps = []
            for value, bit in zip(values, (4, 2)):
                at = (seq_at // bit) % 2
                send = lax.dynamic_index_in_dim(value, 1 - at, 1, keepdims=False)
                keep_part = lax.dynamic_index_in_dim(value, at, 1, keepdims=False)
                steps.append((send, keep_part, bit))
            return steps

        def third_step(kept_parts, arrived_parts):
            value = jnp.concatenate(
                [
                    (kept_part.astype(f32) + arrived_part.astype(f32)).astype(bf16)
                    for kept_part, arrived_part in zip(kept_parts, arrived_parts)
                ],
                axis=1,
            )
            at = (seq_at // 8) % 2
            send = lax.dynamic_index_in_dim(value, 1 - at, 0, keepdims=False)
            return send, lax.dynamic_index_in_dim(value, at, 0, keepdims=False)

        down_values = [reduced(down_parts[1], down_first[0]), reduced(down_parts[3], down_first[1])]
        down_steps = second_step(down_values)
        down_second = [flip(send, bit) for send, ignored, bit in down_steps]
        up_parts = term(
            place,
            [
                (
                    [columns_of(value) for value in (grad_pre, pre_side)],
                    [columns_of(value) for value in (*mids, *mids_side)],
                ),
                (
                    [columns_of(value, D, D) for value in (own_pack, crossed, own_side, crossed_side)],
                    [
                        columns_of(value, 0, half)
                        for value in (own_pack, crossed, own_side, crossed_side)
                    ],
                ),
            ],
            half,
            5,
        )
        up_first = (flip(up_parts[0], 2), flip(up_parts[2], 4))
        arrivals[0] = after(arrivals[0], up_parts, q_side)
    grad_kv = parts[0].astype(f32)
    for arrival in arrivals:
        grad_kv = grad_kv + arrival.astype(f32)
    grad_kv = grad_kv.astype(bf16)
    if fast:
        grad_queries, down_second = lax.optimization_barrier((grad_queries, down_second))
    both_out, in_sums = in_back(
        place, qkv_sources, grad_queries, grad_kv, tokens_here, *mods, grad_mid, block_out
    )
    if fast:
        kv_crossed = cross(grad_kv)
        down_second = after(down_second, in_sums)
        down_send, down_keep = third_step([step[1] for step in down_steps], down_second)
        down_last = flip(down_send, 8)
        kv_crossed, in_sums = lax.optimization_barrier((kv_crossed, in_sums))
        up_first, grad_kv, q_crossed_late, ignored = lax.optimization_barrier(
            (up_first, grad_kv, q_crossed, kv_crossed)
        )

    def by_crop(sums):
        sums = sums.reshape(-1, repeats, slots, D)
        sums = jnp.sum(sums, axis=1) if repeats > 1 else sums[:, 0]
        return jnp.einsum("sc,nsd->cnd", selector, sums, precision=highest).astype(bf16)

    mod_grads = jnp.concatenate([in_sums, mid_sums], axis=0)
    if not fast:

        def product(acts, grads):
            return lax.dot_general(
                acts, grads, (((0,), (0,)), ((), ())), preferred_element_type=f32
            ).astype(bf16)

        def both(value):
            value = lax.psum_scatter(value, "fsdp", scatter_dimension=0, tiled=True)
            return lax.psum_scatter(value, "seq", scatter_dimension=1, tiled=True).astype(f32)

        grad_qkv = jnp.concatenate([grad_queries, grad_kv], axis=1)
        qkv_grad = both(product(normed_in, grad_qkv))
        out_grad = both(product(merged, own_pack[:, D:]))
        up_cols = lax.all_to_all(product(mids[0], grad_pre), "fsdp", 0, 1, tiled=True)
        up_grad = lax.psum_scatter(up_cols, "seq", scatter_dimension=1, tiled=True).astype(f32)
        down_cols = product(hidden_act, grad_mlps[0])
        down_grad = lax.psum_scatter(
            down_cols, "seq", scatter_dimension=1, tiled=True
        ).astype(f32)
    else:

        kv_side = flip(grad_kv, 1)
        kv_crossed_side, q_crossed_side = flip(kv_crossed, 1), flip(q_crossed_late, 1)

        def joined(first_part, second_part):
            return columns_of(first_part) + columns_of(second_part)

        up_steps = second_step([reduced(up_parts[1], up_first[0]), reduced(up_parts[3], up_first[1])])
        up_second = [flip(send, bit) for send, ignored, bit in up_steps]
        qkv_parts = term(
            place,
            [
                (
                    [
                        joined(grad_queries, grad_kv),
                        joined(q_crossed, kv_crossed),
                        joined(q_side, kv_side),
                        joined(q_crossed_side, kv_crossed_side),
                    ],
                    [
                        columns_of(value, half, half)
                        for value in (own_pack, crossed, own_side, crossed_side)
                    ],
                )
            ],
            half,
        )
        qkv_first = (flip(qkv_parts[0], 2), flip(qkv_parts[2], 4))
        qkv_steps = second_step(
            [reduced(qkv_parts[1], qkv_first[0]), reduced(qkv_parts[3], qkv_first[1])]
        )
        qkv_second = [flip(send, bit) for send, ignored, bit in qkv_steps]
        up_second, mod_grads, down_last, ignored = lax.optimization_barrier(
            (up_second, mod_grads, down_last, qkv_parts)
        )
        qkv_sends = [step[0] for step in qkv_steps]
        up_send, up_keep = third_step([step[1] for step in up_steps], up_second)
        qkv_send, qkv_keep = third_step([step[1] for step in qkv_steps], qkv_second)
        down_grad = jnp.transpose(down_keep.astype(f32) + down_last.astype(f32))
        up_last, ignored = lax.optimization_barrier((flip(up_send, 8), qkv_send))
        qkv_grad = jnp.transpose(qkv_keep.astype(f32) + flip(qkv_send, 8).astype(f32))
        mixed = up_keep.astype(f32) + up_last.astype(f32)
        up_rows, out_rows = hidden // seq, D // seq
        up_low, out_low = up_rows * 5 // 64 * 8, out_rows * 5 // 64 * 8
        parted = up_low + out_low
        rest = parted + up_rows - up_low
        up_mine = jnp.concatenate([mixed[:up_low], mixed[parted:rest]], axis=0).astype(bf16)
        out_grad = jnp.transpose(jnp.concatenate([mixed[up_low:parted], mixed[rest:]], axis=0))
        pairs = []
        for place_seq in range(seq):
            for place_row in range(2):
                high = (place_seq // 8) % 2
                target_seq = (place_seq & 7) | (place_row * 8)
                pairs.append((place_seq * 2 + place_row, target_seq * 2 + high))
        up_grad = jnp.transpose(lax.ppermute(up_mine, ("seq", "fsdp"), pairs)).astype(f32)
    mod_grads = by_crop(mod_grads).reshape(crops, 6 * D)
    if fast:
        share = columns // 2
        quarters = [mod_grads[:, i * share : (i + 1) * share] for i in range(4)]
        first_core = core == 0
        kept_sum = [jnp.where(first_core, quarters[i], quarters[i + 1]) for i in (0, 2)]
        sent_sum = [jnp.where(first_core, quarters[i + 1], quarters[i]) for i in (0, 2)]
        kept_sum, sent_sum = (jnp.stack(value) for value in (kept_sum, sent_sum))
        mod_grads = (kept_sum.astype(f32) + flip(sent_sum, 1).astype(f32)).astype(bf16)
        for bit, ahead in ((8, ()), (2, qkv_sends), (4, qkv_send)):
            mod_grads = (mod_grads.astype(f32) + flip(mod_grads, bit).astype(f32)).astype(bf16)
            mod_grads = after(mod_grads, ahead)
        own = pick(mod_grads[0], mod_grads[1])
        other = cross(pick(mod_grads[1], mod_grads[0]))
        own = jnp.concatenate([own, other], axis=0)
        other = flip(own, 1)
        mod_grads = jnp.concatenate(
            [jnp.where(first_core, own, other), jnp.where(first_core, other, own)], axis=1
        )
    else:
        mod_grads = lax.psum(mod_grads, "seq")
        split = jnp.transpose(mod_grads.reshape(crops, rows, columns), (1, 0, 2))
        mod_grads = lax.all_to_all(split, "fsdp", 0, 0).reshape(rows * crops, columns)
    ada_grad = outer(cond_rows, mod_grads)

    both_out = from_slots(both_out, f32, *(qkv_sends if fast else ()))
    block_out, input_grad = both_out[:, :D].astype(bf16), both_out[:, D:]
    return (
        block_out[None],
        input_grad[None],
        qkv_grad,
        out_grad,
        up_grad,
        down_grad,
        ada_grad,
    )


def solution(mesh):
    in_specs = (
        P("fsdp", "seq", None),
        P("fsdp", None, None),
        P("fsdp", None),
        P("fsdp", None),
        P("fsdp", None, None),
        P("fsdp", None, None),
        P("fsdp", "seq"),
        P("fsdp", None),
        P("fsdp", None),
        P("fsdp", None),
        P("fsdp", None),
        P(None, "fsdp"),
        P("fsdp", "seq", None),
    )
    out_specs = (
        P("fsdp", "seq", None),
        P("fsdp", "seq", None),
        P("fsdp", "seq"),
        P("fsdp", "seq"),
        P("fsdp", "seq"),
        P("fsdp", "seq"),
        P(None, "fsdp"),
    )
    return jax.shard_map(local, mesh=mesh, in_specs=in_specs, out_specs=out_specs, check_vma=False)
```

```python
import functools

import jax
import jax.numpy as jnp
import numpy as np
from jax import lax
from jax.experimental import pallas as pl
from jax.experimental.pallas import tpu as pltpu
from jax.sharding import PartitionSpec as P

D = 1152
H = 16
HD = 72
CHAN_GROUP = 128
PIECE_MAX = 16
PERIOD = 16

bf16 = jnp.bfloat16
f32 = jnp.float32
highest = lax.Precision.HIGHEST
norm_epsilon = 1e-06
masked_score = -1e30
score_scale = HD ** (-0.5)
VMEM_LIMIT = 56 * 1024 * 1024
VMEM_SPEC = pl.BlockSpec(memory_space=pltpu.VMEM)
COST = pl.CostEstimate(flops=1, transcendentals=0, bytes_accessed=1)


def params():
    return pltpu.CompilerParams(vmem_limit_bytes=VMEM_LIMIT)


def dot_nt(a, b):
    return lax.dot_general(a, b, (((1,), (1,)), ((), ())), preferred_element_type=f32)


def dot_nn(a, b):
    return lax.dot_general(a, b, (((1,), (0,)), ((), ())), preferred_element_type=f32)


def dot_tn(a, b):
    return lax.dot_general(a, b, (((0,), (0,)), ((), ())), preferred_element_type=f32)


def source_inputs(sources):
    arrays = [source[0] for source in sources]
    specs = [pl.BlockSpec(source[1], source[2]) for source in sources]
    parts = [(source[3], source[4]) for source in sources]
    return arrays, specs, parts


def fill(target_ref, place_ref, refs, parts):
    half = target_ref.shape[0] // 2
    mine = place_ref[0]
    for ref, (step, column) in zip(refs, parts):
        rows, cols = ref.shape
        if step == "all":
            start = 0
        elif step is None:
            start = pl.multiple_of(mine * half, 16)
        else:
            part = place_ref[step[0]] ^ step[1]
            start = pl.multiple_of((1 - mine) * half + part * rows, 16)
        target_ref[pl.ds(start, rows), pl.ds(column, cols)] = ref[...]


def whole(shape):
    return pl.BlockSpec(shape, lambda i, place: (0,) * len(shape))


def copies_in(target_ref, place_ref, refs, parts, sems):
    half = target_ref.shape[0] // 2
    mine = place_ref[0]
    copies = []
    for index, (ref, (source_column, cols, step, column)) in enumerate(zip(refs, parts)):
        rows = ref.shape[0]
        if step == "all":
            start = 0
        elif step is None:
            start = pl.multiple_of(mine * half, 16)
        else:
            part = place_ref[step[0]] ^ step[1]
            start = pl.multiple_of((1 - mine) * half + part * rows, 16)
        copies.append(
            (
                column,
                pltpu.make_async_copy(
                    ref.at[:, pl.ds(source_column, cols)],
                    target_ref.at[pl.ds(start, rows), pl.ds(column, cols)],
                    sems.at[index],
                ),
            )
        )
    return copies


def wait_for(copies, column):
    for at, copy in copies:
        if at == column:
            copy.wait()


def staged_call(kernel, place, sources, inputs, out_shapes, scratch, name):
    arrays = [source[0] for source in sources]
    parts = [source[1:] for source in sources]
    return pl.pallas_call(
        functools.partial(kernel, parts=parts),
        out_shape=out_shapes,
        grid_spec=pltpu.PrefetchScalarGridSpec(
            num_scalar_prefetch=1,
            grid=(1,),
            in_specs=[pl.BlockSpec(memory_space=pl.ANY)] * len(arrays)
            + [whole(value.shape) for value in inputs],
            out_specs=[whole(out.shape) for out in out_shapes],
            scratch_shapes=scratch + [pltpu.SemaphoreType.DMA((len(arrays),))],
        ),
        compiler_params=params(),
        cost_estimate=COST,
        name=name,
    )(place, *arrays, *inputs)


def shaped(*shape, dtype=f32):
    return jax.ShapeDtypeStruct(shape, dtype)


def normalized(values):
    centred = values - jnp.mean(values, axis=1, keepdims=True)
    inverse = lax.rsqrt(jnp.mean(centred * centred, axis=1, keepdims=True) + norm_epsilon)
    return centred * inverse, inverse


def normalized_back(grad, normed, inverse):
    mean_grad = jnp.mean(grad, axis=1, keepdims=True)
    mean_dot = jnp.mean(grad * normed, axis=1, keepdims=True)
    return (grad - mean_grad - normed * mean_dot) * inverse


def slot_rows(value):
    repeats = PERIOD // value.shape[0]
    return jnp.concatenate([value] * repeats, axis=0) if repeats > 1 else value


def mod_attn(place_ref, own_ref, other_ref, index):
    columns = pl.ds(index * D, D)
    return slot_rows(jnp.where(place_ref[6] == 0, own_ref[:, columns], other_ref[:, columns]))


def mod_mlp(place_ref, own_ref, other_ref, index):
    return mod_attn(place_ref, other_ref, own_ref, index)


def norm_in_kernel(place_ref, tokens_ref, own_ref, other_ref, out_ref, grad_ref):
    shift = mod_attn(place_ref, own_ref, other_ref, 0)
    scale = 1.0 + mod_attn(place_ref, own_ref, other_ref, 1)
    gate = mod_mlp(place_ref, own_ref, other_ref, 2)
    for start in range(0, tokens_ref.shape[0], PERIOD):
        rows = pl.ds(start, PERIOD)
        normed, ignored = normalized(tokens_ref[rows, pl.ds(0, D)].astype(f32))
        out_ref[rows, :] = (normed * scale + shift).astype(bf16)
        keep = tokens_ref[rows, pl.ds(2 * D, 128)].astype(f32)[:, :1]
        grad = tokens_ref[rows, pl.ds(D, D)].astype(f32)
        grad_ref[rows, :] = (grad * gate * keep).astype(bf16)


def norm_in(place, tokens, own, other):
    return pl.pallas_call(
        norm_in_kernel,
        out_shape=[shaped(tokens.shape[0], D, dtype=bf16)] * 2,
        in_specs=[pl.BlockSpec(memory_space=pltpu.SMEM)] + [VMEM_SPEC] * 3,
        out_specs=[VMEM_SPEC] * 2,
        compiler_params=params(),
        cost_estimate=COST,
        name="norm_in",
    )(place, tokens, own, other)


def project_kernel(place_ref, *refs, parts):
    count = len(parts)
    q_ref, kv_ref, weight_ref, window_ref, sems = refs[-5:]
    window_parts = refs[count:-5]
    copies = copies_in(weight_ref, place_ref, refs[:count], parts, sems)
    for column in (D, 2 * D, 0):
        for at, copy in copies:
            if at == column:
                copy.start()
    tokens = q_ref.shape[0]
    for index, part in enumerate(window_parts):
        window_ref[pl.ds(index * tokens, tokens), :] = part[...]
    for column in (D, 2 * D):
        wait_for(copies, column)
        for start in range(0, D, 384):
            kv_ref[:, pl.ds(column - D + start, 384)] = dot_nn(
                window_ref[...], weight_ref[:, pl.ds(column + start, 384)]
            ).astype(bf16)
    wait_for(copies, 0)
    for start in range(0, D, 384):
        q_ref[:, pl.ds(start, 384)] = dot_nn(
            window_parts[0][...], weight_ref[:, pl.ds(start, 384)]
        ).astype(bf16)


def project(place, sources, window_parts):
    tokens = window_parts[0].shape[0]
    keys = tokens * len(window_parts)
    return staged_call(
        project_kernel,
        place,
        sources,
        window_parts,
        [shaped(tokens, D, dtype=bf16), shaped(keys, 2 * D, dtype=bf16)],
        [pltpu.VMEM((D, 3 * D), bf16), pltpu.VMEM((keys, D), bf16)],
        "project",
    )


def head_window(head):
    start = head * HD
    low = start // 128 * 128
    width = 128 if start + HD - low <= 128 else 256
    return low, min(width, D - low), start - low


HEAD_GROUPS = ((0, 1), (2, 3), (4, 5), (6, 7), (8,), (9, 10), (11, 12), (13, 14), (15,))


def group_window(heads):
    windows = [head_window(head) for head in heads]
    return windows[0][0], max(window[1] for window in windows), [window[2] for window in windows]


def masked_rows(value, lanes):
    zero = jnp.zeros((), value.dtype)
    parts = [jnp.where(lane, value, zero) for lane in lanes]
    return jnp.concatenate(parts, axis=0) if len(parts) > 1 else parts[0]


def head_lanes(rows, width, first):
    lane = lax.broadcasted_iota(jnp.int32, (rows, width), 1)
    return (lane >= first) & (lane < first + HD)


def attend_kernel(place_ref, *refs, parts):
    count = len(parts)
    q_ref, kv_ref, bias_ref, mask_ref, tokens_ref, own_ref, other_ref = refs[count : count + 7]
    merged_ref, proj_ref, mid_ref, normed_ref, acc_ref, weight_ref, sems = refs[count + 7 :]
    gate = mod_attn(place_ref, own_ref, other_ref, 2)
    shift = mod_mlp(place_ref, own_ref, other_ref, 0)
    scale = 1.0 + mod_mlp(place_ref, own_ref, other_ref, 1)
    tokens = q_ref.shape[0]
    copies = copies_in(weight_ref, place_ref, refs[:count], parts, sems)
    for ignored, copy in copies:
        copy.start()
    acc_ref[...] = jnp.zeros_like(acc_ref)
    for heads in HEAD_GROUPS:
        low, width, firsts = group_window(heads)
        window = pl.ds(low, width)
        lanes = [head_lanes(tokens, width, first) for first in firsts]
        bias = jnp.concatenate([bias_ref[...]] * len(heads), axis=0)
        query = masked_rows(q_ref[:, window], lanes)
        scores = dot_nt(query, kv_ref[:, window]) * score_scale + bias
        top = jnp.max(scores, axis=1, keepdims=True)
        weights = jnp.exp(scores - top)
        probs = (weights * (1.0 / jnp.sum(weights, axis=1, keepdims=True))).astype(bf16)
        out = dot_nn(probs, kv_ref[:, pl.ds(D + low, width)])
        value = acc_ref[:, window]
        for index, lane in enumerate(lanes):
            value = value + jnp.where(lane, out[index * tokens : (index + 1) * tokens], 0.0)
        acc_ref[:, window] = value
    for start in range(0, tokens, PERIOD):
        rows = pl.ds(start, PERIOD)
        merged_ref[rows, :] = (acc_ref[rows, :] * mask_ref[...]).astype(bf16)
    wait_for(copies, 0)
    proj_ref[...] = dot_nn(merged_ref[...], weight_ref[...])
    for start in range(0, tokens, PERIOD):
        rows = pl.ds(start, PERIOD)
        mid = tokens_ref[rows, pl.ds(0, D)].astype(f32) + gate * proj_ref[rows, :]
        mid_ref[rows, :] = mid
        normed, ignored = normalized(mid)
        normed_ref[rows, :] = (normed * scale + shift).astype(bf16)


def attend(place, sources, *inputs):
    tokens = inputs[0].shape[0]
    return staged_call(
        attend_kernel,
        place,
        sources,
        inputs,
        [
            shaped(tokens, D, dtype=bf16),
            shaped(tokens, D),
            shaped(tokens, D),
            shaped(tokens, D, dtype=bf16),
        ],
        [pltpu.VMEM((tokens, D), f32), pltpu.VMEM((D, D), bf16)],
        "attend",
    )


def attend_back_kernel(
    q_ref, kv_ref, bias_ref, grad_ref, dq_ref, *refs
):
    tokens = q_ref.shape[0]
    dkv_refs, (dq_acc, dk_acc, dv_acc) = refs[:-3], refs[-3:]
    dq_acc[...] = jnp.zeros_like(dq_acc)
    dk_acc[...] = jnp.zeros_like(dk_acc)
    dv_acc[...] = jnp.zeros_like(dv_acc)
    for heads in HEAD_GROUPS:
        low, width, firsts = group_window(heads)
        window = pl.ds(low, width)
        lanes = [head_lanes(tokens, width, first) for first in firsts]
        bias = jnp.concatenate([bias_ref[...]] * len(heads), axis=1)
        query = masked_rows(q_ref[:, window], lanes)
        grad = masked_rows(grad_ref[:, window], lanes)
        keys = kv_ref[:, window]
        scores = dot_nt(keys, query) * score_scale + bias
        top = jnp.max(scores, axis=0, keepdims=True)
        weights = jnp.exp(scores - top)
        probs = weights * (1.0 / jnp.sum(weights, axis=0, keepdims=True))
        probs_low = probs.astype(bf16)
        grad_probs = dot_nt(kv_ref[:, pl.ds(D + low, width)], grad)
        row_dot = jnp.sum(probs_low.astype(f32) * grad_probs, axis=0, keepdims=True)
        grad_scores = (probs * (grad_probs - row_dot)).astype(bf16)
        dk_acc[:, window] += dot_nn(grad_scores, query)
        dv_acc[:, window] += dot_nn(probs_low, grad)
        back = dot_tn(grad_scores, keys)
        value = dq_acc[:, window]
        for index, lane in enumerate(lanes):
            value = value + jnp.where(lane, back[index * tokens : (index + 1) * tokens], 0.0)
        dq_acc[:, window] = value
    dq_ref[...] = (dq_acc[...] * score_scale).astype(bf16)
    for index, dkv_ref in enumerate(dkv_refs):
        rows = pl.ds(index * tokens, tokens)
        dkv_ref[:, pl.ds(0, D)] = (dk_acc[rows, :] * score_scale).astype(bf16)
        dkv_ref[:, pl.ds(D, D)] = dv_acc[rows, :].astype(bf16)


def attend_back(queries, kv_window, bias_t, grad_heads):
    tokens = queries.shape[0]
    keys = kv_window.shape[0]
    outs = [shaped(tokens, D, dtype=bf16)]
    outs += [shaped(tokens, 2 * D, dtype=bf16)] * (keys // tokens)
    return pl.pallas_call(
        attend_back_kernel,
        out_shape=outs,
        in_specs=[VMEM_SPEC] * 4,
        out_specs=[VMEM_SPEC] * len(outs),
        scratch_shapes=[
            pltpu.VMEM((tokens, D), f32),
            pltpu.VMEM((keys, D), f32),
            pltpu.VMEM((keys, D), f32),
        ],
        compiler_params=params(),
        cost_estimate=COST,
        name="attend_back",
    )(queries, kv_window, bias_t, grad_heads)


def feed_kernel(place_ref, *refs, parts, arrays):
    count = len(parts)
    mid_refs, grad_refs = refs[count : count + arrays], refs[count + arrays : count + 2 * arrays]
    channel_ref, down_ref = refs[count + 2 * arrays : count + 2 * arrays + 2]
    act_ref, pre_ref, grad_own, out_own, low_ref = refs[-12:-7]
    weight_ref, grad_acc, out_acc, mid_all, grad_all, pre_acc, back_acc = refs[-7:]
    own_rows = grad_own.shape[0]
    step, steps = pl.program_id(0), pl.num_programs(0)
    rows, cols = act_ref.shape
    groups = channel_ref.shape[0]
    tokens = rows // groups

    @pl.when(step == 0)
    def _():
        grad_acc[...] = jnp.zeros_like(grad_acc)
        out_acc[...] = jnp.zeros_like(out_acc)
        share = rows // arrays
        for index in range(arrays):
            part = pl.ds(index * share, share)
            mid_all[part, :] = mid_refs[index][...]
            grad_all[part, :] = grad_refs[index][...]

    fill(weight_ref, place_ref, refs[:count], parts)
    root = 0.7978845608028654
    pre_acc[...] = dot_nn(mid_all[...], weight_ref[...])
    blocks = [(g, t) for g in range(groups) for t in range(0, tokens, PERIOD)]
    for group, start in blocks:
        span = pl.ds(group * tokens + start, PERIOD)
        channels = channel_ref[group]
        pre = pre_acc[span, :]
        square = pre * pre
        inner = jnp.tanh(root * (pre + 0.044715 * (square * pre)))
        half_sum = 0.5 + 0.5 * inner
        act_ref[span, :] = (pre * half_sum * channels).astype(bf16)
        slope = half_sum + (0.5 * pre) * (1.0 - inner * inner) * (
            root + (3.0 * 0.044715 * root) * square
        )
        pre_acc[span, :] = channels * slope
    back_acc[...] = dot_nt(grad_all[...], down_ref[...])
    out_acc[...] += dot_nn(act_ref[...], down_ref[...])
    for group, start in blocks:
        span = pl.ds(group * tokens + start, PERIOD)
        pre_ref[span, :] = (back_acc[span, :] * pre_acc[span, :]).astype(bf16)
    grad_acc[...] += dot_nt(pre_ref[...], weight_ref[...])

    @pl.when(step == steps - 1)
    def _():
        skip = rows - low_ref.shape[0]
        grad_own[...] = grad_acc[pl.ds(0, own_rows), :]
        out_own[...] = out_acc[pl.ds(0, own_rows), :]
        low_ref[:, pl.ds(0, D)] = grad_acc[pl.ds(skip, rows - skip), :].astype(bf16)
        low_ref[:, pl.ds(D, D)] = out_acc[pl.ds(skip, rows - skip), :].astype(bf16)


def feed(place, sources, mids, grads, channels, down, chunk, tokens, low_rows):
    arrays, specs, parts = source_inputs(sources)
    rows = sum(mid.shape[0] for mid in mids)
    width = down.shape[0]
    by_chunk = pl.BlockSpec((rows, chunk), lambda i, place: (0, i))
    own, low = (tokens, D), (low_rows, 2 * D)
    return pl.pallas_call(
        functools.partial(feed_kernel, parts=parts, arrays=len(mids)),
        out_shape=[
            shaped(rows, width, dtype=bf16),
            shaped(rows, width, dtype=bf16),
            shaped(*own),
            shaped(*own),
            shaped(*low, dtype=bf16),
        ],
        grid_spec=pltpu.PrefetchScalarGridSpec(
            num_scalar_prefetch=1,
            grid=(width // chunk,),
            in_specs=specs
            + [whole(value.shape) for value in (*mids, *grads)]
            + [
                pl.BlockSpec(
                    (channels.shape[0], PERIOD, chunk), lambda i, place: (0, 0, i)
                ),
                pl.BlockSpec((chunk, D), lambda i, place: (i, 0)),
            ],
            out_specs=[by_chunk, by_chunk, whole(own), whole(own), whole(low)],
            scratch_shapes=[
                pltpu.VMEM((D, chunk), bf16),
                pltpu.VMEM((rows, D), f32),
                pltpu.VMEM((rows, D), f32),
                pltpu.VMEM((rows, D), bf16),
                pltpu.VMEM((rows, D), bf16),
                pltpu.VMEM((rows, chunk), f32),
                pltpu.VMEM((rows, chunk), f32),
            ],
        ),
        compiler_params=params(),
        cost_estimate=COST,
        name="feed",
    )(place, *arrays, *mids, *grads, channels, down)


def mid_back_kernel(place_ref, *refs, parts):
    count = len(parts)
    own_ref, out_ref, other_ref, mid_ref, proj_ref, late_ref = refs[count : count + 6]
    mod_own, mod_other, mask_ref, attn_ref, normed_ref = refs[count + 6 : count + 11]
    grad_mid_ref, own_pack_ref, pack_ref, heads_ref, block_ref, sums_ref = refs[
        count + 11 : count + 17
    ]
    weight_ref, merged_ref, sems = refs[count + 17 :]
    copies = copies_in(weight_ref, place_ref, refs[:count], parts, sems)
    for ignored, copy in copies:
        copy.start()
    scale = 1.0 + mod_mlp(place_ref, mod_own, mod_other, 1)
    gate = mod_attn(place_ref, mod_own, mod_other, 2)
    out_gate = mod_mlp(place_ref, mod_own, mod_other, 2)
    first = place_ref[0] == 0
    half = D // 2
    for index, ref in enumerate((attn_ref, normed_ref)):
        low, high = ref[:, pl.ds(0, half)], ref[:, pl.ds(half, half)]
        own_pack_ref[:, pl.ds(index * half, half)] = jnp.where(first, low, high)
        pack_ref[:, pl.ds(index * half, half)] = jnp.where(first, high, low)
    tokens = own_ref.shape[0]
    sums = [jnp.zeros((PERIOD, D), f32) for ignored in range(4)]
    for start in range(0, tokens, PERIOD):
        rows = pl.ds(start, PERIOD)
        normed, inverse = normalized(mid_ref[rows, :])
        grad = own_ref[rows, :] + other_ref[rows, pl.ds(0, D)].astype(f32)
        grad_out = late_ref[rows, pl.ds(D, D)].astype(f32)
        grad_mid = grad_out + normalized_back(grad * scale, normed, inverse)
        grad_mid_ref[rows, :] = grad_mid
        grad_attn = (grad_mid * gate).astype(bf16)
        own_pack_ref[rows, pl.ds(D, D)] = grad_attn
        pack_ref[rows, pl.ds(D, D)] = grad_attn
        out = out_ref[rows, :] + other_ref[rows, pl.ds(D, D)].astype(f32)
        out = out * late_ref[rows, pl.ds(2 * D, 128)].astype(f32)[:, :1]
        block_ref[rows, :] = (mid_ref[rows, :] + out_gate * out).astype(bf16)
        for index, value in enumerate(
            (grad_mid * proj_ref[rows, :], grad, grad * normed, grad_out * out)
        ):
            sums[index] += value
    for index in range(4):
        sums_ref[index] = sums[index]
    wait_for(copies, 0)
    merged_ref[...] = dot_nt(pack_ref[:, pl.ds(D, D)], weight_ref[...])
    for start in range(0, tokens, PERIOD):
        rows = pl.ds(start, PERIOD)
        heads_ref[rows, :] = (merged_ref[rows, :] * mask_ref[...]).astype(bf16)


def mid_back(place, sources, *inputs):
    tokens = inputs[0].shape[0]
    return staged_call(
        mid_back_kernel,
        place,
        sources,
        inputs,
        [
            shaped(tokens, D),
            shaped(tokens, 2 * D, dtype=bf16),
            shaped(tokens, 2 * D, dtype=bf16),
            shaped(tokens, D, dtype=bf16),
            shaped(tokens, D, dtype=bf16),
            shaped(4, PERIOD, D),
        ],
        [pltpu.VMEM((D, D), bf16), pltpu.VMEM((tokens, D), f32)],
        "mid_back",
    )


def in_back_kernel(place_ref, *refs, parts):
    count = len(parts)
    dq_ref, dkv_ref, tokens_ref, mod_own, mod_other = refs[count : count + 5]
    grad_mid_ref, block_ref = refs[count + 5 : count + 7]
    both_ref, sums_ref, weight_ref, grad_ref, normed_ref, inverse_ref, sems = refs[count + 7 :]
    tokens = dq_ref.shape[0]
    copies = copies_in(weight_ref, place_ref, refs[:count], parts, sems)
    for column in (D, 2 * D, 0):
        for at, copy in copies:
            if at == column:
                copy.start()
    both_ref[:, pl.ds(0, D)] = block_ref[...]
    for start in range(0, tokens, PERIOD):
        rows = pl.ds(start, PERIOD)
        normed, inverse = normalized(tokens_ref[rows, pl.ds(0, D)].astype(f32))
        normed_ref[rows, :] = normed
        inverse_ref[rows, :] = jnp.broadcast_to(inverse, (PERIOD, 128))
    wait_for(copies, D)
    grad_ref[...] = dot_nt(dkv_ref[:, pl.ds(0, D)], weight_ref[:, pl.ds(D, D)])
    wait_for(copies, 2 * D)
    grad_ref[...] += dot_nt(dkv_ref[:, pl.ds(D, D)], weight_ref[:, pl.ds(2 * D, D)])
    wait_for(copies, 0)
    grad_ref[...] += dot_nt(dq_ref[...], weight_ref[:, pl.ds(0, D)])
    scale = 1.0 + mod_attn(place_ref, mod_own, mod_other, 1)
    shift_sum = jnp.zeros((PERIOD, D), f32)
    scale_sum = jnp.zeros((PERIOD, D), f32)
    for start in range(0, tokens, PERIOD):
        rows = pl.ds(start, PERIOD)
        normed, inverse = normed_ref[rows, :], inverse_ref[rows, :][:, :1]
        grad = grad_ref[rows, :]
        back = normalized_back(grad * scale, normed, inverse)
        both_ref[rows, pl.ds(D, D)] = (grad_mid_ref[rows, :] + back).astype(bf16)
        shift_sum += grad
        scale_sum += grad * normed
    sums_ref[0] = shift_sum
    sums_ref[1] = scale_sum


def in_back(place, sources, *inputs):
    tokens = inputs[0].shape[0]
    return staged_call(
        in_back_kernel,
        place,
        sources,
        inputs,
        [shaped(tokens, 2 * D, dtype=bf16), shaped(2, PERIOD, D)],
        [
            pltpu.VMEM((D, 3 * D), bf16),
            pltpu.VMEM((tokens, D), f32),
            pltpu.VMEM((tokens, D), f32),
            pltpu.VMEM((tokens, 128), f32),
        ],
        "in_back",
    )


def term_kernel(place_ref, *refs, layout, outputs):
    joined = refs[-3 * len(layout) :]
    place_at = {0: place_ref[3], 1: place_ref[4]}
    core = place_ref[2]
    first_out = len(refs) - 3 * len(layout) - 2 * outputs
    for index, (pieces, chunk, plan) in enumerate(layout):
        grads_ref, acts_ref, acc_ref = joined[3 * index : 3 * index + 3]
        for target, ref_at, column, cols, row_to, col_to in pieces:
            value = refs[ref_at][:, pl.ds(column, cols)]
            into = grads_ref if target == 0 else acts_ref
            into[pl.ds(row_to, value.shape[0]), pl.ds(col_to, cols)] = value
        width = acts_ref.shape[1]
        acc_ref[...] = dot_tn(grads_ref[...], acts_ref[...])
        for out_index, (first, count, into_row, axis) in enumerate(plan):
            at = place_at[axis]
            for side_at, side in ((0, 1 - at), (1, at)):
                out_ref = refs[first_out + 2 * out_index + side_at]
                blocks, lanes = out_ref.shape[0], out_ref.shape[2]
                lane_blocks = width // lanes
                for block in range(blocks):
                    lane, rest = divmod(block, blocks // lane_blocks)
                    if axis == 0:
                        line = rest * 4 + side * 2 + core
                    else:
                        line = (rest // 2) * 8 + side * 4 + (rest % 2) * 2 + core
                    start = pl.multiple_of(line * chunk + first, 8)
                    out_ref[block, pl.ds(into_row, count), :] = acc_ref[
                        pl.ds(start, count), pl.ds(lane * lanes, lanes)
                    ].astype(bf16)


def term(place, weights, width, eighths=4):
    arrays, layout, scratch, rows_out = [], [], [], [0, 0]
    for grads, acts in weights:
        pieces, shapes = [], []
        for target, value in ((0, grads), (1, acts)):
            row_to = 0
            for group in value:
                col_to = 0
                for array, column, cols in group:
                    pieces.append((target, len(arrays), column, cols, row_to, col_to))
                    arrays.append(array)
                    col_to += cols
                row_to += group[0][0].shape[0]
            shapes.append((row_to, col_to))
        (depth, columns), (_, rows) = shapes
        chunk = columns // (16 * width // rows)
        first = chunk * eighths // 64 * 8
        plan = [(0, first, rows_out[0], 0), (first, chunk - first, rows_out[1], 1)]
        rows_out = [rows_out[0] + first, rows_out[1] + chunk - first]
        layout.append((pieces, chunk, plan))
        scratch += [
            pltpu.VMEM((depth, columns), bf16),
            pltpu.VMEM((depth, rows), bf16),
            pltpu.VMEM((columns, rows), f32),
        ]
    outs = [shaped(4, rows_out[axis], width, dtype=bf16) for axis in (0, 0, 1, 1)]
    return pl.pallas_call(
        functools.partial(term_kernel, layout=layout, outputs=2),
        out_shape=outs,
        in_specs=[pl.BlockSpec(memory_space=pltpu.SMEM)] + [VMEM_SPEC] * len(arrays),
        out_specs=[VMEM_SPEC] * len(outs),
        scratch_shapes=scratch,
        compiler_params=params(),
        cost_estimate=COST,
        name="term",
    )(place, *arrays)


def outer_kernel(left_ref, right_ref, out_ref, value_ref, sems):
    copies = []
    for index in range(value_ref.shape[0] // 128):
        rows = pl.ds(index * 128, 128)
        value_ref[rows, :] = dot_tn(left_ref[:, rows], right_ref[...])
        copies.append(
            pltpu.make_async_copy(value_ref.at[rows, :], out_ref.at[rows, :], sems.at[index])
        )
        copies[-1].start()
    for copy in copies:
        copy.wait()


def outer(left, right):
    depth, rows = left.shape
    columns = right.shape[1]
    return pl.pallas_call(
        outer_kernel,
        out_shape=shaped(rows, columns),
        in_specs=[VMEM_SPEC] * 2,
        out_specs=pl.BlockSpec(memory_space=pl.ANY),
        scratch_shapes=[
            pltpu.VMEM((rows, columns), f32),
            pltpu.SemaphoreType.DMA((rows // 128,)),
        ],
        compiler_params=params(),
        cost_estimate=COST,
        name="outer",
    )(left, right)


def running_ends(pieces):
    index = jnp.arange(pieces.shape[0], dtype=jnp.int32)
    return jnp.sum(jnp.where(index[None, :] <= index[:, None], pieces[None, :], 0), axis=1)


def crop_of(slots, ends):
    return jnp.sum((slots[..., None] >= ends[:-1]).astype(jnp.int32), axis=-1)


def one_hot(crops, count):
    return (crops[..., None] == jnp.arange(count, dtype=jnp.int32)).astype(f32)


def block_order(size):
    def device(block):
        chip, core = block // 2, block % 2
        return 2 * (chip ^ ((chip >> 1) & 1)) + core if size % 8 == 0 else block

    return [device(block) for block in range(size)]


def local(
    tokens_in,
    condition,
    crop_pieces,
    pad_counts,
    head_mask,
    channel_mask,
    keep_mask,
    qkv_weight,
    out_weight,
    up_weight,
    down_weight,
    ada_weight,
    cotangent,
):
    seq = lax.axis_size("seq")
    rows = lax.axis_size("fsdp")
    tokens = tokens_in.shape[1]
    slots = tokens // seq
    repeats = PERIOD // slots
    crops = crop_pieces.shape[1]
    hidden = up_weight.shape[1]
    hidden_part = hidden // rows
    half = D // rows
    seq_at = lax.axis_index("seq")
    row_at = lax.axis_index("fsdp")
    fast = rows == 2 and seq == 16
    order = block_order(seq)
    core = seq_at % 2
    if seq % 8 == 0:
        chip = seq_at // 2
        block_at = 2 * (chip ^ ((chip >> 1) & 1)) + core
    else:
        block_at = seq_at
    place = jnp.stack(
        [
            row_at,
            seq_at & 3,
            core,
            (seq_at // 2) % 2,
            (seq_at // 4) % 2,
            (seq_at // 4) % 2 * 2 + core,
            row_at if fast else jnp.zeros_like(row_at),
            (seq_at // 8) % 2,
        ]
    ).astype(jnp.int32)

    def flip(value, bit):
        return lax.ppermute(value, "seq", [(i, i ^ bit) for i in range(seq)])

    def cross(value):
        return lax.ppermute(value, "fsdp", [(0, 1), (1, 0)])

    def shift(value, distance):
        pairs = [
            (order[b], order[b + distance]) for b in range(seq) if 0 <= b + distance < seq
        ]
        return lax.ppermute(value, "seq", pairs)

    swap_rows = jnp.asarray(
        np.kron(np.eye(seq)[np.array(order)], np.eye(slots)), bf16
    )

    def to_slots(value):
        moved = jnp.dot(swap_rows, value, preferred_element_type=f32).astype(bf16)
        moved = lax.all_to_all(moved.reshape(seq, slots, -1), "seq", 0, 0)
        return moved.reshape(tokens, -1)

    def from_slots(value, dtype, *earlier):
        value = lax.all_to_all(value.reshape(seq, slots, -1), "seq", 0, 0)
        value = after(value, *earlier) if earlier else value
        value = value.reshape(tokens, -1)
        return jnp.dot(swap_rows, value, preferred_element_type=f32).astype(dtype)

    def after(value, *earlier):
        return lax.optimization_barrier((value, *earlier))[0]

    def fetch_first(slices, bit, *earlier):
        count = 2 if bit is None else 4
        part = core if bit is None else (seq_at // bit) % 2 * 2 + core
        row = after(part * (half // count), *earlier)
        parts = [
            lax.dynamic_slice(weight, (row, column), (half // count, cols))
            for weight, column, cols in slices
        ]
        return cross(jnp.concatenate(parts, axis=1) if len(parts) > 1 else parts[0])

    def gather_rows(value):
        if rows == 2:
            return jnp.stack([value, cross(value)])
        return lax.all_gather(value, "fsdp", axis=0)

    def pick(low_part, high_part):
        return jnp.where(row_at == 0, low_part, high_part)

    def tiled(value):
        return jnp.concatenate([value] * repeats, axis=-2) if repeats > 1 else value

    slot_index = block_at * slots + jnp.arange(slots, dtype=jnp.int32)
    ends = running_ends(crop_pieces[0])
    crop_here = crop_of(slot_index, ends)
    selector = one_hot(crop_here, crops)
    pads = pad_counts[0]

    cond_act = jax.nn.silu(condition[0]).astype(bf16)
    extra = jnp.concatenate(
        [channel_mask[0].astype(bf16), crop_pieces[0].astype(bf16)[:, None]], axis=1
    )
    extra = jnp.pad(extra, ((0, 0), (0, 128 - extra.shape[1])))
    packed = gather_rows(jnp.concatenate([cond_act, extra], axis=1))
    groups = channel_mask.shape[2]
    cond_rows = packed[:, :, :D].reshape(rows * crops, D)
    group_rows = packed[:, :, D : D + groups].astype(f32)
    ends_rows = jax.vmap(running_ends)(packed[:, :, D + groups].astype(jnp.int32))
    selector_rows = jax.vmap(lambda own: one_hot(crop_of(slot_index, own), crops))(ends_rows)

    columns = ada_weight.shape[1]
    quarter = half // 4
    if fast:
        k_first = fetch_first([(qkv_weight, D, D), (out_weight, 0, D)], 2, seq_at)
        k_second = flip(k_first, 2)
    mod_rows = jnp.dot(cond_rows, ada_weight, preferred_element_type=f32)
    mod_rows = mod_rows.reshape(rows, crops, columns)
    if rows == 2:
        mod_slots = jnp.einsum("rsc,rcm->rsm", selector_rows, mod_rows, precision=highest)
        if fast:
            mod_slots = after(mod_slots, k_first)
        arrived = cross(mod_slots[1])
        mods = (mod_slots[0], arrived)
    else:
        mine = lax.all_to_all(mod_rows, "fsdp", 0, 0)
        mine = jnp.transpose(mine, (1, 0, 2)).reshape(crops, rows * columns)
        mine = jnp.dot(selector, mine, precision=highest)
        mods = (mine[:, : 3 * D], mine[:, 3 * D :])

    kept = jnp.broadcast_to(keep_mask[0].astype(bf16)[:, None], (tokens, 128))
    tokens_here = to_slots(jnp.concatenate([tokens_in[0], cotangent[0], kept], axis=1))
    def block(at):
        return lambda i, place: (0, at)

    if fast:
        chunk = 768

        def spread(first, second):
            return (first, flip(first, 1), second, flip(second, 1))

        other_part = (1 - row_at) * hidden_part
        v_first = fetch_first([(qkv_weight, 2 * D, D)], 4, mod_slots)
        q_first = fetch_first([(qkv_weight, 0, D)], None, arrived)
        tokens_here = after(tokens_here, k_second)
        normed_in, grad_mlp = norm_in(place, tokens_here, *mods)
        up_first_piece = fetch_first(
            [(up_weight, other_part, hidden_part)], 2, q_first, normed_in
        )
        v_second = flip(v_first, 4)
        k_pieces, v_pieces = spread(k_first, k_second), spread(v_first, v_second)
        q_pieces = (q_first, flip(q_first, 1))
        qkv_sources = [(qkv_weight, column, D, None, column) for column in (0, D, 2 * D)]
        for at, column, pieces in ((2, 0, q_pieces), (1, D, k_pieces), (5, 2 * D, v_pieces)):
            qkv_sources += [
                (piece, 0, D, (at, step), column) for step, piece in enumerate(pieces)
            ]
        out_sources = [(out_weight, 0, D, None, 0)]
        out_sources += [(piece, D, D, (1, step), 0) for step, piece in enumerate(k_pieces)]
        low_rows = tokens
    else:
        chunk = hidden_part
        qkv_full = lax.all_gather(qkv_weight, "fsdp", axis=0, tiled=True)
        out_full = lax.all_gather(out_weight, "fsdp", axis=0, tiled=True)
        up_part = lax.all_to_all(up_weight, "fsdp", 1, 0, tiled=True)
        qkv_sources = [(qkv_full, column, D, "all", column) for column in (0, D, 2 * D)]
        out_sources = [(out_full, 0, D, "all", 0)]
        up_sources = [(up_part, (D, hidden_part), block(0), "all", 0)]
        low_rows = rows * tokens

    if not fast:
        normed_in, grad_mlp = norm_in(place, tokens_here, *mods)

    reach = -(-(PIECE_MAX - 1) // slots)
    paired = reach == 2 and seq % 2 == 0
    if paired:
        below, above = shift(normed_in, 2), shift(normed_in, -2)
        if fast:
            above = after(above, v_second, q_first)
        passed = flip(jnp.where(core == 0, above, below), 1)
        near = [normed_in, flip(normed_in, 1), below, above, passed]
        near_at = [
            block_at,
            block_at ^ 1,
            block_at - 2,
            block_at + 2,
            block_at - 1 + 2 * core,
        ]
    else:
        near, near_at = [normed_in], [block_at]
        for distance in range(1, reach + 1):
            near += [shift(normed_in, distance), shift(normed_in, -distance)]
            near_at += [block_at - distance, block_at + distance]
    near_at = after(jnp.stack(near_at), normed_in)
    key_slots = near_at[:, None] * slots + jnp.arange(slots, dtype=jnp.int32)[None, :]
    inside = (near_at >= 0) & (near_at < seq)
    key_crop = jnp.where(inside[:, None], crop_of(key_slots, ends), -1)
    key_crop = jnp.where(
        key_slots[:, None, :] < tokens - pads[None, :, None], key_crop[:, None, :], -1
    ).reshape(-1)
    query_crop = jnp.broadcast_to(crop_here[None, :], (seq, slots)).reshape(tokens)
    bias = jnp.where(query_crop[:, None] == key_crop[None, :], 0.0, masked_score).astype(f32)
    bias_t = jnp.where(key_crop[:, None] == query_crop[None, :], 0.0, masked_score).astype(f32)
    head_slots = tiled(
        jnp.repeat(jnp.dot(selector, head_mask[0].astype(f32), precision=highest), HD, axis=1)
    )

    def row_list(value):
        if rows == 2:
            return [value, cross(value)]
        return [lax.all_gather(value, "fsdp", axis=0, tiled=True)]

    grad_mlps = row_list(grad_mlp)
    if fast:
        near[-1] = after(near[-1], grad_mlps[1])
    queries, kv_window = project(place, qkv_sources, near)
    if fast:
        up_second_piece = flip(after(up_first_piece, queries), 2)

    merged, attn_proj, mid_state, normed_mid = attend(
        place,
        out_sources,
        queries,
        kv_window,
        bias,
        head_slots,
        tokens_here,
        *mods,
    )

    mids = row_list(normed_mid)
    if fast:
        up_pieces = spread(up_first_piece, after(up_second_piece, mids[1]))
        chunks = hidden_part // chunk
        up_sources = [
            (up_weight, (half, chunk), lambda i, place: (0, place[0] * chunks + i), None, 0)
        ]
        up_sources += [
            (piece, (quarter, chunk), lambda i, place: (0, i), (1, step), 0)
            for step, piece in enumerate(up_pieces)
        ]
        grad_mlps_side = [flip(value, 1) for value in grad_mlps]
        mids_side = [flip(value, 1) for value in mids]
        mids[1] = after(mids[1], grad_mlps_side)
    channels = jnp.einsum("rsc,rcg->rsg", selector_rows, group_rows, precision=highest)
    channels = lax.dynamic_slice_in_dim(
        jnp.repeat(tiled(channels), CHAN_GROUP, axis=2), row_at * hidden_part, hidden_part, 2
    )
    hidden_act, grad_pre, grad_own, out_own, low = feed(
        place,
        up_sources,
        mids,
        grad_mlps,
        channels,
        down_weight,
        chunk,
        tokens,
        low_rows,
    )

    if rows == 2:
        low = cross(low)
    else:
        low = low.reshape(rows, tokens, 2 * D)
        low = lax.psum_scatter(low, "fsdp", scatter_dimension=0, tiled=True)
        low = low.reshape(tokens, 2 * D)
        grad_own, out_own = jnp.zeros_like(grad_own), jnp.zeros_like(out_own)

    if fast:

        def columns_of(array, column=0, cols=None):
            return [(array, column, array.shape[1] if cols is None else cols)]

        act_side, pre_side = flip(hidden_act, 1), flip(grad_pre, 1)
        down_parts = term(
            place,
            [
                (
                    [columns_of(value) for value in (*grad_mlps, *grad_mlps_side)],
                    [columns_of(value) for value in (hidden_act, act_side)],
                )
            ],
            hidden_part,
        )
        grad_own = after(grad_own, down_parts)
        down_first = (flip(down_parts[0], 2), flip(down_parts[2], 4))

    grad_mid, own_pack, pack, grad_heads, block_out, mid_sums = mid_back(
        place,
        out_sources,
        grad_own,
        out_own,
        low,
        mid_state,
        attn_proj,
        tokens_here,
        *mods,
        head_slots,
        merged,
        normed_in,
    )
    if fast:

        crossed = cross(pack)
        own_side = flip(own_pack, 1)
        grad_heads = after(grad_heads, pack, own_side, pre_side, mids_side)
    grad_queries, *parts = attend_back(queries, kv_window, bias_t, grad_heads)
    if fast:
        parts[4], down_first = lax.optimization_barrier((parts[4], down_first))
    if paired:
        handed = flip(parts[4], 1)
        near_side = flip(parts[1], 1)
        zero = jnp.zeros((), bf16)
        down_part = parts[2] + jnp.where(core == 1, handed, zero)
        up_side = parts[3] + jnp.where(core == 0, handed, zero)
        from_above, from_below = shift(down_part, -2), shift(up_side, 2)
        arrivals = [near_side, from_above, from_below]
    else:
        arrivals = []
        for distance in range(1, reach + 1):
            arrivals += [
                shift(parts[2 * distance - 1], -distance),
                shift(parts[2 * distance], distance),
            ]
    if fast:
        q_crossed = cross(grad_queries)
        q_side = flip(grad_queries, 1)
        crossed_side = flip(crossed, 1)
        down_first, ignored = lax.optimization_barrier((down_first, (down_part, up_side)))

        def reduced(kept, arrived_part):
            value = (kept.astype(f32) + arrived_part.astype(f32)).astype(bf16)
            return value.reshape(2, value.shape[0] // 2, *value.shape[1:])

        def second_step(values):
            steps = []
            for value, bit in zip(values, (4, 2)):
                at = (seq_at // bit) % 2
                send = lax.dynamic_index_in_dim(value, 1 - at, 1, keepdims=False)
                keep_part = lax.dynamic_index_in_dim(value, at, 1, keepdims=False)
                steps.append((send, keep_part, bit))
            return steps

        def third_step(kept_parts, arrived_parts):
            value = jnp.concatenate(
                [
                    (kept_part.astype(f32) + arrived_part.astype(f32)).astype(bf16)
                    for kept_part, arrived_part in zip(kept_parts, arrived_parts)
                ],
                axis=1,
            )
            at = (seq_at // 8) % 2
            send = lax.dynamic_index_in_dim(value, 1 - at, 0, keepdims=False)
            return send, lax.dynamic_index_in_dim(value, at, 0, keepdims=False)

        down_values = [reduced(down_parts[1], down_first[0]), reduced(down_parts[3], down_first[1])]
        down_steps = second_step(down_values)
        down_second = [flip(send, bit) for send, ignored, bit in down_steps]
        up_parts = term(
            place,
            [
                (
                    [columns_of(value) for value in (grad_pre, pre_side)],
                    [columns_of(value) for value in (*mids, *mids_side)],
                ),
                (
                    [columns_of(value, D, D) for value in (own_pack, crossed, own_side, crossed_side)],
                    [
                        columns_of(value, 0, half)
                        for value in (own_pack, crossed, own_side, crossed_side)
                    ],
                ),
            ],
            half,
            5,
        )
        up_first = (flip(up_parts[0], 2), flip(up_parts[2], 4))
        arrivals[0] = after(arrivals[0], up_parts, q_side)
    grad_kv = parts[0].astype(f32)
    for arrival in arrivals:
        grad_kv = grad_kv + arrival.astype(f32)
    grad_kv = grad_kv.astype(bf16)
    if fast:
        grad_queries, down_second = lax.optimization_barrier((grad_queries, down_second))
    both_out, in_sums = in_back(
        place, qkv_sources, grad_queries, grad_kv, tokens_here, *mods, grad_mid, block_out
    )
    if fast:
        kv_crossed = cross(grad_kv)
        down_second = after(down_second, in_sums)
        down_send, down_keep = third_step([step[1] for step in down_steps], down_second)
        down_last = flip(down_send, 8)
        kv_crossed, in_sums = lax.optimization_barrier((kv_crossed, in_sums))
        up_first, grad_kv, q_crossed_late, ignored = lax.optimization_barrier(
            (up_first, grad_kv, q_crossed, kv_crossed)
        )

    def by_crop(sums):
        sums = sums.reshape(-1, repeats, slots, D)
        sums = jnp.sum(sums, axis=1) if repeats > 1 else sums[:, 0]
        return jnp.einsum("sc,nsd->cnd", selector, sums, precision=highest).astype(bf16)

    mod_grads = jnp.concatenate([in_sums, mid_sums], axis=0)
    if not fast:

        def product(acts, grads):
            return lax.dot_general(
                acts, grads, (((0,), (0,)), ((), ())), preferred_element_type=f32
            ).astype(bf16)

        def both(value):
            value = lax.psum_scatter(value, "fsdp", scatter_dimension=0, tiled=True)
            return lax.psum_scatter(value, "seq", scatter_dimension=1, tiled=True).astype(f32)

        grad_qkv = jnp.concatenate([grad_queries, grad_kv], axis=1)
        qkv_grad = both(product(normed_in, grad_qkv))
        out_grad = both(product(merged, own_pack[:, D:]))
        up_cols = lax.all_to_all(product(mids[0], grad_pre), "fsdp", 0, 1, tiled=True)
        up_grad = lax.psum_scatter(up_cols, "seq", scatter_dimension=1, tiled=True).astype(f32)
        down_cols = product(hidden_act, grad_mlps[0])
        down_grad = lax.psum_scatter(
            down_cols, "seq", scatter_dimension=1, tiled=True
        ).astype(f32)
    else:

        kv_side = flip(grad_kv, 1)
        kv_crossed_side, q_crossed_side = flip(kv_crossed, 1), flip(q_crossed_late, 1)

        def joined(first_part, second_part):
            return columns_of(first_part) + columns_of(second_part)

        up_steps = second_step([reduced(up_parts[1], up_first[0]), reduced(up_parts[3], up_first[1])])
        up_second = [flip(send, bit) for send, ignored, bit in up_steps]
        qkv_parts = term(
            place,
            [
                (
                    [
                        joined(grad_queries, grad_kv),
                        joined(q_crossed, kv_crossed),
                        joined(q_side, kv_side),
                        joined(q_crossed_side, kv_crossed_side),
                    ],
                    [
                        columns_of(value, half, half)
                        for value in (own_pack, crossed, own_side, crossed_side)
                    ],
                )
            ],
            half,
        )
        qkv_first = (flip(qkv_parts[0], 2), flip(qkv_parts[2], 4))
        qkv_steps = second_step(
            [reduced(qkv_parts[1], qkv_first[0]), reduced(qkv_parts[3], qkv_first[1])]
        )
        qkv_second = [flip(send, bit) for send, ignored, bit in qkv_steps]
        up_second, mod_grads, down_last, ignored = lax.optimization_barrier(
            (up_second, mod_grads, down_last, qkv_parts)
        )
        qkv_sends = [step[0] for step in qkv_steps]
        up_send, up_keep = third_step([step[1] for step in up_steps], up_second)
        qkv_send, qkv_keep = third_step([step[1] for step in qkv_steps], qkv_second)
        down_grad = jnp.transpose(down_keep.astype(f32) + down_last.astype(f32))
        up_last, ignored = lax.optimization_barrier((flip(up_send, 8), qkv_send))
        qkv_grad = jnp.transpose(qkv_keep.astype(f32) + flip(qkv_send, 8).astype(f32))
        mixed = up_keep.astype(f32) + up_last.astype(f32)
        up_rows, out_rows = hidden // seq, D // seq
        up_low, out_low = up_rows * 5 // 64 * 8, out_rows * 5 // 64 * 8
        parted = up_low + out_low
        rest = parted + up_rows - up_low
        up_mine = jnp.concatenate([mixed[:up_low], mixed[parted:rest]], axis=0).astype(bf16)
        out_grad = jnp.transpose(jnp.concatenate([mixed[up_low:parted], mixed[rest:]], axis=0))
        pairs = []
        for place_seq in range(seq):
            for place_row in range(2):
                high = (place_seq // 8) % 2
                target_seq = (place_seq & 7) | (place_row * 8)
                pairs.append((place_seq * 2 + place_row, target_seq * 2 + high))
        up_grad = jnp.transpose(lax.ppermute(up_mine, ("seq", "fsdp"), pairs)).astype(f32)
    mod_grads = by_crop(mod_grads).reshape(crops, 6 * D)
    if fast:
        share = columns // 2
        quarters = [mod_grads[:, i * share : (i + 1) * share] for i in range(4)]
        first_core = core == 0
        kept_sum = [jnp.where(first_core, quarters[i], quarters[i + 1]) for i in (0, 2)]
        sent_sum = [jnp.where(first_core, quarters[i + 1], quarters[i]) for i in (0, 2)]
        kept_sum, sent_sum = (jnp.stack(value) for value in (kept_sum, sent_sum))
        mod_grads = (kept_sum.astype(f32) + flip(sent_sum, 1).astype(f32)).astype(bf16)
        for bit, ahead in ((8, ()), (2, qkv_sends), (4, qkv_send)):
            mod_grads = (mod_grads.astype(f32) + flip(mod_grads, bit).astype(f32)).astype(bf16)
            mod_grads = after(mod_grads, ahead)
        own = pick(mod_grads[0], mod_grads[1])
        other = cross(pick(mod_grads[1], mod_grads[0]))
        own = jnp.concatenate([own, other], axis=0)
        other = flip(own, 1)
        mod_grads = jnp.concatenate(
            [jnp.where(first_core, own, other), jnp.where(first_core, other, own)], axis=1
        )
    else:
        mod_grads = lax.psum(mod_grads, "seq")
        split = jnp.transpose(mod_grads.reshape(crops, rows, columns), (1, 0, 2))
        mod_grads = lax.all_to_all(split, "fsdp", 0, 0).reshape(rows * crops, columns)
    ada_grad = outer(cond_rows, mod_grads)

    both_out = from_slots(both_out, f32, *(qkv_sends if fast else ()))
    block_out, input_grad = both_out[:, :D].astype(bf16), both_out[:, D:]
    return (
        block_out[None],
        input_grad[None],
        qkv_grad,
        out_grad,
        up_grad,
        down_grad,
        ada_grad,
    )


def solution(mesh):
    in_specs = (
        P("fsdp", "seq", None),
        P("fsdp", None, None),
        P("fsdp", None),
        P("fsdp", None),
        P("fsdp", None, None),
        P("fsdp", None, None),
        P("fsdp", "seq"),
        P("fsdp", None),
        P("fsdp", None),
        P("fsdp", None),
        P("fsdp", None),
        P(None, "fsdp"),
        P("fsdp", "seq", None),
    )
    out_specs = (
        P("fsdp", "seq", None),
        P("fsdp", "seq", None),
        P("fsdp", "seq"),
        P("fsdp", "seq"),
        P("fsdp", "seq"),
        P("fsdp", "seq"),
        P(None, "fsdp"),
    )
    return jax.shard_map(local, mesh=mesh, in_specs=in_specs, out_specs=out_specs, check_vma=False)
```
